32 devices in a mesh: seq: 8 (over z, y), head: 4 (over x, core).
Axes of the slice: x: 2, y: 2, z: 4, core: 2. Of those that a mesh axis runs over, the one named last changes fastest.
Arguments:
- query_rows: bfloat16 [16384, 2048], P('seq', 'head'), may hold values from -6 to 6
- key_rows: bfloat16 [16384, 2048], P('seq', 'head'), may hold values from -6 to 6
- value_rows: bfloat16 [16384, 2048], P('seq', 'head'), may hold values from -6 to 6
- out_cotangent: bfloat16 [16384, 2048], P('seq', 'head'), may hold values from -6 to 6
- norm_gain: float32 [2048], P('head'), may hold values from 0.5 to 1.5
- decay_rate: float32 [16], P('head'), may hold values from 1.2207031e-05 to 0.0333333333
- document_lengths: int32 [32], replicated, may hold values from 1 to 8192, 16384 in all
- group_home: int32 [64], P('seq'), may hold values from 0 to 63, as said below
Outputs:
- query_grad: bfloat16 [16384, 2048], P('seq', 'head')
- key_grad: bfloat16 [16384, 2048], P('seq', 'head')
- value_grad: bfloat16 [16384, 2048], P('seq', 'head')
The draws below stay inside these ranges and needn't reach their ends.
Inputs may be any that keep to these rules, and one draw needn't show every extreme that they name: document_lengths sum to 16384; the longest holds exactly half of them. group_home is a permutation of the 64 sequence groups; the groups stored on one device along seq hold exactly one group of each device's aligned block of sequence groups.
All inputs are finite; a program needn't handle non-finite values.
Results may differ from the reference program's by a relative error of at most 0.0095.
Values may be sent and summed in bfloat16 or wider, within the bound.
No kernel may reach another device: no remote copies, remote signals or barrier semaphores. Data moves between devices by JAX's collectives and lax.ppermute only.
A program may use at most 128 MiB of HBM per device.

```python
import math
import jax
import jax.numpy as jnp
import numpy as np
from jax import lax

HEAD_SIZE = 128
SPAN = 256
DOCS = 32
TOK_DEV = 2048
TOKENS = 16384
SPANS = 64
GROUP = 256
GROUPS = 64
HEADS = 16
CHANNELS = 2048


def draw_decay_rate(key, part):
    pick_key, fast_key, slow_key = jax.random.split(key, 3)
    slow_share = 0.5
    slow_heads = jax.random.uniform(pick_key, (HEADS,)) < slow_share
    fast_rate = jnp.exp(jax.random.uniform(fast_key, (HEADS,), minval=jnp.log(1.0 / 50.0), maxval=jnp.log(1.0 / 30.0)))
    slow_rate = jnp.exp(jax.random.uniform(slow_key, (HEADS,), minval=jnp.log(0.2 / TOKENS), maxval=jnp.log(2.0 / TOKENS)))
    return jnp.where(slow_heads, slow_rate, fast_rate).astype(jnp.float32)


def draw_group_home(key, part):
    devices = TOK_DEV // GROUP
    offset_key, source_key, target_key = jax.random.split(key, 3)
    shifts = jax.random.permutation(offset_key, devices)
    source_order = jax.vmap(lambda row_key: jax.random.permutation(row_key, devices))(jax.random.split(source_key, devices))
    target_order = jax.vmap(lambda row_key: jax.random.permutation(row_key, devices))(jax.random.split(target_key, devices))
    sources = jnp.arange(devices, dtype=jnp.int32)[:, None]
    targets = (sources + shifts[None, :]) % devices
    stored = sources * devices + source_order
    sources_full = jnp.broadcast_to(sources, targets.shape)
    home = targets * devices + target_order[targets, sources_full]
    return jnp.zeros((GROUPS,), jnp.int32).at[stored.reshape(-1)].set(home.reshape(-1).astype(jnp.int32))


def block_scale(key, extent, cuts, low, high):
    factor_of = 1.0
    for dim, parts in cuts:
        draws = jax.random.uniform(jax.random.fold_in(jax.random.fold_in(key, 6), dim), (parts,), jnp.float32, low / len(cuts), high / len(cuts))
        factor_of = factor_of * jnp.repeat(jnp.exp(draws), extent[dim] // parts).reshape((-1,) + (1,) * (len(extent) - 1 - dim))
    return factor_of


def length_profile(count, total, most, skew):
    loads = [(1 << 20) // math.isqrt(standing ** skew) + 1 for standing in range(2, count + 1)]
    surplus, given = total - most - (count - 1), [1] * (count - 1)
    while surplus > 0:
        candidates = [i for i in range(count - 1) if given[i] < most]
        pool, left = sum([loads[i] for i in candidates]), surplus
        for i in candidates:
            addition = min(most - given[i], max(1, left * loads[i] // pool), surplus)
            given[i] = given[i] + addition
            surplus = surplus - addition
    return np.array([most] + given)


def ragged_sizes(own_key, number_of, total, limit, skew):
    if number_of == 2:
        one = jax.random.randint(own_key, (), max(1, total - limit), min(limit, total - 1) + 1)
        return jnp.stack([one, total - one])
    sizes = jnp.asarray(length_profile(number_of, total, limit, skew), jnp.int32)
    twos = (number_of - 1) // 2
    giver, receiver = sizes[1:1 + 2 * twos:2], sizes[2:2 + 2 * twos:2]
    margin = jnp.minimum(giver - 1, limit - receiver)
    passed = jax.random.randint(jax.random.fold_in(own_key, 1), (twos,), 0, 1 << 20) % (margin + 1)
    sizes = sizes.at[1:1 + 2 * twos:2].set(giver - passed).at[2:2 + 2 * twos:2].set(receiver + passed)
    return sizes[jax.random.permutation(jax.random.fold_in(own_key, 2), number_of)]


def scatter_about(key, extent, deviation, limit, cuts=(), held_as=jnp.bfloat16):
    entries = jax.random.normal(key, extent, jnp.float32) * deviation
    if len(cuts) > 0:
        entries = block_scale(key, extent, cuts, -0.22, 0.18) * entries
    return jnp.clip(entries, min=-limit, max=limit).astype(held_as)


def setup_inputs(seed: int = 0) -> dict:
    key_of = jax.random.split(jax.random.key(seed), 9)
    return {
        "query_rows": scatter_about(key_of[0], (TOKENS, CHANNELS), 1.0, 6.0, ((0, 8), (1, 4))),
        "key_rows": scatter_about(key_of[1], (TOKENS, CHANNELS), 1.0, 6.0, ((0, 8), (1, 4))),
        "value_rows": scatter_about(key_of[2], (TOKENS, CHANNELS), 1.0, 6.0, ((0, 8), (1, 4))),
        "out_cotangent": scatter_about(key_of[3], (TOKENS, CHANNELS), 1.0, 6.0, ((0, 8), (1, 4))),
        "norm_gain": jnp.clip(1.0 + 0.1 * jax.random.normal(key_of[4], (CHANNELS,), jnp.float32), 0.5, 1.5),
        "decay_rate": draw_decay_rate(jax.random.fold_in(key_of[8], 71), 0),
        "document_lengths": ragged_sizes(key_of[6], DOCS, TOKENS, TOKENS // 2, 2).astype(jnp.int32),
        "group_home": draw_group_home(jax.random.fold_in(key_of[8], 71), 0),
    }


EPSILON = 1e-06

def segment_of(positions, doc_ends):
    return lax.optimization_barrier(jnp.sum((doc_ends <= positions[..., None]).astype(jnp.int32), axis=-1))

def span_weights(seq_spans, doc_ends, decay_rates, span_width):
    offsets = jnp.arange(span_width, dtype=jnp.int32)
    positions = seq_spans[:, None] * span_width + offsets[None, :]
    segment = segment_of(positions, doc_ends)
    before = jnp.where(seq_spans == 0, -1, segment_of(seq_spans * span_width - 1, doc_ends))
    last_segment = segment[:, -1]
    step_float = offsets.astype(jnp.float32)
    query_side = jnp.exp(-decay_rates[None, None, :] * (step_float[None, :, None] + 1.0)) * (segment == before[:, None]).astype(jnp.float32)[:, :, None]
    key_side = jnp.exp(-decay_rates[None, None, :] * (span_width - 1.0 - step_float)[None, :, None]) * (segment == last_segment[:, None]).astype(jnp.float32)[:, :, None]
    carry_rate = jnp.exp(-decay_rates * span_width)[None, :] * (before == last_segment).astype(jnp.float32)[:, None]
    return (query_side, key_side, carry_rate, segment)

def span_masks(segment, decay_rates, span_width):
    step_float = jnp.arange(span_width, dtype=jnp.float32)
    spread = step_float[:, None] - step_float[None, :]
    same_doc = (segment[:, :, None] == segment[:, None, :]) & (spread >= 0.0)[None]
    return jnp.where(same_doc[:, None], jnp.exp(-decay_rates[None, :, None, None] * jnp.maximum(spread, 0.0)[None, None]), 0.0)

def rounded(values):
    return lax.optimization_barrier(values.astype(jnp.bfloat16)).astype(jnp.float32)

def reference(query_rows, key_rows, value_rows, out_cotangent, norm_gain, decay_rate, document_lengths, group_home):
    doc_ends = jnp.cumsum(document_lengths).astype(jnp.int32)

    def to_sequence(stored):
        blocks = stored.reshape(GROUPS, GROUP, HEADS, HEAD_SIZE)
        ordered = jnp.zeros_like(blocks).at[group_home].set(blocks)
        return ordered.reshape(SPANS, SPAN, HEADS, HEAD_SIZE)
    query_seq = to_sequence(query_rows)
    key_seq = to_sequence(key_rows)
    value_seq = to_sequence(value_rows)
    upstream = to_sequence(out_cotangent)
    all_spans = jnp.arange(SPANS, dtype=jnp.int32)
    query_side, key_side, carry_rate, segment = span_weights(all_spans, doc_ends, decay_rate, SPAN)

    def forward_step(state, inputs):
        query_c, key_c, value_c, query_w, key_w, carry_c, segment_c = inputs
        decay_mask = span_masks(segment_c[None], decay_rate, SPAN)[0]
        query_f = query_c.astype(jnp.float32)
        key_f = key_c.astype(jnp.float32)
        value_f = value_c.astype(jnp.float32)
        prev_state = rounded(state)
        scores = jnp.einsum('jhd,lhd->hjl', query_f, key_f)
        mixing = rounded(scores * decay_mask)
        output = jnp.einsum('hjl,lhe->jhe', mixing, value_f) + query_w[..., None] * jnp.einsum('jhd,hde->jhe', query_f, prev_state)
        weighted = rounded(key_w[..., None] * value_f)
        summary = jnp.einsum('jhd,jhe->hde', key_f, weighted)
        return (carry_c[:, None, None] * state + summary, (output, prev_state))
    zero_state = jnp.zeros((HEADS, HEAD_SIZE, HEAD_SIZE), jnp.float32)
    _, (attn_out, prev_states) = lax.scan(forward_step, zero_state, (query_seq, key_seq, value_seq, query_side, key_side, carry_rate, segment))
    flat_out = attn_out.reshape(TOKENS, CHANNELS)
    upstream_f = upstream.reshape(TOKENS, CHANNELS).astype(jnp.float32)
    scaling = 1.0 / jnp.sqrt(lax.optimization_barrier(jnp.mean(flat_out * flat_out, axis=1)) + EPSILON)
    pulled = lax.optimization_barrier(jnp.mean(norm_gain * upstream_f * flat_out, axis=1))
    grad_in = (scaling[:, None] * norm_gain * upstream_f - (scaling ** 3)[:, None] * flat_out * pulled[:, None]).astype(jnp.bfloat16)
    grad_in = grad_in.reshape(SPANS, SPAN, HEADS, HEAD_SIZE)

    def backward_step(state, inputs):
        query_c, key_c, value_c, grad_c, query_w, key_w, carry_c, segment_c, prev_state = inputs
        decay_mask = span_masks(segment_c[None], decay_rate, SPAN)[0]
        query_f = query_c.astype(jnp.float32)
        key_f = key_c.astype(jnp.float32)
        value_f = value_c.astype(jnp.float32)
        grad_f = grad_c.astype(jnp.float32)
        after_state = rounded(state)
        mixing = rounded(jnp.einsum('jhd,lhd->hjl', query_f, key_f) * decay_mask)
        score_grad = rounded(jnp.einsum('jhe,lhe->hjl', grad_f, value_f) * decay_mask)
        query_grad = jnp.einsum('hjl,lhd->jhd', score_grad, key_f) + query_w[..., None] * jnp.einsum('jhe,hde->jhd', grad_f, prev_state)
        key_grad = jnp.einsum('hjl,jhd->lhd', score_grad, query_f) + key_w[..., None] * jnp.einsum('lhe,hde->lhd', value_f, after_state)
        value_grad = jnp.einsum('hjl,jhe->lhe', mixing, grad_f) + key_w[..., None] * jnp.einsum('lhd,hde->lhe', key_f, after_state)
        rev_summary = jnp.einsum('jhd,jhe->hde', query_f, rounded(query_w[..., None] * grad_f))
        return (rev_summary + carry_c[:, None, None] * state, (query_grad, key_grad, value_grad))
    _, (query_grad, key_grad, value_grad) = lax.scan(backward_step, zero_state, (query_seq, key_seq, value_seq, grad_in, query_side, key_side, carry_rate, segment, prev_states), reverse=True)

    def to_stored(values):
        blocks = values.reshape(GROUPS, GROUP, HEADS, HEAD_SIZE)
        return blocks[group_home].reshape(TOKENS, CHANNELS).astype(jnp.bfloat16)
    return (to_stored(query_grad), to_stored(key_grad), to_stored(value_grad))
```

```python
import functools

import jax
import jax.numpy as jnp
from jax import lax
from jax.experimental import pallas as pl
from jax.experimental.pallas import tpu as pltpu
from jax.sharding import PartitionSpec as P

HEAD_SIZE = 128
LANES = 128
EPSILON = 1e-06
TAIL = 16
F32 = jnp.float32
BF16 = jnp.bfloat16


def dot(a, b, ca, cb):
    return lax.dot_general(a, b, (((ca,), (cb,)), ((), ())), preferred_element_type=F32)


def head_cols(h):
    return slice(h * HEAD_SIZE, (h + 1) * HEAD_SIZE)


def token_index(span):
    return lax.broadcasted_iota(jnp.int32, (span, LANES), 0)


def key_table(rate, span):
    return jnp.exp(-rate * (span - 1.0 - token_index(span).astype(F32)))


def query_table(rate, span):
    return jnp.exp(-rate * (token_index(span).astype(F32) + 1.0))


def row_to_cols(row, width):
    cols = jnp.transpose(jnp.broadcast_to(row, (LANES, row.shape[1])))
    return jnp.concatenate([cols] * (width // LANES), axis=1) if width > LANES else cols


def cols_to_row(cols):
    return jnp.sum(jnp.transpose(cols), axis=0, keepdims=True)


def put_state(out_ref, step, h, rows, value):
    chunks = HEAD_SIZE // rows
    for part in range(chunks):
        out_ref[h * chunks + part, pl.ds(pl.multiple_of(step * rows, rows), rows), :] = value[
            part * rows : (part + 1) * rows
        ]


def get_state(ref, h, rows):
    chunks = HEAD_SIZE // rows
    return ref[h * chunks : (h + 1) * chunks, 0].reshape(HEAD_SIZE, HEAD_SIZE)


def summary_kernel(heads, rows, last_ref, home_ref, rate_ref, k_ref, v_ref, out_ref, table):
    step = pl.program_id(0)
    span = k_ref.shape[0]

    @pl.when(step == 0)
    def _():
        for h in range(heads):
            table[h] = key_table(rate_ref[h], span)
        tail = jnp.zeros((TAIL, LANES), F32)
        lane = lax.broadcasted_iota(jnp.int32, (TAIL, LANES), 1)
        for i in range(home_ref.shape[0]):
            tail = jnp.where(lane == i, home_ref[i].astype(F32), tail)
        for d in range(out_ref.shape[0]):
            out_ref[d, out_ref.shape[1] - TAIL :, :] = tail.astype(BF16)

    live = token_index(span) >= last_ref[step]
    for h in range(heads):
        side = jnp.where(live, table[h], 0.0)
        weighted = (side * v_ref[:, head_cols(h)].astype(F32)).astype(BF16)
        put_state(out_ref, step, h, rows, dot(k_ref[:, head_cols(h)], weighted, 0, 0).astype(BF16))


def scan_kernel(rows, spans, order_ref, cont_ref, rate_ref, in_ref, out_ref):
    slots = out_ref.shape[1] // rows
    factor = jnp.exp(jnp.full((8, LANES), rate_ref[0], F32))[0:1]

    def body(c, state):
        place = order_ref[c]
        device, slot = place // slots, place % slots
        at = pl.ds(pl.multiple_of(slot * rows, rows), rows)
        out_ref[device, at, :] = state.astype(BF16)
        carried = jnp.where(cont_ref[c] > 0, factor * state, 0.0)
        return carried + in_ref[device, at, :].astype(F32)

    lax.fori_loop(0, spans, body, jnp.zeros((rows, LANES), F32))


def fill_decay(decay, rate_ref, heads, span):
    j = lax.broadcasted_iota(jnp.int32, (span, span), 0)
    l = lax.broadcasted_iota(jnp.int32, (span, span), 1)
    spread = (j - l).astype(F32)
    for h in range(heads):
        decay[h] = jnp.where(
            spread >= 0.0, jnp.exp(-rate_ref[h] * jnp.maximum(spread, 0.0)), 0.0
        )


def local_kernel(heads, rate_ref, seg_ref, q_ref, k_ref, v_ref, out_ref, decay):
    span = q_ref.shape[0]

    @pl.when(pl.program_id(0) == 0)
    def _():
        fill_decay(decay, rate_ref, heads, span)

    seg = seg_ref[0]
    same = row_to_cols(seg, span) == seg
    for h in range(heads):
        cols = head_cols(h)
        scores = dot(q_ref[:, cols], k_ref[:, cols], 1, 1)
        mixing = (scores * jnp.where(same, decay[h], 0.0)).astype(BF16)
        out_ref[:, cols] = dot(mixing, v_ref[:, cols], 1, 0)


def output_kernel(
    heads, rows, first_ref, rate_ref, gain_ref, q_ref, u_ref, inner_ref, prev_ref, out_ref, sums_ref, table
):
    step = pl.program_id(0)
    span = q_ref.shape[0]

    @pl.when(step == 0)
    def _():
        for h in range(heads):
            table[h] = query_table(rate_ref[h], span)

    live = token_index(span) < first_ref[step]
    squares = jnp.zeros((span, LANES), F32)
    crossed = jnp.zeros((span, LANES), F32)
    for h in range(heads):
        cols = head_cols(h)
        outer = dot(q_ref[:, cols], get_state(prev_ref, h, rows), 1, 0)
        attn = inner_ref[:, cols] + jnp.where(live, table[h], 0.0) * outer
        out_ref[:, cols] = attn
        squares += attn * attn
        crossed += gain_ref[:, cols] * u_ref[:, cols].astype(F32) * attn
    sums_ref[0, 0:1, :] = cols_to_row(squares)
    sums_ref[0, 1:2, :] = cols_to_row(crossed)


def cotangent_kernel(
    heads, rows, channels, first_ref, rate_ref, gain_ref, sums_ref, q_ref, u_ref, attn_ref, g_ref, out_ref, table
):
    step = pl.program_id(0)
    span = q_ref.shape[0]

    @pl.when(step == 0)
    def _():
        for h in range(heads):
            table[h] = query_table(rate_ref[h], span)

    total = jnp.sum(sums_ref[:, 0], axis=0)
    scaling = 1.0 / jnp.sqrt(total[0:1] / channels + EPSILON)
    pulled = total[1:2] / channels
    first = row_to_cols(scaling, LANES)
    second = row_to_cols(scaling * scaling * scaling * pulled, LANES)
    live = token_index(span) < first_ref[step]
    for h in range(heads):
        cols = head_cols(h)
        grad = first * gain_ref[:, cols] * u_ref[:, cols].astype(F32) - second * attn_ref[:, cols]
        grad = grad.astype(BF16)
        g_ref[:, cols] = grad
        weighted = (jnp.where(live, table[h], 0.0) * grad.astype(F32)).astype(BF16)
        put_state(out_ref, step, h, rows, dot(q_ref[:, cols], weighted, 0, 0).astype(BF16))


def inner_grads_kernel(
    heads, rows, first_ref, rate_ref, seg_ref, q_ref, k_ref, v_ref, g_ref, prev_ref,
    dq_ref, dk_ref, dv_ref, decay, table,
):
    step = pl.program_id(0)
    span = q_ref.shape[0]

    @pl.when(step == 0)
    def _():
        fill_decay(decay, rate_ref, heads, span)
        for h in range(heads):
            table[h] = query_table(rate_ref[h], span)

    seg = seg_ref[0]
    same = row_to_cols(seg, span) == seg
    live = token_index(span) < first_ref[step]
    for h in range(heads):
        cols = head_cols(h)
        q, k, v, g = q_ref[:, cols], k_ref[:, cols], v_ref[:, cols], g_ref[:, cols]
        mask = jnp.where(same, decay[h], 0.0)
        mixing = (dot(q, k, 1, 1) * mask).astype(BF16)
        score_grad = (dot(g, v, 1, 1) * mask).astype(BF16)
        outer = dot(g, get_state(prev_ref, h, rows), 1, 1)
        dq = dot(score_grad, k, 1, 0) + jnp.where(live, table[h], 0.0) * outer
        dq_ref[:, cols] = dq.astype(BF16)
        dk_ref[:, cols] = dot(score_grad, q, 0, 0)
        dv_ref[:, cols] = dot(mixing, g, 0, 0)


def outer_grads_kernel(
    heads, rows, last_ref, rate_ref, k_ref, v_ref, after_ref, dk_in, dv_in, dk_ref, dv_ref, table
):
    step = pl.program_id(0)
    span = k_ref.shape[0]

    @pl.when(step == 0)
    def _():
        for h in range(heads):
            table[h] = key_table(rate_ref[h], span)

    live = token_index(span) >= last_ref[step]
    for h in range(heads):
        cols = head_cols(h)
        side = jnp.where(live, table[h], 0.0)
        after = get_state(after_ref, h, rows)
        dk = dk_in[:, cols] + side * dot(v_ref[:, cols], after, 1, 1)
        dv = dv_in[:, cols] + side * dot(k_ref[:, cols], after, 1, 0)
        dk_ref[:, cols] = dk.astype(BF16)
        dv_ref[:, cols] = dv.astype(BF16)


def exchange(blocks):
    return lax.all_to_all(blocks, "seq", split_axis=0, concat_axis=0, tiled=True)


def shards(query, key, value, upstream, norm_gain, decay_rate, document_lengths, group_home):
    devices = lax.axis_size("seq")
    position = lax.axis_index("seq")
    tokens, width = query.shape
    heads = width // HEAD_SIZE
    slots = group_home.shape[0]
    span = tokens // slots
    spans = slots * devices
    rows = width // devices
    channels = width * lax.axis_size("head")
    params = pltpu.CompilerParams(dimension_semantics=("arbitrary",), vmem_limit_bytes=32 << 20)

    doc_ends = jnp.cumsum(document_lengths)
    starts = group_home * span
    later = doc_ends[None, :] >= jnp.maximum(starts, 1)[:, None]
    first_end = jnp.min(jnp.where(later, doc_ends[None, :], tokens * devices), axis=1) - starts
    first_end = jnp.where(starts == 0, 0, first_end)
    earlier = doc_ends[None, :] < (starts + span)[:, None]
    last_start = jnp.max(jnp.where(earlier, doc_ends[None, :], 0), axis=1) - starts
    positions = starts[:, None, None] + jnp.arange(span, dtype=jnp.int32)[None, None, :]
    seg = jnp.sum((doc_ends <= positions[..., None]).astype(F32), axis=-1)
    all_starts = jnp.arange(spans, dtype=jnp.int32) * span
    crosses = (doc_ends[None, :] >= all_starts[:, None]) & (doc_ends[None, :] < (all_starts + span)[:, None])
    cont = jnp.logical_not(jnp.any(crosses, axis=1)).astype(jnp.int32)
    scan_rate = -span * jnp.sum(
        jnp.where(jnp.arange(heads) == (position * rows) // HEAD_SIZE, decay_rate, 0.0), keepdims=True
    )

    smem = pl.BlockSpec(memory_space=pltpu.SMEM)
    tok = pl.BlockSpec((span, width), lambda i: (i, 0))
    seg_spec = pl.BlockSpec((1, 1, span), lambda i: (i, 0, 0))
    gain_spec = pl.BlockSpec((1, width), lambda i: (0, 0))
    state_spec = pl.BlockSpec((devices, 1, rows, LANES), lambda i: (0, i, 0, 0))
    gain = norm_gain.reshape(1, width)

    def whole(shape):
        return pl.BlockSpec(shape, lambda i: (0,) * len(shape))

    def shaped(shape, dtype):
        return jax.ShapeDtypeStruct(shape, dtype)

    side_table = pltpu.VMEM((heads, span, LANES), F32)
    decay_table = pltpu.VMEM((heads, span, span), F32)
    packed = (devices, slots * rows + TAIL, LANES)
    plain = (devices, slots * rows, LANES)

    sent = pl.pallas_call(
        functools.partial(summary_kernel, heads, rows),
        grid=(slots,),
        in_specs=[smem, smem, smem, tok, tok],
        out_specs=whole(packed),
        out_shape=shaped(packed, BF16),
        scratch_shapes=[side_table],
        compiler_params=params,
        name="summaries",
    )(last_start, group_home, decay_rate, key, value)

    arrived = exchange(sent)

    inner = pl.pallas_call(
        functools.partial(local_kernel, heads),
        grid=(slots,),
        in_specs=[smem, seg_spec, tok, tok, tok],
        out_specs=tok,
        out_shape=shaped((tokens, width), F32),
        scratch_shapes=[decay_table],
        compiler_params=params,
        name="inner",
    )(decay_rate, seg, query, key, value)

    homes = arrived[:, slots * rows, :slots].astype(jnp.int32).reshape(-1)
    hits = homes[None, :] == jnp.arange(spans, dtype=jnp.int32)[:, None]
    order = jnp.sum(jnp.where(hits, jnp.arange(spans, dtype=jnp.int32)[None, :], 0), axis=1)

    def scan(blocks, order, cont):
        return pl.pallas_call(
            functools.partial(scan_kernel, rows, spans),
            grid=(1,),
            in_specs=[smem, smem, smem, whole(blocks.shape)],
            out_specs=whole(plain),
            out_shape=shaped(plain, BF16),
            compiler_params=params,
            name="scan",
        )(order, cont, scan_rate, blocks)

    prev = exchange(scan(arrived, order, cont)).reshape(devices, slots, rows, LANES)

    attn, sums = pl.pallas_call(
        functools.partial(output_kernel, heads, rows),
        grid=(slots,),
        in_specs=[smem, smem, gain_spec, tok, tok, tok, state_spec],
        out_specs=[tok, pl.BlockSpec((1, 2, span), lambda i: (i, 0, 0))],
        out_shape=[shaped((tokens, width), F32), shaped((slots, 2, span), F32)],
        scratch_shapes=[side_table],
        compiler_params=params,
        name="output",
    )(first_end, decay_rate, gain, query, upstream, inner, prev)

    sums = lax.all_gather(sums, "head")

    grad_in, rev_sent = pl.pallas_call(
        functools.partial(cotangent_kernel, heads, rows, channels),
        grid=(slots,),
        in_specs=[
            smem, smem, gain_spec,
            pl.BlockSpec((sums.shape[0], 1, 2, span), lambda i: (0, i, 0, 0)),
            tok, tok, tok,
        ],
        out_specs=[tok, whole(plain)],
        out_shape=[shaped((tokens, width), BF16), shaped(plain, BF16)],
        scratch_shapes=[side_table],
        compiler_params=params,
        name="cotangent",
    )(first_end, decay_rate, gain, sums, query, upstream, attn)

    rev_arrived = exchange(rev_sent)

    query_grad, key_inner, value_inner = pl.pallas_call(
        functools.partial(inner_grads_kernel, heads, rows),
        grid=(slots,),
        in_specs=[smem, smem, seg_spec, tok, tok, tok, tok, state_spec],
        out_specs=[tok, tok, tok],
        out_shape=[shaped((tokens, width), BF16), shaped((tokens, width), F32), shaped((tokens, width), F32)],
        scratch_shapes=[decay_table, side_table],
        compiler_params=params,
        name="inner_grads",
    )(first_end, decay_rate, seg, query, key, value, grad_in, prev)

    after = exchange(scan(rev_arrived, order[::-1], cont[::-1])).reshape(devices, slots, rows, LANES)

    key_grad, value_grad = pl.pallas_call(
        functools.partial(outer_grads_kernel, heads, rows),
        grid=(slots,),
        in_specs=[smem, smem, tok, tok, state_spec, tok, tok],
        out_specs=[tok, tok],
        out_shape=[shaped((tokens, width), BF16)] * 2,
        scratch_shapes=[side_table],
        compiler_params=params,
        name="outer_grads",
    )(last_start, decay_rate, key, value, after, key_inner, value_inner)
    return query_grad, key_grad, value_grad


def solution(mesh):
    in_specs = (
        P("seq", "head"),
        P("seq", "head"),
        P("seq", "head"),
        P("seq", "head"),
        P("head"),
        P("head"),
        P(),
        P("seq"),
    )
    out_specs = (P("seq", "head"), P("seq", "head"), P("seq", "head"))
    return jax.shard_map(shards, mesh=mesh, in_specs=in_specs, out_specs=out_specs, check_vma=False)
```

```python
import functools

import jax
import jax.numpy as jnp
from jax import lax
from jax.experimental import pallas as pl
from jax.experimental.pallas import tpu as pltpu
from jax.sharding import PartitionSpec as P

HEAD_SIZE = 128
LANES = 128
EPSILON = 1e-06
TAIL = 16
F32 = jnp.float32
BF16 = jnp.bfloat16


def dot(a, b, ca, cb):
    return lax.dot_general(a, b, (((ca,), (cb,)), ((), ())), preferred_element_type=F32)


def head_cols(h):
    return slice(h * HEAD_SIZE, (h + 1) * HEAD_SIZE)


def token_index(span):
    return lax.broadcasted_iota(jnp.int32, (span, LANES), 0)


def key_table(rate, span):
    return jnp.exp(-rate * (span - 1.0 - token_index(span).astype(F32)))


def query_table(rate, span):
    return jnp.exp(-rate * (token_index(span).astype(F32) + 1.0))


def row_to_cols(row, width):
    cols = jnp.transpose(jnp.broadcast_to(row, (LANES, row.shape[1])))
    return jnp.concatenate([cols] * (width // LANES), axis=1) if width > LANES else cols


def cols_to_row(cols):
    return jnp.sum(jnp.transpose(cols), axis=0, keepdims=True)


def doc_bounds(len_ref, start, span):
    end = jnp.int32(0)
    first = jnp.int32(0)
    last = jnp.int32(0)
    for d in range(len_ref.shape[0]):
        before = end
        end = end + len_ref[d]
        first = jnp.where((before < start) & (end >= start), end, first)
        last = jnp.where(end < start + span, end, last)
    return first - start, last - start


def segment_row(len_ref, start, span):
    position = start + lax.broadcasted_iota(jnp.int32, (1, span), 1)
    end = jnp.int32(0)
    segment = jnp.zeros((1, span), F32)
    for d in range(len_ref.shape[0]):
        end = end + len_ref[d]
        segment += jnp.where(end <= position, 1.0, 0.0)
    return segment


def put_state(out_ref, step, h, rows, value):
    chunks = HEAD_SIZE // rows
    for part in range(chunks):
        out_ref[h * chunks + part, pl.ds(pl.multiple_of(step * rows, rows), rows), :] = value[
            part * rows : (part + 1) * rows
        ]


def get_state(ref, h, rows):
    chunks = HEAD_SIZE // rows
    return ref[h * chunks : (h + 1) * chunks, 0].reshape(HEAD_SIZE, HEAD_SIZE)


def summary_kernel(heads, rows, len_ref, home_ref, rate_ref, k_ref, v_ref, out_ref, table):
    step = pl.program_id(0)
    span = k_ref.shape[0]

    @pl.when(step == 0)
    def _():
        for h in range(heads):
            table[h] = key_table(rate_ref[h], span)
        tail = jnp.zeros((TAIL, LANES), F32)
        lane = lax.broadcasted_iota(jnp.int32, (TAIL, LANES), 1)
        for i in range(home_ref.shape[0]):
            tail = jnp.where(lane == i, home_ref[i].astype(F32), tail)
        for d in range(out_ref.shape[0]):
            out_ref[d, out_ref.shape[1] - TAIL :, :] = tail.astype(BF16)

    _, last = doc_bounds(len_ref, home_ref[step] * span, span)
    live = token_index(span) >= last
    for h in range(heads):
        side = jnp.where(live, table[h], 0.0)
        weighted = (side * v_ref[:, head_cols(h)].astype(F32)).astype(BF16)
        put_state(out_ref, step, h, rows, dot(k_ref[:, head_cols(h)], weighted, 0, 0).astype(BF16))


def scan_kernel(rows, spans, span, reverse, len_ref, order_ref, rate_ref, in_ref, out_ref, cont):
    slots = out_ref.shape[1] // rows
    head = (lax.axis_index("seq") * rows) // HEAD_SIZE
    factor = jnp.exp(jnp.full((8, LANES), -rate_ref[head] * span, F32))[0:1]

    def reset(c, carry):
        cont[c] = 1
        return carry

    def cut(d, end):
        end = end + len_ref[d]
        cont[end // span] = 0
        return end

    lax.fori_loop(0, spans + 1, reset, 0)
    lax.fori_loop(0, len_ref.shape[0], cut, jnp.int32(0))

    def body(i, state):
        c = spans - 1 - i if reverse else i
        place = order_ref[c]
        device, slot = place // slots, place % slots
        at = pl.ds(pl.multiple_of(slot * rows, rows), rows)
        out_ref[device, at, :] = state.astype(BF16)
        carried = jnp.where(cont[c] > 0, factor * state, 0.0)
        return carried + in_ref[device, at, :].astype(F32)

    lax.fori_loop(0, spans, body, jnp.zeros((rows, LANES), F32))


def fill_decay(decay, rate_ref, heads, span):
    j = lax.broadcasted_iota(jnp.int32, (span, span), 0)
    l = lax.broadcasted_iota(jnp.int32, (span, span), 1)
    spread = (j - l).astype(F32)
    for h in range(heads):
        decay[h] = jnp.where(
            spread >= 0.0, jnp.exp(-rate_ref[h] * jnp.maximum(spread, 0.0)), 0.0
        )


def local_kernel(heads, len_ref, home_ref, rate_ref, q_ref, k_ref, v_ref, out_ref, decay):
    step = pl.program_id(0)
    span = q_ref.shape[0]

    @pl.when(step == 0)
    def _():
        fill_decay(decay, rate_ref, heads, span)

    seg = segment_row(len_ref, home_ref[step] * span, span)
    same = row_to_cols(seg, span) == seg
    for h in range(heads):
        cols = head_cols(h)
        scores = dot(q_ref[:, cols], k_ref[:, cols], 1, 1)
        mixing = (scores * jnp.where(same, decay[h], 0.0)).astype(BF16)
        out_ref[:, cols] = dot(mixing, v_ref[:, cols], 1, 0).astype(BF16)


def output_kernel(
    heads, rows, len_ref, home_ref, rate_ref, gain_ref, q_ref, u_ref, inner_ref, prev_ref, out_ref, sums_ref, table
):
    step = pl.program_id(0)
    span = q_ref.shape[0]

    @pl.when(step == 0)
    def _():
        for h in range(heads):
            table[h] = query_table(rate_ref[h], span)

    first, _ = doc_bounds(len_ref, home_ref[step] * span, span)
    live = token_index(span) < first
    squares = jnp.zeros((span, LANES), F32)
    crossed = jnp.zeros((span, LANES), F32)
    for h in range(heads):
        cols = head_cols(h)
        outer = dot(q_ref[:, cols], get_state(prev_ref, h, rows), 1, 0)
        attn = inner_ref[:, cols].astype(F32) + jnp.where(live, table[h], 0.0) * outer
        out_ref[:, cols] = attn.astype(BF16)
        squares += attn * attn
        crossed += gain_ref[:, cols] * u_ref[:, cols].astype(F32) * attn
    sums_ref[0, 0:1, :] = cols_to_row(squares)
    sums_ref[0, 1:2, :] = cols_to_row(crossed)


def cotangent_kernel(
    heads, rows, channels, len_ref, home_ref, rate_ref, gain_ref, sums_ref, q_ref, u_ref, attn_ref, g_ref, out_ref, table
):
    step = pl.program_id(0)
    span = q_ref.shape[0]

    @pl.when(step == 0)
    def _():
        for h in range(heads):
            table[h] = query_table(rate_ref[h], span)

    total = jnp.sum(sums_ref[:, 0], axis=0)
    scaling = 1.0 / jnp.sqrt(total[0:1] / channels + EPSILON)
    pulled = total[1:2] / channels
    direct = row_to_cols(scaling, LANES)
    along = row_to_cols(scaling * scaling * scaling * pulled, LANES)
    first, _ = doc_bounds(len_ref, home_ref[step] * span, span)
    live = token_index(span) < first
    for h in range(heads):
        cols = head_cols(h)
        grad = direct * gain_ref[:, cols] * u_ref[:, cols].astype(F32)
        grad = grad - along * attn_ref[:, cols].astype(F32)
        grad = grad.astype(BF16)
        g_ref[:, cols] = grad
        weighted = (jnp.where(live, table[h], 0.0) * grad.astype(F32)).astype(BF16)
        put_state(out_ref, step, h, rows, dot(q_ref[:, cols], weighted, 0, 0).astype(BF16))


def inner_grads_kernel(
    heads, rows, len_ref, home_ref, rate_ref, q_ref, k_ref, v_ref, g_ref, prev_ref,
    dq_ref, dk_ref, dv_ref, decay, table,
):
    step = pl.program_id(0)
    span = q_ref.shape[0]

    @pl.when(step == 0)
    def _():
        fill_decay(decay, rate_ref, heads, span)
        for h in range(heads):
            table[h] = query_table(rate_ref[h], span)

    seg = segment_row(len_ref, home_ref[step] * span, span)
    same = row_to_cols(seg, span) == seg
    first, _ = doc_bounds(len_ref, home_ref[step] * span, span)
    live = token_index(span) < first
    for h in range(heads):
        cols = head_cols(h)
        q, k, v, g = q_ref[:, cols], k_ref[:, cols], v_ref[:, cols], g_ref[:, cols]
        mask = jnp.where(same, decay[h], 0.0)
        mixing = (dot(q, k, 1, 1) * mask).astype(BF16)
        score_grad = (dot(g, v, 1, 1) * mask).astype(BF16)
        outer = dot(g, get_state(prev_ref, h, rows), 1, 1)
        dq = dot(score_grad, k, 1, 0) + jnp.where(live, table[h], 0.0) * outer
        dq_ref[:, cols] = dq.astype(BF16)
        dk_ref[:, cols] = dot(score_grad, q, 0, 0).astype(BF16)
        dv_ref[:, cols] = dot(mixing, g, 0, 0).astype(BF16)


def outer_grads_kernel(
    heads, rows, len_ref, home_ref, rate_ref, k_ref, v_ref, after_ref, dk_in, dv_in, dk_ref, dv_ref, table
):
    step = pl.program_id(0)
    span = k_ref.shape[0]

    @pl.when(step == 0)
    def _():
        for h in range(heads):
            table[h] = key_table(rate_ref[h], span)

    _, last = doc_bounds(len_ref, home_ref[step] * span, span)
    live = token_index(span) >= last
    for h in range(heads):
        cols = head_cols(h)
        side = jnp.where(live, table[h], 0.0)
        after = get_state(after_ref, h, rows)
        dk = dk_in[:, cols].astype(F32) + side * dot(v_ref[:, cols], after, 1, 1)
        dv = dv_in[:, cols].astype(F32) + side * dot(k_ref[:, cols], after, 1, 0)
        dk_ref[:, cols] = dk.astype(BF16)
        dv_ref[:, cols] = dv.astype(BF16)


def exchange(blocks):
    return lax.all_to_all(blocks, "seq", split_axis=0, concat_axis=0, tiled=True)


def shards(query, key, value, upstream, norm_gain, decay_rate, document_lengths, group_home):
    devices = lax.axis_size("seq")
    tokens, width = query.shape
    heads = width // HEAD_SIZE
    slots = group_home.shape[0]
    span = tokens // slots
    spans = slots * devices
    rows = width // devices
    channels = width * lax.axis_size("head")
    params = pltpu.CompilerParams(vmem_limit_bytes=60 << 20)
    roomy = pltpu.CompilerParams(vmem_limit_bytes=16 << 20)

    smem = pl.BlockSpec(memory_space=pltpu.SMEM)
    tok = pl.BlockSpec((span, width), lambda i: (i, 0))
    gain_spec = pl.BlockSpec((1, width), lambda i: (0, 0))
    state_spec = pl.BlockSpec((devices, 1, rows, LANES), lambda i: (0, i, 0, 0))
    gain = norm_gain.reshape(1, width)

    def whole(shape):
        return pl.BlockSpec(shape, lambda i: (0,) * len(shape))

    def shaped(shape, dtype):
        return jax.ShapeDtypeStruct(shape, dtype)

    side_table = pltpu.VMEM((heads, span, LANES), F32)
    decay_table = pltpu.VMEM((heads, span, span), F32)
    packed = (devices, slots * rows + TAIL, LANES)
    plain = (devices, slots * rows, LANES)

    sent = pl.pallas_call(
        functools.partial(summary_kernel, heads, rows),
        grid=(slots,),
        in_specs=[smem, smem, smem, tok, tok],
        out_specs=whole(packed),
        out_shape=shaped(packed, BF16),
        scratch_shapes=[side_table],
        compiler_params=params,
        name="summaries",
    )(document_lengths, group_home, decay_rate, key, value)

    arrived = exchange(sent)

    inner = pl.pallas_call(
        functools.partial(local_kernel, heads),
        grid=(slots,),
        in_specs=[smem, smem, smem, tok, tok, tok],
        out_specs=tok,
        out_shape=shaped((tokens, width), BF16),
        scratch_shapes=[decay_table],
        compiler_params=params,
        name="inner",
    )(document_lengths, group_home, decay_rate, query, key, value)

    homes = arrived[:, slots * rows, :slots].astype(jnp.int32).reshape(-1)
    hits = homes[None, :] == jnp.arange(spans, dtype=jnp.int32)[:, None]
    order = jnp.sum(jnp.where(hits, jnp.arange(spans, dtype=jnp.int32)[None, :], 0), axis=1)

    def scan(blocks, reverse):
        return pl.pallas_call(
            functools.partial(scan_kernel, rows, spans, span, reverse),
            grid=(1,),
            in_specs=[smem, smem, smem, whole(blocks.shape)],
            out_specs=whole(plain),
            out_shape=shaped(plain, BF16),
            scratch_shapes=[pltpu.SMEM((spans + 1,), jnp.int32)],
            compiler_params=roomy,
            name="scan",
        )(document_lengths, order, decay_rate, blocks)

    prev = exchange(scan(arrived, False)).reshape(devices, slots, rows, LANES)

    attn, sums = pl.pallas_call(
        functools.partial(output_kernel, heads, rows),
        grid=(slots,),
        in_specs=[smem, smem, smem, gain_spec, tok, tok, tok, state_spec],
        out_specs=[tok, pl.BlockSpec((1, 2, span), lambda i: (i, 0, 0))],
        out_shape=[shaped((tokens, width), BF16), shaped((slots, 2, span), F32)],
        scratch_shapes=[side_table],
        compiler_params=params,
        name="output",
    )(document_lengths, group_home, decay_rate, gain, query, upstream, inner, prev)

    sums = lax.all_gather(sums, "head")

    grad_in, rev_sent = pl.pallas_call(
        functools.partial(cotangent_kernel, heads, rows, channels),
        grid=(slots,),
        in_specs=[
            smem, smem, smem, gain_spec,
            pl.BlockSpec((sums.shape[0], 1, 2, span), lambda i: (0, i, 0, 0)),
            tok, tok, tok,
        ],
        out_specs=[tok, whole(plain)],
        out_shape=[shaped((tokens, width), BF16), shaped(plain, BF16)],
        scratch_shapes=[side_table],
        compiler_params=params,
        name="cotangent",
    )(document_lengths, group_home, decay_rate, gain, sums, query, upstream, attn)

    rev_arrived = exchange(rev_sent)

    query_grad, key_inner, value_inner = pl.pallas_call(
        functools.partial(inner_grads_kernel, heads, rows),
        grid=(slots,),
        in_specs=[smem, smem, smem, tok, tok, tok, tok, state_spec],
        out_specs=[tok, tok, tok],
        out_shape=[shaped((tokens, width), BF16), shaped((tokens, width), BF16), shaped((tokens, width), BF16)],
        scratch_shapes=[decay_table, side_table],
        compiler_params=params,
        name="inner_grads",
    )(document_lengths, group_home, decay_rate, query, key, value, grad_in, prev)

    after = exchange(scan(rev_arrived, True)).reshape(devices, slots, rows, LANES)

    key_grad, value_grad = pl.pallas_call(
        functools.partial(outer_grads_kernel, heads, rows),
        grid=(slots,),
        in_specs=[smem, smem, smem, tok, tok, state_spec, tok, tok],
        out_specs=[tok, tok],
        out_shape=[shaped((tokens, width), BF16)] * 2,
        scratch_shapes=[side_table],
        compiler_params=params,
        name="outer_grads",
    )(document_lengths, group_home, decay_rate, key, value, after, key_inner, value_inner)
    return query_grad, key_grad, value_grad


def solution(mesh):
    in_specs = (
        P("seq", "head"),
        P("seq", "head"),
        P("seq", "head"),
        P("seq", "head"),
        P("head"),
        P("head"),
        P(),
        P("seq"),
    )
    out_specs = (P("seq", "head"), P("seq", "head"), P("seq", "head"))
    return jax.shard_map(shards, mesh=mesh, in_specs=in_specs, out_specs=out_specs, check_vma=False)
```

```python
import functools

import jax
import jax.numpy as jnp
from jax import lax
from jax.experimental import pallas as pl
from jax.experimental.pallas import tpu as pltpu
from jax.sharding import PartitionSpec as P

HEAD_SIZE = 128
LANES = 128
EPSILON = 1e-06
TAIL = 16
F32 = jnp.float32
BF16 = jnp.bfloat16


def dot(a, b, ca, cb):
    return lax.dot_general(a, b, (((ca,), (cb,)), ((), ())), preferred_element_type=F32)


def head_cols(h):
    return slice(h * HEAD_SIZE, (h + 1) * HEAD_SIZE)


def token_index(span):
    return lax.broadcasted_iota(jnp.int32, (span, LANES), 0)


def key_table(rate, span):
    return jnp.exp(-rate * (span - 1.0 - token_index(span).astype(F32)))


def query_table(rate, span):
    return jnp.exp(-rate * (token_index(span).astype(F32) + 1.0))


def row_to_cols(row, width):
    cols = jnp.transpose(jnp.broadcast_to(row, (LANES, row.shape[1])))
    return jnp.concatenate([cols] * (width // LANES), axis=1) if width > LANES else cols


def cols_to_row(cols):
    return jnp.sum(jnp.transpose(cols), axis=0, keepdims=True)


def fill_tables(len_ref, first_ref, last_ref, span):
    spans = first_ref.shape[0] - 1
    far = jnp.int32(spans * span)

    def reset(c, carry):
        first_ref[c] = far
        last_ref[c] = 0
        return carry

    def note(d, end):
        end = end + len_ref[d]
        c = lax.shift_right_logical(end, span.bit_length() - 1) if span & (span - 1) == 0 else end // span
        inside = end - c * span
        last_ref[c] = inside
        first_ref[c] = jnp.minimum(first_ref[c], inside)
        return end

    lax.fori_loop(0, spans + 1, reset, 0, unroll=8)
    lax.fori_loop(0, len_ref.shape[0], note, jnp.int32(0), unroll=4)
    first_ref[0] = 0


def put_state(out_ref, step, h, rows, value):
    chunks = HEAD_SIZE // rows
    for part in range(chunks):
        out_ref[h * chunks + part, pl.ds(pl.multiple_of(step * rows, rows), rows), :] = value[
            part * rows : (part + 1) * rows
        ]


def get_state(ref, h, rows):
    chunks = HEAD_SIZE // rows
    return ref[h * chunks : (h + 1) * chunks, 0].reshape(HEAD_SIZE, HEAD_SIZE)


def summary_kernel(
    heads, rows, len_ref, home_ref, rate_ref, k_ref, v_ref, out_ref, first_ref, last_ref, table
):
    step = pl.program_id(0)
    span = k_ref.shape[0]

    @pl.when(step == 0)
    def _():
        fill_tables(len_ref, first_ref, last_ref, span)
        for h in range(heads):
            table[h] = key_table(rate_ref[h], span)
        tail = jnp.zeros((TAIL, LANES), F32)
        lane = lax.broadcasted_iota(jnp.int32, (TAIL, LANES), 1)
        for i in range(home_ref.shape[0]):
            tail = jnp.where(lane == i, home_ref[i].astype(F32), tail)
        for d in range(out_ref.shape[0]):
            out_ref[d, out_ref.shape[1] - TAIL :, :] = tail.astype(BF16)

    live = token_index(span) >= last_ref[home_ref[step]]
    for h in range(heads):
        side = jnp.where(live, table[h], 0.0)
        weighted = (side * v_ref[:, head_cols(h)].astype(F32)).astype(BF16)
        put_state(out_ref, step, h, rows, dot(k_ref[:, head_cols(h)], weighted, 0, 0).astype(BF16))


def scan_kernel(rows, spans, span, reverse, first_ref, order_ref, rate_ref, in_ref, out_ref):
    slots = out_ref.shape[1] // rows
    head = (lax.axis_index("seq") * rows) // HEAD_SIZE
    factor = jnp.exp(jnp.full((8, LANES), -rate_ref[head] * span, F32))[0:1]

    def body(i, state):
        c = spans - 1 - i if reverse else i
        place = order_ref[c]
        device, slot = place // slots, place % slots
        at = pl.ds(pl.multiple_of(slot * rows, rows), rows)
        out_ref[device, at, :] = state.astype(BF16)
        carried = jnp.where(first_ref[c] >= span, factor * state, 0.0)
        return carried + in_ref[device, at, :].astype(F32)

    lax.fori_loop(0, spans, body, jnp.zeros((rows, LANES), F32))


def fill_decay(decay, rate_ref, heads, span):
    j = lax.broadcasted_iota(jnp.int32, (span, span), 0)
    l = lax.broadcasted_iota(jnp.int32, (span, span), 1)
    spread = (j - l).astype(F32)
    for h in range(heads):
        decay[h] = jnp.where(
            spread >= 0.0, jnp.exp(-rate_ref[h] * jnp.maximum(spread, 0.0)), 0.0
        )


def local_kernel(heads, rate_ref, seg_ref, q_ref, k_ref, v_ref, out_ref, decay):
    step = pl.program_id(0)
    span = q_ref.shape[0]

    @pl.when(step == 0)
    def _():
        fill_decay(decay, rate_ref, heads, span)

    seg = seg_ref[0]
    same = row_to_cols(seg, span) == seg
    for h in range(heads):
        cols = head_cols(h)
        scores = dot(q_ref[:, cols], k_ref[:, cols], 1, 1)
        mixing = (scores * jnp.where(same, decay[h], 0.0)).astype(BF16)
        out_ref[:, cols] = dot(mixing, v_ref[:, cols], 1, 0).astype(BF16)


def output_kernel(
    heads, rows, first_ref, home_ref, rate_ref, gain_ref, q_ref, u_ref, inner_ref, prev_ref, out_ref, sums_ref, table
):
    step = pl.program_id(0)
    span = q_ref.shape[0]

    @pl.when(step == 0)
    def _():
        for h in range(heads):
            table[h] = query_table(rate_ref[h], span)

    live = token_index(span) < first_ref[home_ref[step]]
    squares = jnp.zeros((span, LANES), F32)
    crossed = jnp.zeros((span, LANES), F32)
    for h in range(heads):
        cols = head_cols(h)
        outer = dot(q_ref[:, cols], get_state(prev_ref, h, rows), 1, 0)
        attn = inner_ref[:, cols].astype(F32) + jnp.where(live, table[h], 0.0) * outer
        out_ref[:, cols] = attn.astype(BF16)
        squares += attn * attn
        crossed += gain_ref[:, cols] * u_ref[:, cols].astype(F32) * attn
    sums_ref[0, 0:1, :] = cols_to_row(squares)
    sums_ref[0, 1:2, :] = cols_to_row(crossed)


def cotangent_kernel(
    heads, rows, channels, first_ref, home_ref, rate_ref, gain_ref, sums_ref, q_ref, u_ref, attn_ref, g_ref, out_ref, table
):
    step = pl.program_id(0)
    span = q_ref.shape[0]

    @pl.when(step == 0)
    def _():
        for h in range(heads):
            table[h] = query_table(rate_ref[h], span)

    total = jnp.sum(sums_ref[:, 0], axis=0)
    scaling = 1.0 / jnp.sqrt(total[0:1] / channels + EPSILON)
    pulled = total[1:2] / channels
    direct = row_to_cols(scaling, LANES)
    along = row_to_cols(scaling * scaling * scaling * pulled, LANES)
    live = token_index(span) < first_ref[home_ref[step]]
    for h in range(heads):
        cols = head_cols(h)
        grad = direct * gain_ref[:, cols] * u_ref[:, cols].astype(F32)
        grad = grad - along * attn_ref[:, cols].astype(F32)
        grad = grad.astype(BF16)
        g_ref[:, cols] = grad
        weighted = (jnp.where(live, table[h], 0.0) * grad.astype(F32)).astype(BF16)
        put_state(out_ref, step, h, rows, dot(q_ref[:, cols], weighted, 0, 0).astype(BF16))


def inner_grads_kernel(
    heads, rows, first_ref, home_ref, rate_ref, seg_ref, q_ref, k_ref, v_ref, g_ref, prev_ref,
    dq_ref, dk_ref, dv_ref, decay, table,
):
    step = pl.program_id(0)
    span = q_ref.shape[0]

    @pl.when(step == 0)
    def _():
        fill_decay(decay, rate_ref, heads, span)
        for h in range(heads):
            table[h] = query_table(rate_ref[h], span)

    seg = seg_ref[0]
    same = row_to_cols(seg, span) == seg
    live = token_index(span) < first_ref[home_ref[step]]
    for h in range(heads):
        cols = head_cols(h)
        q, k, v, g = q_ref[:, cols], k_ref[:, cols], v_ref[:, cols], g_ref[:, cols]
        mask = jnp.where(same, decay[h], 0.0)
        mixing = (dot(q, k, 1, 1) * mask).astype(BF16)
        score_grad = (dot(g, v, 1, 1) * mask).astype(BF16)
        outer = dot(g, get_state(prev_ref, h, rows), 1, 1)
        dq = dot(score_grad, k, 1, 0) + jnp.where(live, table[h], 0.0) * outer
        dq_ref[:, cols] = dq.astype(BF16)
        dk_ref[:, cols] = dot(score_grad, q, 0, 0).astype(BF16)
        dv_ref[:, cols] = dot(mixing, g, 0, 0).astype(BF16)


def outer_grads_kernel(
    heads, rows, last_ref, home_ref, rate_ref, k_ref, v_ref, after_ref, dk_in, dv_in, dk_ref, dv_ref, table
):
    step = pl.program_id(0)
    span = k_ref.shape[0]

    @pl.when(step == 0)
    def _():
        for h in range(heads):
            table[h] = key_table(rate_ref[h], span)

    live = token_index(span) >= last_ref[home_ref[step]]
    for h in range(heads):
        cols = head_cols(h)
        side = jnp.where(live, table[h], 0.0)
        after = get_state(after_ref, h, rows)
        dk = dk_in[:, cols].astype(F32) + side * dot(v_ref[:, cols], after, 1, 1)
        dv = dv_in[:, cols].astype(F32) + side * dot(k_ref[:, cols], after, 1, 0)
        dk_ref[:, cols] = dk.astype(BF16)
        dv_ref[:, cols] = dv.astype(BF16)


def exchange(blocks):
    return lax.all_to_all(blocks, "seq", split_axis=0, concat_axis=0, tiled=True)


def shards(query, key, value, upstream, norm_gain, decay_rate, document_lengths, group_home):
    devices = lax.axis_size("seq")
    tokens, width = query.shape
    heads = width // HEAD_SIZE
    slots = group_home.shape[0]
    span = tokens // slots
    spans = slots * devices
    rows = width // devices
    channels = width * lax.axis_size("head")
    alone = pltpu.CompilerParams(vmem_limit_bytes=60 << 20)
    params = pltpu.CompilerParams(vmem_limit_bytes=52 << 20)
    roomy = pltpu.CompilerParams(vmem_limit_bytes=16 << 20)

    doc_ends = jnp.cumsum(document_lengths)
    positions = (group_home * span)[:, None] + jnp.arange(span, dtype=jnp.int32)[None, :]
    seg = jnp.sum((doc_ends <= positions[..., None]).astype(F32), axis=-1).reshape(slots, 1, span)

    smem = pl.BlockSpec(memory_space=pltpu.SMEM)
    seg_spec = pl.BlockSpec((1, 1, span), lambda i: (i, 0, 0))
    spans_table = jax.ShapeDtypeStruct((spans + 1,), jnp.int32)
    tok = pl.BlockSpec((span, width), lambda i: (i, 0))
    gain_spec = pl.BlockSpec((1, width), lambda i: (0, 0))
    state_spec = pl.BlockSpec((devices, 1, rows, LANES), lambda i: (0, i, 0, 0))
    gain = norm_gain.reshape(1, width)

    def whole(shape):
        return pl.BlockSpec(shape, lambda i: (0,) * len(shape))

    def shaped(shape, dtype):
        return jax.ShapeDtypeStruct(shape, dtype)

    side_table = pltpu.VMEM((heads, span, LANES), F32)
    decay_table = pltpu.VMEM((heads, span, span), F32)
    packed = (devices, slots * rows + TAIL, LANES)
    plain = (devices, slots * rows, LANES)

    sent, first, last = pl.pallas_call(
        functools.partial(summary_kernel, heads, rows),
        grid=(slots,),
        in_specs=[smem, smem, smem, tok, tok],
        out_specs=[whole(packed), smem, smem],
        out_shape=[shaped(packed, BF16), spans_table, spans_table],
        scratch_shapes=[side_table],
        compiler_params=alone,
        name="summaries",
    )(document_lengths, group_home, decay_rate, key, value)

    arrived = exchange(sent)

    inner = pl.pallas_call(
        functools.partial(local_kernel, heads),
        grid=(slots,),
        in_specs=[smem, seg_spec, tok, tok, tok],
        out_specs=tok,
        out_shape=shaped((tokens, width), BF16),
        scratch_shapes=[decay_table],
        compiler_params=params,
        name="inner",
    )(decay_rate, seg, query, key, value)

    homes = arrived[:, slots * rows, :slots].astype(jnp.int32).reshape(-1)
    hits = homes[None, :] == jnp.arange(spans, dtype=jnp.int32)[:, None]
    order = jnp.sum(jnp.where(hits, jnp.arange(spans, dtype=jnp.int32)[None, :], 0), axis=1)

    def scan(blocks, reverse):
        return pl.pallas_call(
            functools.partial(scan_kernel, rows, spans, span, reverse),
            grid=(1,),
            in_specs=[smem, smem, smem, whole(blocks.shape)],
            out_specs=whole(plain),
            out_shape=shaped(plain, BF16),
            compiler_params=roomy,
            name="scan",
        )(first, order, decay_rate, blocks)

    prev = exchange(scan(arrived, False)).reshape(devices, slots, rows, LANES)

    attn, sums = pl.pallas_call(
        functools.partial(output_kernel, heads, rows),
        grid=(slots,),
        in_specs=[smem, smem, smem, gain_spec, tok, tok, tok, state_spec],
        out_specs=[tok, pl.BlockSpec((1, 2, span), lambda i: (i, 0, 0))],
        out_shape=[shaped((tokens, width), BF16), shaped((slots, 2, span), F32)],
        scratch_shapes=[side_table],
        compiler_params=params,
        name="output",
    )(first, group_home, decay_rate, gain, query, upstream, inner, prev)

    sums = lax.all_gather(sums, "head")

    grad_in, rev_sent = pl.pallas_call(
        functools.partial(cotangent_kernel, heads, rows, channels),
        grid=(slots,),
        in_specs=[
            smem, smem, smem, gain_spec,
            pl.BlockSpec((sums.shape[0], 1, 2, span), lambda i: (0, i, 0, 0)),
            tok, tok, tok,
        ],
        out_specs=[tok, whole(plain)],
        out_shape=[shaped((tokens, width), BF16), shaped(plain, BF16)],
        scratch_shapes=[side_table],
        compiler_params=params,
        name="cotangent",
    )(first, group_home, decay_rate, gain, sums, query, upstream, attn)

    rev_arrived = exchange(rev_sent)

    query_grad, key_inner, value_inner = pl.pallas_call(
        functools.partial(inner_grads_kernel, heads, rows),
        grid=(slots,),
        in_specs=[smem, smem, smem, seg_spec, tok, tok, tok, tok, state_spec],
        out_specs=[tok, tok, tok],
        out_shape=[shaped((tokens, width), BF16), shaped((tokens, width), BF16), shaped((tokens, width), BF16)],
        scratch_shapes=[decay_table, side_table],
        compiler_params=params,
        name="inner_grads",
    )(first, group_home, decay_rate, seg, query, key, value, grad_in, prev)

    after = exchange(scan(rev_arrived, True)).reshape(devices, slots, rows, LANES)

    key_grad, value_grad = pl.pallas_call(
        functools.partial(outer_grads_kernel, heads, rows),
        grid=(slots,),
        in_specs=[smem, smem, smem, tok, tok, state_spec, tok, tok],
        out_specs=[tok, tok],
        out_shape=[shaped((tokens, width), BF16)] * 2,
        scratch_shapes=[side_table],
        compiler_params=params,
        name="outer_grads",
    )(last, group_home, decay_rate, key, value, after, key_inner, value_inner)
    return query_grad, key_grad, value_grad


def solution(mesh):
    in_specs = (
        P("seq", "head"),
        P("seq", "head"),
        P("seq", "head"),
        P("seq", "head"),
        P("head"),
        P("head"),
        P(),
        P("seq"),
    )
    out_specs = (P("seq", "head"), P("seq", "head"), P("seq", "head"))
    return jax.shard_map(shards, mesh=mesh, in_specs=in_specs, out_specs=out_specs, check_vma=False)
```

```python
import functools

import jax
import jax.numpy as jnp
from jax import lax
from jax.experimental import pallas as pl
from jax.experimental.pallas import tpu as pltpu
from jax.sharding import PartitionSpec as P

HEAD_SIZE = 128
LANES = 128
EPSILON = 1e-06
LIMIT = 60
HANDOFF = 54
RECEIVE = 40
LASTING = 52
TAIL = 16
F32 = jnp.float32
BF16 = jnp.bfloat16


def dot(a, b, ca, cb):
    return lax.dot_general(a, b, (((ca,), (cb,)), ((), ())), preferred_element_type=F32)


def head_cols(h):
    return slice(h * HEAD_SIZE, (h + 1) * HEAD_SIZE)


def token_index(span):
    return lax.broadcasted_iota(jnp.int32, (span, LANES), 0)


def key_table(rate, span):
    return jnp.exp(-rate * (span - 1.0 - token_index(span).astype(F32)))


def query_table(rate, span):
    return jnp.exp(-rate * (token_index(span).astype(F32) + 1.0))


def row_to_cols(row, width):
    cols = jnp.transpose(jnp.broadcast_to(row, (LANES, row.shape[1])))
    return jnp.concatenate([cols] * (width // LANES), axis=1) if width > LANES else cols


def cols_to_row(cols):
    return jnp.sum(jnp.transpose(cols), axis=0, keepdims=True)


def fill_tables(len_ref, first_ref, last_ref, span):
    spans = first_ref.shape[0] - 1
    far = jnp.int32(spans * span)

    def reset(c, carry):
        first_ref[c] = far
        last_ref[c] = 0
        return carry

    def note(d, end):
        end = end + len_ref[d]
        c = lax.shift_right_logical(end, span.bit_length() - 1) if span & (span - 1) == 0 else end // span
        inside = end - c * span
        last_ref[c] = inside
        first_ref[c] = jnp.minimum(first_ref[c], inside)
        return end

    lax.fori_loop(0, spans + 1, reset, 0, unroll=8)
    lax.fori_loop(0, len_ref.shape[0], note, jnp.int32(0), unroll=4)
    first_ref[0] = 0


def tokens_at(i, span):
    return pl.ds(pl.multiple_of(i * span, span), span)


def rows_at(i, rows):
    return pl.ds(pl.multiple_of(i * rows, rows), rows)


def put_state(ref, i, h, rows, value):
    chunks = HEAD_SIZE // rows
    for part in range(chunks):
        ref[h * chunks + part, rows_at(i, rows), :] = value[part * rows : (part + 1) * rows]


def get_state(ref, i, h, rows):
    chunks = HEAD_SIZE // rows
    return ref[h * chunks : (h + 1) * chunks, rows_at(i, rows), :].reshape(HEAD_SIZE, HEAD_SIZE)


def span_copies(i, span, sources, targets, sem):
    at = tokens_at(i, span)
    return [
        pltpu.make_async_copy(source.at[at], target.at[at], sem.at[a, i])
        for a, (source, target) in enumerate(zip(sources, targets))
    ]


def start_all(copies):
    for copy in copies:
        copy.start()


def wait_all(copies):
    for copy in copies:
        copy.wait()


def each_span(slots, body):
    def turn(i, carry):
        body(i)
        return carry

    lax.fori_loop(0, slots, turn, 0)


def summary_kernel(
    heads, rows, span, len_ref, home_ref, rate_ref, k_hbm, v_hbm,
    sent_hbm, first_ref, last_ref, k_ref, v_ref, table, packed, sem, out_sem,
):
    slots = home_ref.shape[0]
    load = lambda i: span_copies(i, span, (k_hbm, v_hbm), (k_ref, v_ref), sem)

    def store(i):
        at = rows_at(i, rows)
        return pltpu.make_async_copy(packed.at[:, at], sent_hbm.at[:, at], out_sem.at[i])

    for i in range(slots):
        start_all(load(i))
    fill_tables(len_ref, first_ref, last_ref, span)
    for h in range(heads):
        table[h] = key_table(rate_ref[h], span)
    tail = jnp.zeros((TAIL, LANES), F32)
    lane = lax.broadcasted_iota(jnp.int32, (TAIL, LANES), 1)
    for i in range(slots):
        tail = jnp.where(lane == i, home_ref[i].astype(F32), tail)
    for d in range(packed.shape[0]):
        packed[d, slots * rows :, :] = tail.astype(BF16)
    at = pl.ds(slots * rows, TAIL)
    ending = pltpu.make_async_copy(packed.at[:, at], sent_hbm.at[:, at], out_sem.at[slots])
    ending.start()

    def body(i):
        wait_all(load(i))
        at = tokens_at(i, span)
        live = token_index(span) >= last_ref[home_ref[i]]
        for h in range(heads):
            cols = head_cols(h)
            side = jnp.where(live, table[h], 0.0)
            weighted = (side * v_ref[at, cols].astype(F32)).astype(BF16)
            put_state(packed, i, h, rows, dot(k_ref[at, cols], weighted, 0, 0).astype(BF16))
        store(i).start()

    each_span(slots, body)
    for i in range(slots):
        store(i).wait()
    ending.wait()


def scan_kernel(rows, span, reverse, first_ref, order_ref, rate_ref, in_ref, out_hbm, states, sem):
    slots = states.shape[1] // rows
    spans = order_ref.shape[0]
    head = (lax.axis_index("seq") * rows) // HEAD_SIZE
    factor = jnp.exp(jnp.full((8, LANES), -rate_ref[head] * span, F32))[0:1]

    def body(i, state):
        c = spans - 1 - i if reverse else i
        place = order_ref[c]
        device, slot = place // slots, place % slots
        at = rows_at(slot, rows)
        states[device, at, :] = state.astype(BF16)
        carried = jnp.where(first_ref[c] >= span, factor * state, 0.0)
        return carried + in_ref[device, at, :].astype(F32)

    lax.fori_loop(0, spans, body, jnp.zeros((rows, LANES), F32), unroll=4)
    done = pltpu.make_async_copy(states, out_hbm, sem)
    done.start()
    done.wait()


def fill_decay(decay, rate_ref, heads, span):
    j = lax.broadcasted_iota(jnp.int32, (span, span), 0)
    l = lax.broadcasted_iota(jnp.int32, (span, span), 1)
    spread = (j - l).astype(F32)
    for h in range(heads):
        decay[h] = jnp.where(
            spread >= 0.0, jnp.exp(-rate_ref[h] * jnp.maximum(spread, 0.0)), 0.0
        )


def local_kernel(
    heads, span, rate_ref, seg_ref, q_hbm, k_hbm, v_hbm, out_hbm,
    q_ref, k_ref, v_ref, out_ref, decay, sem, out_sem,
):
    slots = seg_ref.shape[0]
    load = lambda i: span_copies(i, span, (q_hbm, k_hbm, v_hbm), (q_ref, k_ref, v_ref), sem)
    store = lambda i: span_copies(i, span, (out_ref,), (out_hbm,), out_sem)
    for i in range(slots):
        start_all(load(i))
    fill_decay(decay, rate_ref, heads, span)

    def body(i):
        wait_all(load(i))
        at = tokens_at(i, span)
        seg = seg_ref[i]
        same = row_to_cols(seg, span) == seg
        for h in range(heads):
            cols = head_cols(h)
            scores = dot(q_ref[at, cols], k_ref[at, cols], 1, 1)
            mixing = (scores * jnp.where(same, decay[h], 0.0)).astype(BF16)
            out_ref[at, cols] = dot(mixing, v_ref[at, cols], 1, 0).astype(BF16)
        start_all(store(i))

    each_span(slots, body)
    for i in range(slots):
        wait_all(store(i))


def output_kernel(
    heads, rows, span, first_ref, home_ref, rate_ref, gain_ref, q_hbm, u_hbm, inner_hbm, prev_ref,
    out_ref, q_ref, u_ref, sums_ref, inner_ref, table, sem,
):
    slots = home_ref.shape[0]
    load = lambda i: span_copies(i, span, (q_hbm, u_hbm, inner_hbm), (q_ref, u_ref, inner_ref), sem)
    for i in range(slots):
        start_all(load(i))
    for h in range(heads):
        table[h] = query_table(rate_ref[h], span)

    def body(i):
        wait_all(load(i))
        at = tokens_at(i, span)
        live = token_index(span) < first_ref[home_ref[i]]
        squares = jnp.zeros((span, LANES), F32)
        crossed = jnp.zeros((span, LANES), F32)
        for h in range(heads):
            cols = head_cols(h)
            outer = dot(q_ref[at, cols], get_state(prev_ref, i, h, rows), 1, 0)
            attn = inner_ref[at, cols].astype(F32) + jnp.where(live, table[h], 0.0) * outer
            out_ref[at, cols] = attn
            squares += attn * attn
            crossed += gain_ref[:, cols] * u_ref[at, cols].astype(F32) * attn
        sums_ref[i, 0:1, :] = cols_to_row(squares)
        sums_ref[i, 1:2, :] = cols_to_row(crossed)

    each_span(slots, body)


def cotangent_kernel(
    heads, rows, span, channels, first_ref, home_ref, rate_ref, gain_ref, sums_ref, q_ref, u_ref, attn_ref,
    g_hbm, sent_hbm, g_ref, table, packed, g_sem, out_sem,
):
    slots = home_ref.shape[0]
    save = lambda i: span_copies(i, span, (g_ref,), (g_hbm,), g_sem)
    for h in range(heads):
        table[h] = query_table(rate_ref[h], span)

    def store(i):
        at = rows_at(i, rows)
        return pltpu.make_async_copy(packed.at[:, at], sent_hbm.at[:, at], out_sem.at[i])

    def body(i):
        at = tokens_at(i, span)
        total = jnp.sum(sums_ref[:, i], axis=0)
        scaling = 1.0 / jnp.sqrt(total[0:1] / channels + EPSILON)
        pulled = total[1:2] / channels
        direct = row_to_cols(scaling, LANES)
        along = row_to_cols(scaling * scaling * scaling * pulled, LANES)
        live = token_index(span) < first_ref[home_ref[i]]
        for h in range(heads):
            cols = head_cols(h)
            grad = direct * gain_ref[:, cols] * u_ref[at, cols].astype(F32) - along * attn_ref[at, cols]
            grad = grad.astype(BF16)
            g_ref[at, cols] = grad
            weighted = (jnp.where(live, table[h], 0.0) * grad.astype(F32)).astype(BF16)
            put_state(packed, i, h, rows, dot(q_ref[at, cols], weighted, 0, 0).astype(BF16))
        store(i).start()
        start_all(save(i))

    each_span(slots, body)
    for i in range(slots):
        store(i).wait()
        wait_all(save(i))


def inner_grads_kernel(
    heads, rows, span, first_ref, home_ref, rate_ref, seg_ref, q_hbm, k_hbm, v_hbm, g_hbm, prev_ref,
    dq_hbm, dk_hbm, dv_hbm, q_ref, k_ref, v_ref, g_ref, dq_ref, dk_ref, dv_ref, decay, table, sem, out_sem,
):
    slots = home_ref.shape[0]
    load = lambda i: span_copies(
        i, span, (q_hbm, k_hbm, v_hbm, g_hbm), (q_ref, k_ref, v_ref, g_ref), sem
    )
    store = lambda i: span_copies(i, span, (dq_ref, dk_ref, dv_ref), (dq_hbm, dk_hbm, dv_hbm), out_sem)
    for i in range(slots):
        start_all(load(i))
    fill_decay(decay, rate_ref, heads, span)
    for h in range(heads):
        table[h] = query_table(rate_ref[h], span)

    def body(i):
        wait_all(load(i))
        at = tokens_at(i, span)
        seg = seg_ref[i]
        same = row_to_cols(seg, span) == seg
        live = token_index(span) < first_ref[home_ref[i]]
        for h in range(heads):
            cols = head_cols(h)
            q, k, v, g = q_ref[at, cols], k_ref[at, cols], v_ref[at, cols], g_ref[at, cols]
            mask = jnp.where(same, decay[h], 0.0)
            mixing = (dot(q, k, 1, 1) * mask).astype(BF16)
            score_grad = (dot(g, v, 1, 1) * mask).astype(BF16)
            outer = dot(g, get_state(prev_ref, i, h, rows), 1, 1)
            dq = dot(score_grad, k, 1, 0) + jnp.where(live, table[h], 0.0) * outer
            dq_ref[at, cols] = dq.astype(BF16)
            dk_ref[at, cols] = dot(score_grad, q, 0, 0).astype(BF16)
            dv_ref[at, cols] = dot(mixing, g, 0, 0).astype(BF16)
        start_all(store(i))

    each_span(slots, body)
    for i in range(slots):
        wait_all(store(i))


def outer_grads_kernel(
    heads, rows, span, last_ref, home_ref, rate_ref, k_hbm, v_hbm, after_ref, dk_part, dv_part,
    dk_hbm, dv_hbm, k_ref, v_ref, dk_in, dv_in, dk_ref, dv_ref, table, sem, out_sem,
):
    slots = home_ref.shape[0]
    load = lambda i: span_copies(
        i, span, (k_hbm, v_hbm, dk_part, dv_part), (k_ref, v_ref, dk_in, dv_in), sem
    )
    store = lambda i: span_copies(i, span, (dk_ref, dv_ref), (dk_hbm, dv_hbm), out_sem)
    for i in range(slots):
        start_all(load(i))
    for h in range(heads):
        table[h] = key_table(rate_ref[h], span)

    def body(i):
        wait_all(load(i))
        at = tokens_at(i, span)
        live = token_index(span) >= last_ref[home_ref[i]]
        for h in range(heads):
            cols = head_cols(h)
            side = jnp.where(live, table[h], 0.0)
            after = get_state(after_ref, i, h, rows)
            dk = dk_in[at, cols].astype(F32) + side * dot(v_ref[at, cols], after, 1, 1)
            dv = dv_in[at, cols].astype(F32) + side * dot(k_ref[at, cols], after, 1, 0)
            dk_ref[at, cols] = dk.astype(BF16)
            dv_ref[at, cols] = dv.astype(BF16)
        start_all(store(i))

    each_span(slots, body)
    for i in range(slots):
        wait_all(store(i))


def exchange(blocks):
    return lax.all_to_all(blocks, "seq", split_axis=0, concat_axis=0, tiled=True)


def shards(query, key, value, upstream, norm_gain, decay_rate, document_lengths, group_home):
    devices = lax.axis_size("seq")
    tokens, width = query.shape
    heads = width // HEAD_SIZE
    slots = group_home.shape[0]
    span = tokens // slots
    spans = slots * devices
    rows = width // devices
    channels = width * lax.axis_size("head")

    doc_ends = jnp.cumsum(document_lengths)
    positions = (group_home * span)[:, None] + jnp.arange(span, dtype=jnp.int32)[None, :]
    seg = jnp.sum((doc_ends <= positions[..., None]).astype(F32), axis=-1).reshape(slots, 1, span)
    gain = norm_gain.reshape(1, width)

    smem = pl.BlockSpec(memory_space=pltpu.SMEM)
    vmem = pl.BlockSpec(memory_space=pltpu.VMEM)
    hbm = pl.BlockSpec(memory_space=pl.ANY)
    table = pltpu.VMEM((heads, span, LANES), F32)
    decay = pltpu.VMEM((heads, span, span), F32)
    packed = (devices, slots * rows + TAIL, LANES)
    plain = (devices, slots * rows, LANES)
    token_bf16 = pltpu.VMEM((tokens, width), BF16)
    token_f32 = pltpu.VMEM((tokens, width), F32)
    per_slot = pltpu.SemaphoreType.DMA((slots,))

    def sems(count):
        return pltpu.SemaphoreType.DMA((count, slots))

    def shaped(shape, dtype):
        return jax.ShapeDtypeStruct(shape, dtype)

    def call(kernel, name, limit, flops, in_specs, out_specs, out_shape, scratch, *static):
        return pl.pallas_call(
            functools.partial(kernel, *static),
            in_specs=in_specs,
            out_specs=out_specs,
            out_shape=out_shape,
            scratch_shapes=scratch,
            compiler_params=pltpu.CompilerParams(vmem_limit_bytes=limit << 20),
            cost_estimate=pl.CostEstimate(flops=flops, bytes_accessed=0, transcendentals=0),
            name=name,
        )

    work = 2 * tokens * width * span
    spans_table = shaped((spans + 1,), jnp.int32)
    sent, first, last = call(
        summary_kernel, "summaries", 60, work // 2,
        [smem, smem, smem, hbm, hbm],
        [hbm, smem, smem],
        [shaped(packed, BF16), spans_table, spans_table],
        [token_bf16] * 2 + [table, pltpu.VMEM(packed, BF16), sems(2), pltpu.SemaphoreType.DMA((slots + 1,))],
        heads, rows, span,
    )(document_lengths, group_home, decay_rate, key, value)

    arrived = exchange(sent)

    inner = call(
        local_kernel, "inner", LIMIT, 2 * work,
        [smem, vmem, hbm, hbm, hbm],
        hbm,
        shaped((tokens, width), BF16),
        [token_bf16] * 4 + [decay, sems(3), sems(1)],
        heads, span,
    )(decay_rate, seg, query, key, value)

    homes = arrived[:, slots * rows, :slots].astype(jnp.int32).reshape(-1)
    hits = homes[None, :] == jnp.arange(spans, dtype=jnp.int32)[:, None]
    order = jnp.sum(jnp.where(hits, jnp.arange(spans, dtype=jnp.int32)[None, :], 0), axis=1)

    def scan(blocks, reverse):
        return call(
            scan_kernel, "scan", 8, work // 8,
            [smem, smem, smem, vmem],
            hbm,
            shaped(plain, BF16),
            [pltpu.VMEM(plain, BF16), pltpu.SemaphoreType.DMA],
            rows, span, reverse,
        )(first, order, decay_rate, blocks)

    prev = exchange(scan(arrived, False))

    attn, query_v, upstream_v, sums = call(
        output_kernel, "output", HANDOFF, work // 2,
        [smem, smem, smem, vmem, hbm, hbm, hbm, vmem],
        [vmem] * 4,
        [token_f32, token_bf16, token_bf16, shaped((slots, 2, span), F32)],
        [token_bf16, table, sems(3)],
        heads, rows, span,
    )(first, group_home, decay_rate, gain, query, upstream, inner, prev)

    sums = lax.all_gather(sums, "head")

    grad_in, rev_sent = call(
        cotangent_kernel, "cotangent", RECEIVE, work // 2,
        [smem, smem, smem, vmem, vmem, vmem, vmem, vmem],
        [hbm, hbm],
        [shaped((tokens, width), BF16), shaped(plain, BF16)],
        [token_bf16, table, pltpu.VMEM(plain, BF16), sems(1), per_slot],
        heads, rows, span, channels,
    )(first, group_home, decay_rate, gain, sums, query_v, upstream_v, attn)

    rev_arrived = exchange(rev_sent)

    query_grad, key_inner, value_inner = call(
        inner_grads_kernel, "inner_grads", LASTING, 6 * work,
        [smem, smem, smem, vmem, hbm, hbm, hbm, hbm, vmem],
        [hbm] * 3,
        [shaped((tokens, width), BF16)] * 3,
        [token_bf16] * 7 + [decay, table, sems(4), sems(3)],
        heads, rows, span,
    )(first, group_home, decay_rate, seg, query, key, value, grad_in, prev)

    after = exchange(scan(rev_arrived, True))

    key_grad, value_grad = call(
        outer_grads_kernel, "outer_grads", LASTING, work,
        [smem, smem, smem, hbm, hbm, vmem, hbm, hbm],
        [hbm, hbm],
        [shaped((tokens, width), BF16)] * 2,
        [token_bf16] * 6 + [table, sems(4), sems(2)],
        heads, rows, span,
    )(last, group_home, decay_rate, key, value, after, key_inner, value_inner)
    return query_grad, key_grad, value_grad


def solution(mesh):
    in_specs = (
        P("seq", "head"),
        P("seq", "head"),
        P("seq", "head"),
        P("seq", "head"),
        P("head"),
        P("head"),
        P(),
        P("seq"),
    )
    out_specs = (P("seq", "head"), P("seq", "head"), P("seq", "head"))
    return jax.shard_map(shards, mesh=mesh, in_specs=in_specs, out_specs=out_specs, check_vma=False)
```

```python
import functools

import jax
import jax.numpy as jnp
from jax import lax
from jax.experimental import pallas as pl
from jax.experimental.pallas import tpu as pltpu
from jax.sharding import PartitionSpec as P


HEAD_SIZE = 128
LANES = 128
EPSILON = 1e-06
TAIL = 16
LIMIT = 60
ROOMY = 16
HANDOFF = 54
RECEIVE = 40
LASTING = 52
F32 = jnp.float32
BF16 = jnp.bfloat16


def dot(a, b, ca, cb):
    return lax.dot_general(a, b, (((ca,), (cb,)), ((), ())), preferred_element_type=F32)


def head_cols(h):
    return slice(h * HEAD_SIZE, (h + 1) * HEAD_SIZE)


def token_index(span):
    return lax.broadcasted_iota(jnp.int32, (span, LANES), 0)


def fill_key_table(table, rate_ref, base, span):
    for h in range(table.shape[0]):
        table[h] = jnp.exp(-rate_ref[base + h] * (span - 1.0 - token_index(span).astype(F32)))


def fill_query_table(table, rate_ref, base, span):
    for h in range(table.shape[0]):
        table[h] = jnp.exp(-rate_ref[base + h] * (token_index(span).astype(F32) + 1.0))


def fill_decay(decay, rate_ref, base, span):
    j = lax.broadcasted_iota(jnp.int32, (span, span), 0)
    l = lax.broadcasted_iota(jnp.int32, (span, span), 1)
    spread = (j - l).astype(F32)
    for h in range(decay.shape[0]):
        falling = jnp.exp(-rate_ref[base + h] * jnp.maximum(spread, 0.0))
        decay[h] = jnp.where(spread >= 0.0, falling, 0.0)


def row_to_cols(row, width):
    cols = jnp.transpose(jnp.broadcast_to(row, (LANES, row.shape[1])))
    return jnp.concatenate([cols] * (width // LANES), axis=1) if width > LANES else cols


def cols_to_row(cols):
    return jnp.sum(jnp.transpose(cols), axis=0, keepdims=True)


def fill_tables(len_ref, first_ref, last_ref, span):
    spans = first_ref.shape[0] - 1
    far = jnp.int32(spans * span)

    def reset(c, carry):
        first_ref[c] = far
        last_ref[c] = 0
        return carry

    def note(d, end):
        end = end + len_ref[d]
        c = lax.shift_right_logical(end, span.bit_length() - 1) if span & (span - 1) == 0 else end // span
        inside = end - c * span
        last_ref[c] = inside
        first_ref[c] = jnp.minimum(first_ref[c], inside)
        return end

    lax.fori_loop(0, spans + 1, reset, 0, unroll=8)
    lax.fori_loop(0, len_ref.shape[0], note, jnp.int32(0), unroll=4)
    first_ref[0] = 0


def tokens_at(i, span):
    return pl.ds(pl.multiple_of(i * span, span), span)


def rows_at(i, rows):
    return pl.ds(pl.multiple_of(i * rows, rows), rows)


def put_state(ref, i, h, rows, value):
    chunks = HEAD_SIZE // rows
    for part in range(chunks):
        ref[h * chunks + part, rows_at(i, rows), :] = value[part * rows : (part + 1) * rows]


def get_state(ref, i, h, rows):
    chunks = HEAD_SIZE // rows
    return ref[h * chunks : (h + 1) * chunks, rows_at(i, rows), :].reshape(HEAD_SIZE, HEAD_SIZE)


def span_copies(i, span, sources, targets, sem):
    at = tokens_at(i, span)
    return [
        pltpu.make_async_copy(source.at[at], target.at[at], sem.at[a, i])
        for a, (source, target) in enumerate(zip(sources, targets))
    ]


def start_all(copies):
    for copy in copies:
        copy.start()


def wait_all(copies):
    for copy in copies:
        copy.wait()


def each_span(slots, body):
    def turn(i, carry):
        body(i)
        return carry

    lax.fori_loop(0, slots, turn, 0)


def columns(base, heads):
    return pl.ds(base * HEAD_SIZE, heads * HEAD_SIZE)


def to_blocks(packed, blocks, sem):
    me = lax.axis_index("seq")
    return [
        pltpu.make_async_copy(packed.at[jnp.bitwise_xor(me, k)], block, sem.at[k])
        for k, block in enumerate(blocks)
    ]


def from_blocks(blocks, packed, sem):
    me = lax.axis_index("seq")
    return [
        pltpu.make_async_copy(block, packed.at[jnp.bitwise_xor(me, k)], sem.at[k])
        for k, block in enumerate(blocks)
    ]


def summary_kernel(base, heads, rows, span, lead, count, *refs):
    if lead:
        len_ref, home_ref, rate_ref, k_hbm, v_hbm, sent_hbm, first_ref, last_ref = refs[:8]
        refs = refs[8:]
    else:
        last_ref, home_ref, rate_ref, k_hbm, v_hbm = refs[:5]
        blocks, refs = refs[5 : 5 + count], refs[5 + count :]
    k_ref, v_ref, table, packed, sem, out_sem = refs
    slots = home_ref.shape[0]
    part = columns(base, heads)
    sources = (k_hbm.at[:, part], v_hbm.at[:, part])
    load = lambda i: span_copies(i, span, sources, (k_ref, v_ref), sem)
    for i in range(slots):
        start_all(load(i))
    if lead:
        fill_tables(len_ref, first_ref, last_ref, span)
    fill_key_table(table, rate_ref, base, span)
    if lead:
        tail = jnp.zeros((TAIL, LANES), F32)
        lane = lax.broadcasted_iota(jnp.int32, (TAIL, LANES), 1)
        for i in range(slots):
            tail = jnp.where(lane == i, home_ref[i].astype(F32), tail)
        for d in range(packed.shape[0]):
            packed[d, slots * rows :, :] = tail.astype(BF16)

    def body(i):
        wait_all(load(i))
        at = tokens_at(i, span)
        live = token_index(span) >= last_ref[home_ref[i]]
        for h in range(heads):
            cols = head_cols(h)
            side = jnp.where(live, table[h], 0.0)
            weighted = (side * v_ref[at, cols].astype(F32)).astype(BF16)
            put_state(packed, i, h, rows, dot(k_ref[at, cols], weighted, 0, 0).astype(BF16))

    each_span(slots, body)
    out = [pltpu.make_async_copy(packed, sent_hbm, out_sem.at[0])] if lead else to_blocks(packed, blocks, out_sem)
    start_all(out)
    wait_all(out)


def scan_kernel(base, rows, span, reverse, lead, count, first_ref, order_ref, rate_ref, *refs):
    sources, refs = refs[:count], refs[count + lead :]
    targets = refs[:count]
    arrived, states, in_sem, out_sem = refs[count:]
    slots = states.shape[1] // rows
    spans = order_ref.shape[0]
    loads = [pltpu.make_async_copy(sources[0], arrived, in_sem.at[0])] if lead else from_blocks(sources, arrived, in_sem)
    start_all(loads)
    head = base + (lax.axis_index("seq") * rows) // HEAD_SIZE
    factor = jnp.exp(jnp.full((8, LANES), -rate_ref[head] * span, F32))[0:1]
    wait_all(loads)

    def body(i, state):
        c = spans - 1 - i if reverse else i
        place = order_ref[c]
        device, slot = place // slots, place % slots
        at = rows_at(slot, rows)
        states[device, at, :] = state.astype(BF16)
        carried = jnp.where(first_ref[c] >= span, factor * state, 0.0)
        return carried + arrived[device, at, :].astype(F32)

    lax.fori_loop(0, spans, body, jnp.zeros((rows, LANES), F32), unroll=4)
    out = [pltpu.make_async_copy(states, targets[0], out_sem.at[0])] if lead else to_blocks(states, targets, out_sem)
    start_all(out)
    wait_all(out)


def local_kernel(
    heads, span, rate_ref, seg_ref, q_hbm, k_hbm, v_hbm, out_hbm,
    q_ref, k_ref, v_ref, out_ref, decay, sem, out_sem,
):
    slots = seg_ref.shape[0]
    load = lambda i: span_copies(i, span, (q_hbm, k_hbm, v_hbm), (q_ref, k_ref, v_ref), sem)
    store = lambda i: span_copies(i, span, (out_ref,), (out_hbm,), out_sem)
    for i in range(slots):
        start_all(load(i))
    fill_decay(decay, rate_ref, 0, span)

    def body(i):
        wait_all(load(i))
        at = tokens_at(i, span)
        seg = seg_ref[i]
        same = row_to_cols(seg, span) == seg
        for h in range(heads):
            cols = head_cols(h)
            scores = dot(q_ref[at, cols], k_ref[at, cols], 1, 1)
            mixing = (scores * jnp.where(same, decay[h], 0.0)).astype(BF16)
            out_ref[at, cols] = dot(mixing, v_ref[at, cols], 1, 0).astype(BF16)
        start_all(store(i))

    each_span(slots, body)
    for i in range(slots):
        wait_all(store(i))


def output_kernel(base, heads, rows, span, lead, count, first_ref, home_ref, rate_ref, gain_ref, q_hbm, u_hbm, inner_hbm, *refs):
    if not lead:
        before_ref, refs = refs[0], refs[1:]
    blocks, refs = refs[:count], refs[count:]
    out_ref, q_ref, u_ref, sums_ref, inner_ref, prev, table, sem, in_sem = refs
    slots = home_ref.shape[0]
    states = [pltpu.make_async_copy(blocks[0], prev, in_sem.at[0])] if lead else from_blocks(blocks, prev, in_sem)
    start_all(states)
    part = columns(base, heads)
    sources = (q_hbm.at[:, part], u_hbm.at[:, part], inner_hbm.at[:, part])
    load = lambda i: span_copies(i, span, sources, (q_ref, u_ref, inner_ref), sem)
    for i in range(slots):
        start_all(load(i))
    fill_query_table(table, rate_ref, base, span)
    wait_all(states)

    def body(i):
        wait_all(load(i))
        at = tokens_at(i, span)
        live = token_index(span) < first_ref[home_ref[i]]
        squares = jnp.zeros((span, LANES), F32)
        crossed = jnp.zeros((span, LANES), F32)
        for h in range(heads):
            cols = head_cols(h)
            outer = dot(q_ref[at, cols], get_state(prev, i, h, rows), 1, 0)
            attn = inner_ref[at, cols].astype(F32) + jnp.where(live, table[h], 0.0) * outer
            out_ref[at, cols] = attn
            squares += attn * attn
            crossed += gain_ref[:, head_cols(base + h)] * u_ref[at, cols].astype(F32) * attn
        squares, crossed = cols_to_row(squares), cols_to_row(crossed)
        if not lead:
            squares += before_ref[i, 0:1, :]
            crossed += before_ref[i, 1:2, :]
        sums_ref[i, 0:1, :] = squares
        sums_ref[i, 1:2, :] = crossed

    each_span(slots, body)


def cotangent_kernel(base, heads, rows, span, lead, count, channels, first_ref, home_ref, rate_ref, gain_ref, sums_ref, q_ref, u_ref, attn_ref, *refs):
    g_hbm, targets = refs[0], refs[1 : 1 + count]
    g_ref, table, packed, g_sem, out_sem = refs[1 + count :]
    slots = home_ref.shape[0]
    save = lambda i: span_copies(i, span, (g_ref,), (g_hbm,), g_sem)
    fill_query_table(table, rate_ref, base, span)

    def body(i):
        at = tokens_at(i, span)
        total = jnp.sum(sums_ref[:, i], axis=0)
        scaling = 1.0 / jnp.sqrt(total[0:1] / channels + EPSILON)
        pulled = total[1:2] / channels
        direct = row_to_cols(scaling, LANES)
        along = row_to_cols(scaling * scaling * scaling * pulled, LANES)
        live = token_index(span) < first_ref[home_ref[i]]
        for h in range(heads):
            cols = head_cols(h)
            grad = direct * gain_ref[:, head_cols(base + h)] * u_ref[at, cols].astype(F32)
            grad = (grad - along * attn_ref[at, cols]).astype(BF16)
            g_ref[at, cols] = grad
            weighted = (jnp.where(live, table[h], 0.0) * grad.astype(F32)).astype(BF16)
            put_state(packed, i, h, rows, dot(q_ref[at, cols], weighted, 0, 0).astype(BF16))
        start_all(save(i))

    each_span(slots, body)
    out = [pltpu.make_async_copy(packed, targets[0], out_sem.at[0])] if lead else to_blocks(packed, targets, out_sem)
    start_all(out)
    wait_all(out)
    for i in range(slots):
        wait_all(save(i))


def inner_grads_kernel(base, heads, rows, span, lead, count, first_ref, home_ref, rate_ref, seg_ref, q_hbm, k_hbm, v_hbm, g_hbm, *refs):
    blocks, refs = refs[:count], refs[count:]
    if not lead:
        refs = refs[3:]
    dq_hbm, dk_hbm, dv_hbm = refs[:3]
    q_ref, k_ref, v_ref, g_ref, dq_ref, dk_ref, dv_ref, prev, decay, table, sem, out_sem, in_sem = refs[3:]
    slots = home_ref.shape[0]
    part = columns(base, heads)
    sources = (q_hbm.at[:, part], k_hbm.at[:, part], v_hbm.at[:, part], g_hbm)
    targets = (dq_hbm.at[:, part], dk_hbm.at[:, part], dv_hbm.at[:, part])
    load = lambda i: span_copies(i, span, sources, (q_ref, k_ref, v_ref, g_ref), sem)
    store = lambda i: span_copies(i, span, (dq_ref, dk_ref, dv_ref), targets, out_sem)
    states = [pltpu.make_async_copy(blocks[0], prev, in_sem.at[0])] if lead else from_blocks(blocks, prev, in_sem)
    start_all(states)
    for i in range(slots):
        start_all(load(i))
    fill_decay(decay, rate_ref, base, span)
    fill_query_table(table, rate_ref, base, span)
    wait_all(states)

    def body(i):
        wait_all(load(i))
        at = tokens_at(i, span)
        seg = seg_ref[i]
        same = row_to_cols(seg, span) == seg
        live = token_index(span) < first_ref[home_ref[i]]
        for h in range(heads):
            cols = head_cols(h)
            q, k, v, g = q_ref[at, cols], k_ref[at, cols], v_ref[at, cols], g_ref[at, cols]
            mask = jnp.where(same, decay[h], 0.0)
            mixing = (dot(q, k, 1, 1) * mask).astype(BF16)
            score_grad = (dot(g, v, 1, 1) * mask).astype(BF16)
            outer = dot(g, get_state(prev, i, h, rows), 1, 1)
            dq = dot(score_grad, k, 1, 0) + jnp.where(live, table[h], 0.0) * outer
            dq_ref[at, cols] = dq.astype(BF16)
            dk_ref[at, cols] = dot(score_grad, q, 0, 0).astype(BF16)
            dv_ref[at, cols] = dot(mixing, g, 0, 0).astype(BF16)
        start_all(store(i))

    each_span(slots, body)
    for i in range(slots):
        wait_all(store(i))


def outer_grads_kernel(base, heads, rows, span, lead, count, last_ref, home_ref, rate_ref, k_hbm, v_hbm, dk_part, dv_part, *refs):
    blocks, refs = refs[:count], refs[count:]
    if not lead:
        refs = refs[2:]
    dk_hbm, dv_hbm = refs[:2]
    k_ref, v_ref, dk_in, dv_in, dk_ref, dv_ref, after_ref, table, sem, out_sem, in_sem = refs[2:]
    slots = home_ref.shape[0]
    part = columns(base, heads)
    sources = [ref.at[:, part] for ref in (k_hbm, v_hbm, dk_part, dv_part)]
    targets = (dk_hbm.at[:, part], dv_hbm.at[:, part])
    load = lambda i: span_copies(i, span, sources, (k_ref, v_ref, dk_in, dv_in), sem)
    store = lambda i: span_copies(i, span, (dk_ref, dv_ref), targets, out_sem)
    states = [pltpu.make_async_copy(blocks[0], after_ref, in_sem.at[0])] if lead else from_blocks(blocks, after_ref, in_sem)
    start_all(states)
    for i in range(slots):
        start_all(load(i))
    fill_key_table(table, rate_ref, base, span)
    wait_all(states)

    def body(i):
        wait_all(load(i))
        at = tokens_at(i, span)
        live = token_index(span) >= last_ref[home_ref[i]]
        for h in range(heads):
            cols = head_cols(h)
            side = jnp.where(live, table[h], 0.0)
            after = get_state(after_ref, i, h, rows)
            dk = dk_in[at, cols].astype(F32) + side * dot(v_ref[at, cols], after, 1, 1)
            dv = dv_in[at, cols].astype(F32) + side * dot(k_ref[at, cols], after, 1, 0)
            dk_ref[at, cols] = dk.astype(BF16)
            dv_ref[at, cols] = dv.astype(BF16)
        start_all(store(i))

    each_span(slots, body)
    for i in range(slots):
        wait_all(store(i))


def exchange(blocks):
    if len(blocks) == 1:
        return (lax.all_to_all(blocks[0], "seq", split_axis=0, concat_axis=0, tiled=True),)
    devices = len(blocks)
    moved = [blocks[0]] + [None] * (devices - 1)
    for k in range(devices - 1, 0, -1):
        moved[k] = lax.ppermute(blocks[k], "seq", [(i, i ^ k) for i in range(devices)])
    return tuple(moved)


def shards(query, key, value, upstream, norm_gain, decay_rate, document_lengths, group_home):
    devices = lax.axis_size("seq")
    assert devices & (devices - 1) == 0
    tokens, width = query.shape
    all_heads = width // HEAD_SIZE
    slots = group_home.shape[0]
    span = tokens // slots
    spans = slots * devices
    channels = width * lax.axis_size("head")
    halves = (all_heads // 2, all_heads - all_heads // 2)
    chunks = ((0, halves[0], True, 1), (halves[0], halves[1], False, devices))

    doc_ends = jnp.cumsum(document_lengths)
    positions = (group_home * span)[:, None] + jnp.arange(span, dtype=jnp.int32)[None, :]
    seg = jnp.sum((doc_ends <= positions[..., None]).astype(F32), axis=-1).reshape(slots, 1, span)
    gain = norm_gain.reshape(1, width)

    smem = pl.BlockSpec(memory_space=pltpu.SMEM)
    vmem = pl.BlockSpec(memory_space=pltpu.VMEM)
    hbm = pl.BlockSpec(memory_space=pl.ANY)
    whole = jax.ShapeDtypeStruct((tokens, width), BF16)
    spans_table = jax.ShapeDtypeStruct((spans + 1,), jnp.int32)

    def sems(*shape):
        return pltpu.SemaphoreType.DMA(shape)

    def call(kernel, limit, flops, in_specs, out_specs, out_shape, scratch, static, aliases={}):
        return pl.pallas_call(
            functools.partial(kernel, *static),
            in_specs=in_specs,
            out_specs=out_specs,
            out_shape=out_shape,
            scratch_shapes=scratch,
            input_output_aliases=aliases,
            compiler_params=pltpu.CompilerParams(vmem_limit_bytes=limit << 20),
            cost_estimate=pl.CostEstimate(flops=flops, bytes_accessed=0, transcendentals=0),
        )

    def shape_of(chunk):
        _, heads, lead, _ = chunk
        rows = heads * HEAD_SIZE // devices
        table = pltpu.VMEM((heads, span, LANES), F32)
        decay = pltpu.VMEM((heads, span, span), F32)
        token = pltpu.VMEM((tokens, heads * HEAD_SIZE), BF16)
        states = (devices, slots * rows, LANES)
        if lead:
            out = [jax.ShapeDtypeStruct(states, BF16)]
        else:
            out = [jax.ShapeDtypeStruct(states[1:], BF16)] * devices
        return rows, table, decay, token, pltpu.VMEM(states, BF16), out

    def static_of(chunk):
        base, heads, lead, count = chunk
        return (base, heads, shape_of(chunk)[0], span, lead, count)

    work = 2 * tokens * width * span

    def summaries(chunk, table_in):
        _, _, lead, count = chunk
        rows, table, _, token, states, out = shape_of(chunk)
        packed = states
        tables = []
        if lead:
            packed = pltpu.VMEM((devices, slots * rows + TAIL, LANES), BF16)
            out = [jax.ShapeDtypeStruct((devices, slots * rows + TAIL, LANES), BF16)]
            tables = [spans_table] * 2
        return call(
            summary_kernel, LIMIT, work // 4,
            [smem, smem, smem, hbm, hbm],
            [hbm] * count + [smem] * len(tables),
            out + tables,
            [token] * 2 + [table, packed, sems(2, slots), sems(count)],
            static_of(chunk),
        )(table_in, group_home, decay_rate, key, value)

    def scan(chunk, blocks, reverse, beside=()):
        base, _, lead, count = chunk
        rows, _, _, _, states, out = shape_of(chunk)
        arrived = pltpu.VMEM(blocks[0].shape, BF16) if lead else states
        return call(
            scan_kernel, ROOMY, work // 16,
            [smem, smem, smem] + [hbm] * (count + len(beside)),
            [hbm] * count,
            out,
            [arrived, states, sems(count), sems(count)],
            (base, rows, span, reverse, lead, count),
        )(first, order, decay_rate, *blocks, *beside)

    def outputs(chunk, inner, before, blocks):
        _, heads, lead, count = chunk
        _, table, _, token, states, _ = shape_of(chunk)
        part = (tokens, heads * HEAD_SIZE)
        extra = [] if lead else [before]
        return call(
            output_kernel, HANDOFF, work // 4,
            [smem, smem, smem, vmem, hbm, hbm, hbm] + [vmem] * len(extra) + [hbm] * count,
            [vmem] * 4,
            [pltpu.VMEM(part, F32), token, token, jax.ShapeDtypeStruct((slots, 2, span), F32)],
            [token, states, table, sems(3, slots), sems(count)],
            static_of(chunk),
        )(first, group_home, decay_rate, gain, query, upstream, inner, *extra, *blocks)

    def cotangents(chunk, sums, query_v, upstream_v, attn):
        _, heads, _, count = chunk
        _, table, _, token, states, out = shape_of(chunk)
        return call(
            cotangent_kernel, RECEIVE, work // 4,
            [smem, smem, smem] + [vmem] * 5,
            [hbm] * (1 + count),
            [jax.ShapeDtypeStruct((tokens, heads * HEAD_SIZE), BF16)] + out,
            [token, table, states, sems(1, slots), sems(count)],
            static_of(chunk) + (channels,),
        )(first, group_home, decay_rate, gain, sums, query_v, upstream_v, attn)

    def inner_grads(chunk, grad_in, blocks, into):
        _, _, _, count = chunk
        _, table, decay, token, states, _ = shape_of(chunk)
        start = 8 + count
        return call(
            inner_grads_kernel, LASTING, 3 * work,
            [smem, smem, smem, vmem] + [hbm] * (4 + count + len(into)),
            [hbm] * 3,
            [whole] * 3,
            [token] * 7 + [states, decay, table, sems(4, slots), sems(3, slots), sems(count)],
            static_of(chunk),
            {start + i: i for i in range(len(into))},
        )(first, group_home, decay_rate, seg, query, key, value, grad_in, *blocks, *into)

    def outer_grads(chunk, parts, blocks, into):
        _, _, _, count = chunk
        _, table, _, token, states, _ = shape_of(chunk)
        start = 7 + count
        return call(
            outer_grads_kernel, LASTING, work // 2,
            [smem, smem, smem] + [hbm] * (4 + count + len(into)),
            [hbm] * 2,
            [whole] * 2,
            [token] * 6 + [states, table, sems(4, slots), sems(2, slots), sems(count)],
            static_of(chunk),
            {start + i: i for i in range(len(into))},
        )(last, group_home, decay_rate, key, value, *parts, *blocks, *into)

    a, b = chunks
    sent_a, first, last = summaries(a, document_lengths)
    arrived_a = exchange([sent_a])
    sent_b = summaries(b, last)
    arrived_b = exchange(sent_b)

    homes = arrived_a[0][:, -TAIL, :slots].astype(jnp.int32).reshape(-1)
    hits = homes[None, :] == jnp.arange(spans, dtype=jnp.int32)[:, None]
    order = jnp.sum(jnp.where(hits, jnp.arange(spans, dtype=jnp.int32)[None, :], 0), axis=1)

    prev_a = exchange(scan(a, arrived_a, False, sent_b[:1]))
    prev_b = exchange(scan(b, arrived_b, False))

    inner = call(
        local_kernel, LIMIT, 2 * work,
        [smem, vmem, hbm, hbm, hbm],
        hbm,
        whole,
        [pltpu.VMEM((tokens, width), BF16)] * 4
        + [pltpu.VMEM((all_heads, span, span), F32), sems(3, slots), sems(1, slots)],
        (all_heads, span),
    )(decay_rate, seg, query, key, value)

    attn_a, query_a, upstream_a, sums = outputs(a, inner, None, prev_a)
    attn_b, query_b, upstream_b, sums = outputs(b, inner, sums, prev_b)
    sums = lax.all_gather(sums, "head")

    grad_a, *rev_a = cotangents(a, sums, query_a, upstream_a, attn_a)
    rev_a = exchange(rev_a)
    grad_b, *rev_b = cotangents(b, sums, query_b, upstream_b, attn_b)
    beside = rev_b[:1]
    rev_b = exchange(rev_b)

    after_a = exchange(scan(a, rev_a, True, beside))
    after_b = exchange(scan(b, rev_b, True))

    parts = inner_grads(a, grad_a, prev_a, ())
    query_grad, key_inner, value_inner = inner_grads(b, grad_b, prev_b, parts)
    finals = outer_grads(a, (key_inner, value_inner), after_a, ())
    key_grad, value_grad = outer_grads(b, (key_inner, value_inner), after_b, finals)
    return query_grad, key_grad, value_grad


def solution(mesh):
    in_specs = (
        P("seq", "head"),
        P("seq", "head"),
        P("seq", "head"),
        P("seq", "head"),
        P("head"),
        P("head"),
        P(),
        P("seq"),
    )
    out_specs = (P("seq", "head"), P("seq", "head"), P("seq", "head"))

    return jax.shard_map(shards, mesh=mesh, in_specs=in_specs, out_specs=out_specs, check_vma=False)
```

```python
import functools

import jax
import jax.numpy as jnp
from jax import lax
from jax.experimental import pallas as pl
from jax.experimental.pallas import tpu as pltpu
from jax.sharding import PartitionSpec as P


HEAD_SIZE = 128
LANES = 128
EPSILON = 1e-06
UNROLL = {"summary": 4, "local": 2, "output": 4, "cotangent": 4, "inner_grads": 2, "outer_grads": 4}
TAIL = 16
ALONE = 58
LIMIT = 16
F32 = jnp.float32
BF16 = jnp.bfloat16


def dot(a, b, ca, cb):
    return lax.dot_general(a, b, (((ca,), (cb,)), ((), ())), preferred_element_type=F32)


def head_cols(h):
    return slice(h * HEAD_SIZE, (h + 1) * HEAD_SIZE)


def token_index(span):
    return lax.broadcasted_iota(jnp.int32, (span, LANES), 0)


def fill_key_table(table, rate_ref, base, span):
    for h in range(table.shape[0]):
        table[h] = jnp.exp(-rate_ref[base + h] * (span - 1.0 - token_index(span).astype(F32)))


def fill_query_table(table, rate_ref, base, span):
    for h in range(table.shape[0]):
        table[h] = jnp.exp(-rate_ref[base + h] * (token_index(span).astype(F32) + 1.0))


def fill_decay(decay, rate_ref, base, span):
    j = lax.broadcasted_iota(jnp.int32, (span, span), 0)
    l = lax.broadcasted_iota(jnp.int32, (span, span), 1)
    spread = (j - l).astype(F32)
    for h in range(decay.shape[0]):
        falling = jnp.exp(-rate_ref[base + h] * jnp.maximum(spread, 0.0))
        decay[h] = jnp.where(spread >= 0.0, falling, 0.0)


def row_to_cols(row, width):
    cols = jnp.transpose(jnp.broadcast_to(row, (LANES, row.shape[1])))
    return jnp.concatenate([cols] * (width // LANES), axis=1) if width > LANES else cols


def cols_to_row(cols):
    return jnp.sum(jnp.transpose(cols), axis=0, keepdims=True)


def fill_tables(len_ref, first_ref, last_ref, span):
    spans = first_ref.shape[0] - 1
    far = jnp.int32(spans * span)

    def reset(c, carry):
        first_ref[c] = far
        last_ref[c] = 0
        return carry

    def note(d, end):
        end = end + len_ref[d]
        c = lax.shift_right_logical(end, span.bit_length() - 1) if span & (span - 1) == 0 else end // span
        inside = end - c * span
        last_ref[c] = inside
        first_ref[c] = jnp.minimum(first_ref[c], inside)
        return end

    lax.fori_loop(0, spans + 1, reset, 0, unroll=8)
    lax.fori_loop(0, len_ref.shape[0], note, jnp.int32(0), unroll=4)
    first_ref[0] = 0


def fill_segments(seg_ref, len_ref, home_ref):
    slots, span = seg_ref.shape
    slot = lax.broadcasted_iota(jnp.int32, (slots, span), 0)
    position = lax.broadcasted_iota(jnp.int32, (slots, span), 1)
    for i in range(slots):
        position += jnp.where(slot == i, home_ref[i] * span, 0)

    def note(d, carry):
        end, segment = carry
        end = end + len_ref[d]
        return end, segment + jnp.where(end <= position, 1.0, 0.0)

    start = (jnp.int32(0), jnp.zeros((slots, span), F32))
    seg_ref[...] = lax.fori_loop(0, len_ref.shape[0], note, start, unroll=4)[1]


def tokens_at(i, span):
    return pl.ds(pl.multiple_of(i * span, span), span)


def rows_at(i, rows):
    return pl.ds(pl.multiple_of(i * rows, rows), rows)


def put_state(ref, i, h, rows, value):
    chunks = HEAD_SIZE // rows
    for part in range(chunks):
        ref[h * chunks + part, rows_at(i, rows), :] = value[part * rows : (part + 1) * rows]


def get_state(ref, i, h, rows):
    chunks = HEAD_SIZE // rows
    return ref[h * chunks : (h + 1) * chunks, rows_at(i, rows), :].reshape(HEAD_SIZE, HEAD_SIZE)


def span_copies(i, span, sources, targets, sem):
    at = tokens_at(i, span)
    return [
        pltpu.make_async_copy(source.at[at], target.at[at], sem.at[a, i])
        for a, (source, target) in enumerate(zip(sources, targets))
    ]


def start_all(copies):
    for copy in copies:
        copy.start()


def wait_all(copies):
    for copy in copies:
        copy.wait()


def each_span(slots, unroll, load, compute, store):
    def turn(g, carry):
        group = [g * unroll + j for j in range(unroll)]
        for i in group:
            wait_all(load(i))
        for i in group:
            compute(i)
        for i in group:
            start_all(store(i))
        return carry

    lax.fori_loop(0, slots // unroll, turn, 0)


def nothing(i):
    return []


def own_index():
    return lax.axis_index("seq")


def block_stores(packed, blocks, i, rows, sem):
    me, at = own_index(), rows_at(i, rows)
    return [
        pltpu.make_async_copy(packed.at[jnp.bitwise_xor(me, k), at], block.at[at], sem.at[k, i])
        for k, block in enumerate(blocks)
    ]


def take_blocks(blocks, packed):
    me = own_index()
    for k, block in enumerate(blocks):
        packed[jnp.bitwise_xor(me, k)] = block[...]


def summary_kernel(heads, rows, span, count, len_ref, home_ref, rate_ref, k_hbm, v_hbm, *refs):
    blocks, refs = refs[:count], refs[count:]
    k_ref, v_ref, first_ref, last_ref, table, packed, tail_ref, sem, out_sem, tail_sem = refs
    slots = home_ref.shape[0]
    load = lambda i: span_copies(i, span, (k_hbm, v_hbm), (k_ref, v_ref), sem)
    for i in range(slots):
        start_all(load(i))
    fill_tables(len_ref, first_ref, last_ref, span)
    fill_key_table(table, rate_ref, 0, span)
    tail = jnp.zeros((TAIL, LANES), F32)
    lane = lax.broadcasted_iota(jnp.int32, (TAIL, LANES), 1)
    for i in range(slots):
        tail = jnp.where(lane == i, home_ref[i].astype(F32), tail)
    tail_ref[...] = tail.astype(BF16)
    ending = [
        pltpu.make_async_copy(tail_ref, block.at[pl.ds(slots * rows, TAIL)], tail_sem.at[k])
        for k, block in enumerate(blocks)
    ]
    start_all(ending)
    send = lambda i: block_stores(packed, blocks, i, rows, out_sem)

    def body(i):
        at = tokens_at(i, span)
        live = token_index(span) >= last_ref[home_ref[i]]
        for h in range(heads):
            cols = head_cols(h)
            side = jnp.where(live, table[h], 0.0)
            weighted = (side * v_ref[at, cols].astype(F32)).astype(BF16)
            put_state(packed, i, h, rows, dot(k_ref[at, cols], weighted, 0, 0).astype(BF16))

    each_span(slots, UNROLL["summary"], load, body, send)
    for i in range(slots):
        wait_all(send(i))
    wait_all(ending)


def scan_kernel(rows, span, reverse, count, first_ref, order_in, rate_ref, *refs):
    sources, targets = refs[:count], refs[count : 2 * count]
    if reverse:
        order_ref = order_in
        arrived, states, out_sem = refs[2 * count :]
    else:
        order_ref, arrived, states, homes, home_ref, home_sem, out_sem = refs[2 * count :]
    slots = states.shape[1] // rows
    spans = order_ref.shape[0]
    if not reverse:
        for k, ref in enumerate(sources):
            homes[k : k + 1, :] = ref[slots * rows :, :].astype(F32)[0:1].astype(jnp.int32)
        gather = pltpu.make_async_copy(homes, home_ref, home_sem)
        gather.start()
    for k, ref in enumerate(sources):
        arrived[k] = ref[: slots * rows]
    head = (own_index() * rows) // HEAD_SIZE
    factor = jnp.exp(jnp.full((8, LANES), -rate_ref[head] * span, F32))[0:1]
    if not reverse:
        gather.wait()

        def note(k, carry):
            for i in range(slots):
                order_ref[home_ref[k, i]] = k * slots + i
            return carry

        lax.fori_loop(0, count, note, 0)

    def body(i, state):
        c = spans - 1 - i if reverse else i
        place = order_ref[c]
        block, slot = place // slots, place % slots
        at = rows_at(slot, rows)
        states[block, at, :] = state.astype(BF16)
        carried = jnp.where(first_ref[c] >= span, factor * state, 0.0)
        return carried + arrived[block, at, :].astype(F32)

    lax.fori_loop(0, spans, body, jnp.zeros((rows, LANES), F32), unroll=4)
    out = [pltpu.make_async_copy(states.at[k], ref, out_sem.at[k]) for k, ref in enumerate(targets)]
    start_all(out)
    wait_all(out)


def local_kernel(
    heads, span, len_ref, home_ref, rate_ref, q_hbm, u_hbm, k_ref, v_ref,
    out_ref, q_ref, u_ref, seg_ref, decay, sem, u_sem,
):
    slots = home_ref.shape[0]
    load = lambda i: span_copies(i, span, (q_hbm,), (q_ref,), sem)
    later = lambda i: span_copies(i, span, (u_hbm,), (u_ref,), u_sem)
    for i in range(slots):
        start_all(load(i))
    for i in range(slots):
        start_all(later(i))
    fill_segments(seg_ref, len_ref, home_ref)
    fill_decay(decay, rate_ref, 0, span)

    def body(i):
        at = tokens_at(i, span)
        seg = seg_ref[pl.ds(i, 1), :]
        same = row_to_cols(seg, span) == seg
        for h in range(heads):
            cols = head_cols(h)
            scores = dot(q_ref[at, cols], k_ref[at, cols], 1, 1)
            mixing = (scores * jnp.where(same, decay[h], 0.0)).astype(BF16)
            out_ref[at, cols] = dot(mixing, v_ref[at, cols], 1, 0)

    each_span(slots, UNROLL["local"], load, body, nothing)
    for i in range(slots):
        wait_all(later(i))


def output_kernel(
    heads, rows, span, count, first_ref, home_ref, rate_ref, gain_ref, q_ref, u_ref, inner_ref, *refs
):
    blocks, refs = refs[:count], refs[count:]
    out_ref, sums_ref, prev, table = refs
    slots = home_ref.shape[0]
    take_blocks(blocks, prev)
    fill_query_table(table, rate_ref, 0, span)

    def body(i):
        at = tokens_at(i, span)
        live = token_index(span) < first_ref[home_ref[i]]
        squares = jnp.zeros((span, LANES), F32)
        crossed = jnp.zeros((span, LANES), F32)
        for h in range(heads):
            cols = head_cols(h)
            outer = dot(q_ref[at, cols], get_state(prev, i, h, rows), 1, 0)
            attn = inner_ref[at, cols] + jnp.where(live, table[h], 0.0) * outer
            out_ref[at, cols] = attn
            squares += attn * attn
            crossed += gain_ref[:, cols] * u_ref[at, cols].astype(F32) * attn
        sums_ref[i, 0:1, :] = cols_to_row(squares)
        sums_ref[i, 1:2, :] = cols_to_row(crossed)

    each_span(slots, UNROLL["output"], nothing, body, nothing)


def cotangent_kernel(
    heads, rows, span, count, channels, first_ref, home_ref, rate_ref, gain_ref, sums_ref, q_ref, u_ref, attn_ref, *refs
):
    g_ref, blocks = refs[0], refs[1 : 1 + count]
    table, packed, out_sem = refs[1 + count :]
    slots = home_ref.shape[0]
    fill_query_table(table, rate_ref, 0, span)

    def body(i):
        at = tokens_at(i, span)
        total = jnp.sum(sums_ref[:, i], axis=0)
        scaling = 1.0 / jnp.sqrt(total[0:1] / channels + EPSILON)
        pulled = total[1:2] / channels
        direct = row_to_cols(scaling, LANES)
        along = row_to_cols(scaling * scaling * scaling * pulled, LANES)
        live = token_index(span) < first_ref[home_ref[i]]
        for h in range(heads):
            cols = head_cols(h)
            grad = direct * gain_ref[:, cols] * u_ref[at, cols].astype(F32)
            grad = (grad - along * attn_ref[at, cols]).astype(BF16)
            g_ref[at, cols] = grad
            weighted = (jnp.where(live, table[h], 0.0) * grad.astype(F32)).astype(BF16)
            put_state(packed, i, h, rows, dot(q_ref[at, cols], weighted, 0, 0).astype(BF16))

    send = lambda i: block_stores(packed, blocks, i, rows, out_sem)
    each_span(slots, UNROLL["cotangent"], nothing, body, send)
    for i in range(slots):
        wait_all(send(i))


def inner_grads_kernel(
    heads, rows, span, count, half, first_ref, home_ref, rate_ref, seg_ref, q_ref, k_ref, v_ref, g_ref, *refs
):
    blocks, refs = refs[:count], refs[count + half :]
    dq_hbm, dk_ref, dv_ref, dq_ref, prev, decay, table, out_sem = refs
    slots = home_ref.shape[0] // 2
    base = half * slots
    target = dq_hbm.at[pl.ds(base * span, slots * span)]
    store = lambda i: span_copies(i, span, (dq_ref,), (target,), out_sem)
    take_blocks(blocks, prev)
    fill_decay(decay, rate_ref, 0, span)
    fill_query_table(table, rate_ref, 0, span)

    def body(own):
        i = base + own
        at, own = tokens_at(i, span), tokens_at(own, span)
        seg = seg_ref[pl.ds(i, 1), :]
        same = row_to_cols(seg, span) == seg
        live = token_index(span) < first_ref[home_ref[i]]
        for h in range(heads):
            cols = head_cols(h)
            q, k, v, g = q_ref[at, cols], k_ref[at, cols], v_ref[at, cols], g_ref[at, cols]
            mask = jnp.where(same, decay[h], 0.0)
            mixing = (dot(q, k, 1, 1) * mask).astype(BF16)
            score_grad = (dot(g, v, 1, 1) * mask).astype(BF16)
            outer = dot(g, get_state(prev, i, h, rows), 1, 1)
            dq = dot(score_grad, k, 1, 0) + jnp.where(live, table[h], 0.0) * outer
            dq_ref[own, cols] = dq.astype(BF16)
            dk_ref[own, cols] = dot(score_grad, q, 0, 0)
            dv_ref[own, cols] = dot(mixing, g, 0, 0)

    each_span(slots, UNROLL["inner_grads"], nothing, body, store)
    for i in range(slots):
        wait_all(store(i))


def outer_grads_kernel(
    heads, rows, span, count, last_ref, home_ref, rate_ref, k_ref, v_ref, dk_0, dv_0, dk_1, dv_1, *refs
):
    blocks, refs = refs[:count], refs[count:]
    dk_hbm, dv_hbm, dk_ref, dv_ref, after_ref, table, out_sem = refs
    slots = home_ref.shape[0]
    store = lambda i: span_copies(i, span, (dk_ref, dv_ref), (dk_hbm, dv_hbm), out_sem)
    take_blocks(blocks, after_ref)
    fill_key_table(table, rate_ref, 0, span)

    def body(half, own):
        dk_in, dv_in = ((dk_0, dv_0), (dk_1, dv_1))[half]
        i = half * (slots // 2) + own
        at, own = tokens_at(i, span), tokens_at(own, span)
        live = token_index(span) >= last_ref[home_ref[i]]
        for h in range(heads):
            cols = head_cols(h)
            side = jnp.where(live, table[h], 0.0)
            after = get_state(after_ref, i, h, rows)
            dk = dk_in[own, cols] + side * dot(v_ref[at, cols], after, 1, 1)
            dv = dv_in[own, cols] + side * dot(k_ref[at, cols], after, 1, 0)
            dk_ref[at, cols] = dk.astype(BF16)
            dv_ref[at, cols] = dv.astype(BF16)

    for half in range(2):
        keep = lambda own, half=half: store(half * (slots // 2) + own)
        each_span(slots // 2, UNROLL["outer_grads"], nothing, functools.partial(body, half), keep)
    for i in range(slots):
        wait_all(store(i))


def exchange(blocks):
    devices = len(blocks)
    moved = [blocks[0]] + [None] * (devices - 1)
    for k in range(devices - 1, 0, -1):
        moved[k] = lax.ppermute(blocks[k], "seq", [(i, i ^ k) for i in range(devices)])
    return tuple(moved)


def shards(query, key, value, upstream, norm_gain, decay_rate, document_lengths, group_home):
    devices = lax.axis_size("seq")
    assert devices & (devices - 1) == 0
    tokens, width = query.shape
    heads = width // HEAD_SIZE
    slots = group_home.shape[0]
    span = tokens // slots
    spans = slots * devices
    rows = width // devices
    channels = width * lax.axis_size("head")

    gain = norm_gain.reshape(1, width)

    smem = pl.BlockSpec(memory_space=pltpu.SMEM)
    vmem = pl.BlockSpec(memory_space=pltpu.VMEM)
    hbm = pl.BlockSpec(memory_space=pl.ANY)
    spans_table = jax.ShapeDtypeStruct((spans + 1,), jnp.int32)
    whole = jax.ShapeDtypeStruct((tokens, width), BF16)
    token_bf16 = pltpu.VMEM((tokens, width), BF16)
    token_f32 = pltpu.VMEM((tokens, width), F32)
    table = pltpu.VMEM((heads, span, LANES), F32)
    decay = pltpu.VMEM((heads, span, span), F32)
    states = pltpu.VMEM((devices, slots * rows, LANES), BF16)
    out = [jax.ShapeDtypeStruct(states.shape[1:], BF16)] * devices
    sent = [jax.ShapeDtypeStruct((slots * rows + TAIL, LANES), BF16)] * devices
    blocks = [hbm] * devices
    taken = [vmem] * devices

    def sems(*shape):
        return pltpu.SemaphoreType.DMA(shape)

    def call(kernel, name, limit, flops, in_specs, out_specs, out_shape, scratch, *static, aliases={}):
        return pl.pallas_call(
            functools.partial(kernel, *static),
            in_specs=in_specs,
            out_specs=out_specs,
            out_shape=out_shape,
            scratch_shapes=scratch,
            input_output_aliases=aliases,
            compiler_params=pltpu.CompilerParams(vmem_limit_bytes=limit << 20),
            cost_estimate=pl.CostEstimate(flops=flops, bytes_accessed=0, transcendentals=0),
            name=name,
        )

    work = 2 * tokens * width * span
    *moving, key_v, value_v, first, last = call(
        summary_kernel, "summaries", ALONE, work // 2,
        [smem, smem, smem, hbm, hbm],
        blocks + [vmem, vmem, smem, smem],
        sent + [token_bf16, token_bf16, spans_table, spans_table],
        [table, states, pltpu.VMEM((TAIL, LANES), BF16), sems(2, slots), sems(devices, slots), sems(devices)],
        heads, rows, span, devices,
    )(document_lengths, group_home, decay_rate, key, value)
    arrived = exchange(moving)

    inner, query_v, upstream_v, seg = call(
        local_kernel, "inner", LIMIT, 2 * work,
        [smem, smem, smem, hbm, hbm, vmem, vmem],
        [vmem, vmem, vmem, vmem],
        [token_f32, token_bf16, token_bf16, pltpu.VMEM((slots, span), F32)],
        [decay, sems(1, slots), sems(1, slots)],
        heads, span,
    )(document_lengths, group_home, decay_rate, query, upstream, key_v, value_v)

    def scan(arrived, order, reverse):
        held = [states, states]
        if reverse:
            extra_specs, extra = [], []
        else:
            extra_specs, extra = [smem], [jax.ShapeDtypeStruct((spans,), jnp.int32)]
            table_shape = (devices, LANES)
            held += [pltpu.VMEM(table_shape, jnp.int32), pltpu.SMEM(table_shape, jnp.int32), pltpu.SemaphoreType.DMA]
        return call(
            scan_kernel, "scan", LIMIT, work // 8,
            [smem, smem, smem] + taken,
            blocks + extra_specs,
            out + extra,
            held + [sems(devices)],
            rows, span, reverse, devices,
        )(first, order, decay_rate, *arrived)

    *moving, order = scan(arrived, group_home, False)
    prev = exchange(moving)
    attn, sums = call(
        output_kernel, "output", LIMIT, work // 2,
        [smem, smem, smem, vmem, vmem, vmem, vmem] + taken,
        [vmem, vmem],
        [token_f32, jax.ShapeDtypeStruct((slots, 2, span), F32)],
        [states, table],
        heads, rows, span, devices,
    )(first, group_home, decay_rate, gain, query_v, upstream_v, inner, *prev)
    sums = lax.all_gather(sums, "head")

    grad_in, *moving = call(
        cotangent_kernel, "cotangent", LIMIT, work // 2,
        [smem, smem, smem, vmem, vmem, vmem, vmem, vmem],
        [vmem] + blocks,
        [token_bf16] + out,
        [table, states, sems(devices, slots)],
        heads, rows, span, devices, channels,
    )(first, group_home, decay_rate, gain, sums, query_v, upstream_v, attn)
    arrived = exchange(moving)

    half_f32 = pltpu.VMEM((tokens // 2, width), F32)

    def inner_grads(half, *into):
        return call(
            inner_grads_kernel, "inner_grads", LIMIT, 3 * work,
            [smem, smem, smem, vmem, vmem, vmem, vmem, vmem] + taken + [hbm] * half,
            [hbm, vmem, vmem],
            [whole, half_f32, half_f32],
            [pltpu.VMEM((tokens // 2, width), BF16), states, decay, table, sems(1, slots // 2)],
            heads, rows, span, devices, half,
            aliases={8 + devices: 0} if half else {},
        )(first, group_home, decay_rate, seg, query_v, key_v, value_v, grad_in, *prev, *into)

    query_half, *parts = inner_grads(0)
    query_grad, *others = inner_grads(1, query_half)
    after = exchange(scan(arrived, order, True))
    key_grad, value_grad = call(
        outer_grads_kernel, "outer_grads", LIMIT, work,
        [smem, smem, smem, vmem, vmem, vmem, vmem, vmem, vmem] + taken,
        [hbm, hbm],
        [whole, whole],
        [token_bf16, token_bf16, states, table, sems(2, slots)],
        heads, rows, span, devices,
    )(last, group_home, decay_rate, key_v, value_v, *parts, *others, *after)
    return query_grad, key_grad, value_grad


def solution(mesh):
    in_specs = (
        P("seq", "head"),
        P("seq", "head"),
        P("seq", "head"),
        P("seq", "head"),
        P("head"),
        P("head"),
        P(),
        P("seq"),
    )
    out_specs = (P("seq", "head"), P("seq", "head"), P("seq", "head"))
    return jax.shard_map(shards, mesh=mesh, in_specs=in_specs, out_specs=out_specs, check_vma=False)
```

```python
import functools

import jax
import jax.numpy as jnp
from jax import lax
from jax.experimental import pallas as pl
from jax.experimental.pallas import tpu as pltpu
from jax.sharding import PartitionSpec as P


HEAD_SIZE = 128
LANES = 128
EPSILON = 1e-06
UNROLL = {"summary": 4, "local": 2, "output": 4, "cotangent": 4, "inner_grads": 2, "outer_grads": 4}
TAIL = 16
ALONE = 58
LIMIT = 16
F32 = jnp.float32
BF16 = jnp.bfloat16


def dot(a, b, ca, cb):
    return lax.dot_general(a, b, (((ca,), (cb,)), ((), ())), preferred_element_type=F32)


def head_cols(h):
    return slice(h * HEAD_SIZE, (h + 1) * HEAD_SIZE)


def token_index(span):
    return lax.broadcasted_iota(jnp.int32, (span, LANES), 0)


def fill_key_table(table, rate_ref, base, span):
    for h in range(table.shape[0]):
        table[h] = jnp.exp(-rate_ref[base + h] * (span - 1.0 - token_index(span).astype(F32)))


def fill_query_table(table, rate_ref, base, span):
    for h in range(table.shape[0]):
        table[h] = jnp.exp(-rate_ref[base + h] * (token_index(span).astype(F32) + 1.0))


def fill_decay(decay, rate_ref, base, span):
    j = lax.broadcasted_iota(jnp.int32, (span, span), 0)
    l = lax.broadcasted_iota(jnp.int32, (span, span), 1)
    spread = (j - l).astype(F32)
    for h in range(decay.shape[0]):
        falling = jnp.exp(-rate_ref[base + h] * jnp.maximum(spread, 0.0))
        decay[h] = jnp.where(spread >= 0.0, falling, 0.0)


def row_to_cols(row, width):
    cols = jnp.transpose(jnp.broadcast_to(row, (LANES, row.shape[1])))
    return jnp.concatenate([cols] * (width // LANES), axis=1) if width > LANES else cols


def cols_to_row(cols):
    return jnp.sum(jnp.transpose(cols), axis=0, keepdims=True)


def fill_tables(len_ref, first_ref, last_ref, span):
    spans = first_ref.shape[0] - 1
    far = jnp.int32(spans * span)

    def reset(c, carry):
        first_ref[c] = far
        last_ref[c] = 0
        return carry

    def note(d, end):
        end = end + len_ref[d]
        c = lax.shift_right_logical(end, span.bit_length() - 1) if span & (span - 1) == 0 else end // span
        inside = end - c * span
        last_ref[c] = inside
        first_ref[c] = jnp.minimum(first_ref[c], inside)
        return end

    lax.fori_loop(0, spans + 1, reset, 0, unroll=8)
    lax.fori_loop(0, len_ref.shape[0], note, jnp.int32(0), unroll=4)
    first_ref[0] = 0


def fill_segments(seg_ref, len_ref, home_ref):
    slots, span = seg_ref.shape
    slot = lax.broadcasted_iota(jnp.int32, (slots, span), 0)
    position = lax.broadcasted_iota(jnp.int32, (slots, span), 1)
    for i in range(slots):
        position += jnp.where(slot == i, home_ref[i] * span, 0)

    def note(d, carry):
        end, segment = carry
        end = end + len_ref[d]
        return end, segment + jnp.where(end <= position, 1.0, 0.0)

    start = (jnp.int32(0), jnp.zeros((slots, span), F32))
    seg_ref[...] = lax.fori_loop(0, len_ref.shape[0], note, start, unroll=4)[1]


def tokens_at(i, span):
    return pl.ds(pl.multiple_of(i * span, span), span)


def rows_at(i, rows):
    return pl.ds(pl.multiple_of(i * rows, rows), rows)


def put_state(ref, i, h, rows, value):
    chunks = HEAD_SIZE // rows
    for part in range(chunks):
        ref[h * chunks + part, rows_at(i, rows), :] = value[part * rows : (part + 1) * rows]


def get_state(ref, i, h, rows):
    chunks = HEAD_SIZE // rows
    return ref[h * chunks : (h + 1) * chunks, rows_at(i, rows), :].reshape(HEAD_SIZE, HEAD_SIZE)


def span_copies(i, span, sources, targets, sem):
    at = tokens_at(i, span)
    return [
        pltpu.make_async_copy(source.at[at], target.at[at], sem.at[a, i])
        for a, (source, target) in enumerate(zip(sources, targets))
    ]


def start_all(copies):
    for copy in copies:
        copy.start()


def wait_all(copies):
    for copy in copies:
        copy.wait()


def each_span(slots, unroll, load, compute, store):
    def turn(g, carry):
        group = [g * unroll + j for j in range(unroll)]
        for i in group:
            wait_all(load(i))
        for i in group:
            compute(i)
        for i in group:
            start_all(store(i))
        return carry

    lax.fori_loop(0, slots // unroll, turn, 0)


def nothing(i):
    return []


def partner_masks(devices):
    return [0] + list(range(devices - 1, 0, -1))


def own_index():
    return lax.axis_index("seq")


def block_stores(packed, blocks, i, rows, sem):
    me, at = own_index(), rows_at(i, rows)
    masks = partner_masks(len(blocks))
    return [
        pltpu.make_async_copy(packed.at[jnp.bitwise_xor(me, masks[k]), at], block.at[at], sem.at[k, i])
        for k, block in enumerate(blocks)
    ]


def take_blocks(blocks, packed):
    me = own_index()
    for mask, block in zip(partner_masks(len(blocks)), blocks):
        packed[jnp.bitwise_xor(me, mask)] = block[...]


def summary_kernel(heads, rows, span, count, len_ref, home_ref, rate_ref, k_hbm, v_hbm, *refs):
    blocks, refs = refs[:count], refs[count:]
    k_ref, v_ref, first_ref, last_ref, table, packed, tail_ref, sem, out_sem, tail_sem = refs
    slots = home_ref.shape[0]
    load = lambda i: span_copies(i, span, (k_hbm, v_hbm), (k_ref, v_ref), sem)
    for i in range(slots):
        start_all(load(i))
    fill_tables(len_ref, first_ref, last_ref, span)
    fill_key_table(table, rate_ref, 0, span)
    tail = jnp.zeros((TAIL, LANES), F32)
    lane = lax.broadcasted_iota(jnp.int32, (TAIL, LANES), 1)
    for i in range(slots):
        tail = jnp.where(lane == i, home_ref[i].astype(F32), tail)
    tail_ref[...] = tail.astype(BF16)
    ending = [
        pltpu.make_async_copy(tail_ref, block.at[pl.ds(slots * rows, TAIL)], tail_sem.at[k])
        for k, block in enumerate(blocks)
    ]
    start_all(ending)
    send = lambda i: block_stores(packed, blocks, i, rows, out_sem)

    def body(i):
        at = tokens_at(i, span)
        live = token_index(span) >= last_ref[home_ref[i]]
        for h in range(heads):
            cols = head_cols(h)
            side = jnp.where(live, table[h], 0.0)
            weighted = (side * v_ref[at, cols].astype(F32)).astype(BF16)
            put_state(packed, i, h, rows, dot(k_ref[at, cols], weighted, 0, 0).astype(BF16))

    each_span(slots, UNROLL["summary"], load, body, send)
    for i in range(slots):
        wait_all(send(i))
    wait_all(ending)


def scan_kernel(rows, span, reverse, count, first_ref, order_in, rate_ref, *refs):
    sources, refs = refs[:count], refs[count if reverse else count + 1 :]
    targets, refs = refs[:count], refs[count:]
    if reverse:
        order_ref = order_in
        arrived, states, out_sem = refs
    else:
        order_ref, arrived, states, homes, home_ref, home_sem, out_sem = refs
    slots = states.shape[1] // rows
    spans = order_ref.shape[0]
    if not reverse:
        for k, ref in enumerate(sources):
            homes[k : k + 1, :] = ref[slots * rows :, :].astype(F32)[0:1].astype(jnp.int32)
        gather = pltpu.make_async_copy(homes, home_ref, home_sem)
        gather.start()
    for k, ref in enumerate(sources):
        arrived[k] = ref[: slots * rows]
    head = (own_index() * rows) // HEAD_SIZE
    factor = jnp.exp(jnp.full((8, LANES), -rate_ref[head] * span, F32))[0:1]
    if not reverse:
        gather.wait()

        def note(k, carry):
            for i in range(slots):
                order_ref[home_ref[k, i]] = k * slots + i
            return carry

        lax.fori_loop(0, count, note, 0)

    def body(i, state):
        c = spans - 1 - i if reverse else i
        place = order_ref[c]
        block, slot = place // slots, place % slots
        at = rows_at(slot, rows)
        states[block, at, :] = state.astype(BF16)
        carried = jnp.where(first_ref[c] >= span, factor * state, 0.0)
        return carried + arrived[block, at, :].astype(F32)

    lax.fori_loop(0, spans, body, jnp.zeros((rows, LANES), F32), unroll=4)
    out = [pltpu.make_async_copy(states.at[k], ref, out_sem.at[k]) for k, ref in enumerate(targets)]
    start_all(out)
    wait_all(out)


def local_kernel(
    heads, span, len_ref, home_ref, rate_ref, q_hbm, u_hbm, k_ref, v_ref,
    out_ref, q_ref, u_ref, seg_ref, decay, sem, u_sem,
):
    slots = home_ref.shape[0]
    load = lambda i: span_copies(i, span, (q_hbm,), (q_ref,), sem)
    later = lambda i: span_copies(i, span, (u_hbm,), (u_ref,), u_sem)
    for i in range(slots):
        start_all(load(i))
    for i in range(slots):
        start_all(later(i))
    fill_segments(seg_ref, len_ref, home_ref)
    fill_decay(decay, rate_ref, 0, span)

    def body(i):
        at = tokens_at(i, span)
        seg = seg_ref[pl.ds(i, 1), :]
        same = row_to_cols(seg, span) == seg
        for h in range(heads):
            cols = head_cols(h)
            scores = dot(q_ref[at, cols], k_ref[at, cols], 1, 1)
            mixing = (scores * jnp.where(same, decay[h], 0.0)).astype(BF16)
            out_ref[at, cols] = dot(mixing, v_ref[at, cols], 1, 0)

    each_span(slots, UNROLL["local"], load, body, nothing)
    for i in range(slots):
        wait_all(later(i))


def output_kernel(
    heads, rows, span, count, first_ref, home_ref, rate_ref, gain_ref, q_ref, u_ref, inner_ref, *refs
):
    blocks, refs = refs[:count], refs[count:]
    out_ref, sums_ref, prev, table = refs
    slots = home_ref.shape[0]
    take_blocks(blocks, prev)
    fill_query_table(table, rate_ref, 0, span)

    def body(i):
        at = tokens_at(i, span)
        live = token_index(span) < first_ref[home_ref[i]]
        squares = jnp.zeros((span, LANES), F32)
        crossed = jnp.zeros((span, LANES), F32)
        for h in range(heads):
            cols = head_cols(h)
            outer = dot(q_ref[at, cols], get_state(prev, i, h, rows), 1, 0)
            attn = inner_ref[at, cols] + jnp.where(live, table[h], 0.0) * outer
            out_ref[at, cols] = attn
            squares += attn * attn
            crossed += gain_ref[:, cols] * u_ref[at, cols].astype(F32) * attn
        sums_ref[0, pl.ds(i, 1), :] = cols_to_row(squares)
        sums_ref[1, pl.ds(i, 1), :] = cols_to_row(crossed)

    each_span(slots, UNROLL["output"], nothing, body, nothing)


def cotangent_kernel(
    heads, rows, span, count, channels, first_ref, home_ref, rate_ref, gain_ref, sums_ref, q_ref, u_ref, attn_ref, *refs
):
    g_ref, blocks = refs[0], refs[1 : 1 + count]
    table, factors, packed, out_sem = refs[1 + count :]
    slots = home_ref.shape[0]
    scaling = 1.0 / jnp.sqrt(jnp.sum(sums_ref[:, 0], axis=0) / channels + EPSILON)
    pulled = jnp.sum(sums_ref[:, 1], axis=0) / channels
    factors[0] = scaling
    factors[1] = scaling * scaling * scaling * pulled
    fill_query_table(table, rate_ref, 0, span)

    def body(i):
        at = tokens_at(i, span)
        direct = row_to_cols(factors[0, pl.ds(i, 1), :], LANES)
        along = row_to_cols(factors[1, pl.ds(i, 1), :], LANES)
        live = token_index(span) < first_ref[home_ref[i]]
        for h in range(heads):
            cols = head_cols(h)
            grad = direct * gain_ref[:, cols] * u_ref[at, cols].astype(F32)
            grad = (grad - along * attn_ref[at, cols]).astype(BF16)
            g_ref[at, cols] = grad
            weighted = (jnp.where(live, table[h], 0.0) * grad.astype(F32)).astype(BF16)
            put_state(packed, i, h, rows, dot(q_ref[at, cols], weighted, 0, 0).astype(BF16))

    send = lambda i: block_stores(packed, blocks, i, rows, out_sem)
    each_span(slots, UNROLL["cotangent"], nothing, body, send)
    for i in range(slots):
        wait_all(send(i))


def inner_grads_kernel(
    heads, rows, span, count, half, first_ref, home_ref, rate_ref, seg_ref, q_ref, k_ref, v_ref, g_ref, *refs
):
    blocks, refs = refs[:count], refs[count + half :]
    dq_hbm, dk_ref, dv_ref, dq_ref, prev, decay, table, out_sem = refs
    slots = home_ref.shape[0] // 2
    base = half * slots
    target = dq_hbm.at[pl.ds(base * span, slots * span)]
    store = lambda i: span_copies(i, span, (dq_ref,), (target,), out_sem)
    take_blocks(blocks, prev)
    fill_decay(decay, rate_ref, 0, span)
    fill_query_table(table, rate_ref, 0, span)

    def body(own):
        i = base + own
        at, own = tokens_at(i, span), tokens_at(own, span)
        seg = seg_ref[pl.ds(i, 1), :]
        same = row_to_cols(seg, span) == seg
        live = token_index(span) < first_ref[home_ref[i]]
        for h in range(heads):
            cols = head_cols(h)
            q, k, v, g = q_ref[at, cols], k_ref[at, cols], v_ref[at, cols], g_ref[at, cols]
            mask = jnp.where(same, decay[h], 0.0)
            mixing = (dot(q, k, 1, 1) * mask).astype(BF16)
            score_grad = (dot(g, v, 1, 1) * mask).astype(BF16)
            outer = dot(g, get_state(prev, i, h, rows), 1, 1)
            dq = dot(score_grad, k, 1, 0) + jnp.where(live, table[h], 0.0) * outer
            dq_ref[own, cols] = dq.astype(BF16)
            dk_ref[own, cols] = dot(score_grad, q, 0, 0)
            dv_ref[own, cols] = dot(mixing, g, 0, 0)

    each_span(slots, UNROLL["inner_grads"], nothing, body, store)
    for i in range(slots):
        wait_all(store(i))


def outer_grads_kernel(
    heads, rows, span, count, last_ref, home_ref, rate_ref, k_ref, v_ref, dk_0, dv_0, dk_1, dv_1, *refs
):
    blocks, refs = refs[:count], refs[count:]
    dk_hbm, dv_hbm, dk_ref, dv_ref, after_ref, table, out_sem = refs
    slots = home_ref.shape[0]
    store = lambda i: span_copies(i, span, (dk_ref, dv_ref), (dk_hbm, dv_hbm), out_sem)
    take_blocks(blocks, after_ref)
    fill_key_table(table, rate_ref, 0, span)

    def body(half, own):
        dk_in, dv_in = ((dk_0, dv_0), (dk_1, dv_1))[half]
        i = half * (slots // 2) + own
        at, own = tokens_at(i, span), tokens_at(own, span)
        live = token_index(span) >= last_ref[home_ref[i]]
        for h in range(heads):
            cols = head_cols(h)
            side = jnp.where(live, table[h], 0.0)
            after = get_state(after_ref, i, h, rows)
            dk = dk_in[own, cols] + side * dot(v_ref[at, cols], after, 1, 1)
            dv = dv_in[own, cols] + side * dot(k_ref[at, cols], after, 1, 0)
            dk_ref[at, cols] = dk.astype(BF16)
            dv_ref[at, cols] = dv.astype(BF16)

    for half in range(2):
        keep = lambda own, half=half: store(half * (slots // 2) + own)
        each_span(slots // 2, UNROLL["outer_grads"], nothing, functools.partial(body, half), keep)
    for i in range(slots):
        wait_all(store(i))


def exchange(blocks):
    devices = len(blocks)
    return tuple(
        lax.ppermute(block, "seq", [(i, i ^ mask) for i in range(devices)]) if mask else block
        for mask, block in zip(partner_masks(devices), blocks)
    )


def shards(query, key, value, upstream, norm_gain, decay_rate, document_lengths, group_home):
    devices = lax.axis_size("seq")
    assert devices & (devices - 1) == 0
    tokens, width = query.shape
    heads = width // HEAD_SIZE
    slots = group_home.shape[0]
    span = tokens // slots
    spans = slots * devices
    rows = width // devices
    channels = width * lax.axis_size("head")

    gain = norm_gain.reshape(1, width)

    smem = pl.BlockSpec(memory_space=pltpu.SMEM)
    vmem = pl.BlockSpec(memory_space=pltpu.VMEM)
    hbm = pl.BlockSpec(memory_space=pl.ANY)
    spans_table = jax.ShapeDtypeStruct((spans + 1,), jnp.int32)
    whole = jax.ShapeDtypeStruct((tokens, width), BF16)
    token_bf16 = pltpu.VMEM((tokens, width), BF16)
    token_f32 = pltpu.VMEM((tokens, width), F32)
    table = pltpu.VMEM((heads, span, LANES), F32)
    decay = pltpu.VMEM((heads, span, span), F32)
    states = pltpu.VMEM((devices, slots * rows, LANES), BF16)
    out = [jax.ShapeDtypeStruct(states.shape[1:], BF16)] * devices
    sent = [jax.ShapeDtypeStruct((slots * rows + TAIL, LANES), BF16)] * devices
    blocks = [hbm] * devices
    taken = [vmem] * devices

    def sems(*shape):
        return pltpu.SemaphoreType.DMA(shape)

    def call(kernel, name, limit, flops, in_specs, out_specs, out_shape, scratch, *static, aliases={}):
        return pl.pallas_call(
            functools.partial(kernel, *static),
            in_specs=in_specs,
            out_specs=out_specs,
            out_shape=out_shape,
            scratch_shapes=scratch,
            input_output_aliases=aliases,
            compiler_params=pltpu.CompilerParams(vmem_limit_bytes=limit << 20),
            cost_estimate=pl.CostEstimate(flops=flops, bytes_accessed=0, transcendentals=0),
            name=name,
        )

    work = 2 * tokens * width * span
    *moving, key_v, value_v, first, last = call(
        summary_kernel, "summaries", ALONE, work // 2,
        [smem, smem, smem, hbm, hbm],
        blocks + [vmem, vmem, smem, smem],
        sent + [token_bf16, token_bf16, spans_table, spans_table],
        [table, states, pltpu.VMEM((TAIL, LANES), BF16), sems(2, slots), sems(devices, slots), sems(devices)],
        heads, rows, span, devices,
    )(document_lengths, group_home, decay_rate, key, value)
    arrived = exchange(moving)

    inner, query_v, upstream_v, seg = call(
        local_kernel, "inner", LIMIT, 2 * work,
        [smem, smem, smem, hbm, hbm, vmem, vmem],
        [vmem, vmem, vmem, vmem],
        [token_f32, token_bf16, token_bf16, pltpu.VMEM((slots, span), F32)],
        [decay, sems(1, slots), sems(1, slots)],
        heads, span,
    )(document_lengths, group_home, decay_rate, query, upstream, key_v, value_v)

    def scan(arrived, order, reverse, *after_it):
        held = [states, states]
        if reverse:
            extra_specs, extra = [], []
        else:
            extra_specs, extra = [smem], [jax.ShapeDtypeStruct((spans,), jnp.int32)]
            table_shape = (devices, LANES)
            held += [pltpu.VMEM(table_shape, jnp.int32), pltpu.SMEM(table_shape, jnp.int32), pltpu.SemaphoreType.DMA]
        return call(
            scan_kernel, "scan", LIMIT, work // 8,
            [smem, smem, smem] + taken + [hbm] * len(after_it),
            blocks + extra_specs,
            out + extra,
            held + [sems(devices)],
            rows, span, reverse, devices,
        )(first, order, decay_rate, *arrived, *after_it)

    *moving, order = scan(arrived, group_home, False, seg)
    prev = exchange(moving)
    attn, sums = call(
        output_kernel, "output", LIMIT, work // 2,
        [smem, smem, smem, vmem, vmem, vmem, vmem] + taken,
        [vmem, vmem],
        [token_f32, jax.ShapeDtypeStruct((2, slots, span), F32)],
        [states, table],
        heads, rows, span, devices,
    )(first, group_home, decay_rate, gain, query_v, upstream_v, inner, *prev)
    sums = lax.all_gather(sums, "head")

    grad_in, *moving = call(
        cotangent_kernel, "cotangent", LIMIT, work // 2,
        [smem, smem, smem, vmem, vmem, vmem, vmem, vmem],
        [vmem] + blocks,
        [token_bf16] + out,
        [table, pltpu.VMEM((2, slots, span), F32), states, sems(devices, slots)],
        heads, rows, span, devices, channels,
    )(first, group_home, decay_rate, gain, sums, query_v, upstream_v, attn)
    arrived = exchange(moving)

    half_f32 = pltpu.VMEM((tokens // 2, width), F32)

    def inner_grads(half, *into):
        return call(
            inner_grads_kernel, "inner_grads", LIMIT, 3 * work,
            [smem, smem, smem, vmem, vmem, vmem, vmem, vmem] + taken + [hbm] * half,
            [hbm, vmem, vmem],
            [whole, half_f32, half_f32],
            [pltpu.VMEM((tokens // 2, width), BF16), states, decay, table, sems(1, slots // 2)],
            heads, rows, span, devices, half,
            aliases={8 + devices: 0} if half else {},
        )(first, group_home, decay_rate, seg, query_v, key_v, value_v, grad_in, *prev, *into)

    query_half, *parts = inner_grads(0)
    query_grad, *others = inner_grads(1, query_half)
    after = exchange(scan(arrived, order, True))
    key_grad, value_grad = call(
        outer_grads_kernel, "outer_grads", LIMIT, work,
        [smem, smem, smem, vmem, vmem, vmem, vmem, vmem, vmem] + taken,
        [hbm, hbm],
        [whole, whole],
        [token_bf16, token_bf16, states, table, sems(2, slots)],
        heads, rows, span, devices,
    )(last, group_home, decay_rate, key_v, value_v, *parts, *others, *after)
    return query_grad, key_grad, value_grad


def solution(mesh):
    in_specs = (
        P("seq", "head"),
        P("seq", "head"),
        P("seq", "head"),
        P("seq", "head"),
        P("head"),
        P("head"),
        P(),
        P("seq"),
    )
    out_specs = (P("seq", "head"), P("seq", "head"), P("seq", "head"))
    return jax.shard_map(shards, mesh=mesh, in_specs=in_specs, out_specs=out_specs, check_vma=False)
```

```python
import functools

import jax
import jax.numpy as jnp
from jax import lax
from jax.experimental import pallas as pl
from jax.experimental.pallas import tpu as pltpu
from jax.sharding import PartitionSpec as P


HEAD_SIZE = 128
LANES = 128
EPSILON = 1e-06
UNROLL = {"summary": 4, "local": 2, "output": 4, "cotangent": 4, "inner_grads": 2, "outer_grads": 4}
TAIL = 16
ALONE = 58
LIMIT = 16
F32 = jnp.float32
BF16 = jnp.bfloat16


def dot(a, b, ca, cb):
    return lax.dot_general(a, b, (((ca,), (cb,)), ((), ())), preferred_element_type=F32)


def head_cols(h):
    return slice(h * HEAD_SIZE, (h + 1) * HEAD_SIZE)


def token_index(span):
    return lax.broadcasted_iota(jnp.int32, (span, LANES), 0)


def fill_key_table(table, rate_ref, base, span):
    for h in range(table.shape[0]):
        table[h] = jnp.exp(-rate_ref[base + h] * (span - 1.0 - token_index(span).astype(F32)))


def fill_query_table(table, rate_ref, base, span):
    for h in range(table.shape[0]):
        table[h] = jnp.exp(-rate_ref[base + h] * (token_index(span).astype(F32) + 1.0))


def fill_decay(decay, rate_ref, base, span):
    j = lax.broadcasted_iota(jnp.int32, (span, span), 0)
    l = lax.broadcasted_iota(jnp.int32, (span, span), 1)
    spread = (j - l).astype(F32)
    for h in range(decay.shape[0]):
        falling = jnp.exp(-rate_ref[base + h] * jnp.maximum(spread, 0.0))
        decay[h] = jnp.where(spread >= 0.0, falling, 0.0)


def row_to_cols(row, width):
    cols = jnp.transpose(jnp.broadcast_to(row, (LANES, row.shape[1])))
    return jnp.concatenate([cols] * (width // LANES), axis=1) if width > LANES else cols


def cols_to_row(cols):
    return jnp.sum(jnp.transpose(cols), axis=0, keepdims=True)


def fill_tables(len_ref, first_ref, last_ref, span):
    spans = first_ref.shape[0] - 1
    far = jnp.int32(spans * span)

    def reset(c, carry):
        first_ref[c] = far
        last_ref[c] = 0
        return carry

    def note(d, end):
        end = end + len_ref[d]
        c = lax.shift_right_logical(end, span.bit_length() - 1) if span & (span - 1) == 0 else end // span
        inside = end - c * span
        last_ref[c] = inside
        first_ref[c] = jnp.minimum(first_ref[c], inside)
        return end

    lax.fori_loop(0, spans + 1, reset, 0, unroll=8)
    lax.fori_loop(0, len_ref.shape[0], note, jnp.int32(0), unroll=4)
    first_ref[0] = 0


def fill_segments(seg_ref, len_ref, home_ref):
    slots, span = seg_ref.shape
    slot = lax.broadcasted_iota(jnp.int32, (slots, span), 0)
    position = lax.broadcasted_iota(jnp.int32, (slots, span), 1)
    for i in range(slots):
        position += jnp.where(slot == i, home_ref[i] * span, 0)

    def note(d, carry):
        end, segment = carry
        end = end + len_ref[d]
        return end, segment + jnp.where(end <= position, 1.0, 0.0)

    start = (jnp.int32(0), jnp.zeros((slots, span), F32))
    seg_ref[...] = lax.fori_loop(0, len_ref.shape[0], note, start, unroll=4)[1]


def tokens_at(i, span):
    return pl.ds(pl.multiple_of(i * span, span), span)


def rows_at(i, rows):
    return pl.ds(pl.multiple_of(i * rows, rows), rows)


def put_state(ref, i, h, rows, value):
    chunks = HEAD_SIZE // rows
    for part in range(chunks):
        ref[h * chunks + part, rows_at(i, rows), :] = value[part * rows : (part + 1) * rows]


def get_state(ref, i, h, rows):
    chunks = HEAD_SIZE // rows
    return ref[h * chunks : (h + 1) * chunks, rows_at(i, rows), :].reshape(HEAD_SIZE, HEAD_SIZE)


def span_copies(i, span, sources, targets, sem):
    at = tokens_at(i, span)
    return [
        pltpu.make_async_copy(source.at[at], target.at[at], sem.at[a, i])
        for a, (source, target) in enumerate(zip(sources, targets))
    ]


def start_all(copies):
    for copy in copies:
        copy.start()


def wait_all(copies):
    for copy in copies:
        copy.wait()


def each_span(slots, unroll, load, compute, store):
    def turn(g, carry):
        group = [g * unroll + j for j in range(unroll)]
        for i in group:
            wait_all(load(i))
        for i in group:
            compute(i)
        for i in group:
            start_all(store(i))
        return carry

    lax.fori_loop(0, slots // unroll, turn, 0)


def nothing(i):
    return []


def partner_masks(devices):
    return [0] + list(range(devices - 1, 0, -1))


def own_index():
    return lax.axis_index("seq")


def give_blocks(packed, blocks, size):
    me = own_index()
    for mask, block in zip(partner_masks(len(blocks)), blocks):
        block[:size] = packed[jnp.bitwise_xor(me, mask)]


def take_blocks(blocks, packed):
    me = own_index()
    for mask, block in zip(partner_masks(len(blocks)), blocks):
        packed[jnp.bitwise_xor(me, mask)] = block[...]


def summary_kernel(heads, rows, span, count, len_ref, home_ref, rate_ref, k_hbm, v_hbm, *refs):
    blocks, refs = refs[:count], refs[count:]
    k_ref, v_ref, first_ref, last_ref, table, packed, sem = refs
    slots = home_ref.shape[0]
    load = lambda i: span_copies(i, span, (k_hbm, v_hbm), (k_ref, v_ref), sem)
    for i in range(slots):
        start_all(load(i))
    fill_tables(len_ref, first_ref, last_ref, span)
    fill_key_table(table, rate_ref, 0, span)
    tail = jnp.zeros((TAIL, LANES), F32)
    lane = lax.broadcasted_iota(jnp.int32, (TAIL, LANES), 1)
    for i in range(slots):
        tail = jnp.where(lane == i, home_ref[i].astype(F32), tail)
    for block in blocks:
        block[slots * rows :, :] = tail.astype(BF16)

    def body(i):
        at = tokens_at(i, span)
        live = token_index(span) >= last_ref[home_ref[i]]
        for h in range(heads):
            cols = head_cols(h)
            side = jnp.where(live, table[h], 0.0)
            weighted = (side * v_ref[at, cols].astype(F32)).astype(BF16)
            put_state(packed, i, h, rows, dot(k_ref[at, cols], weighted, 0, 0).astype(BF16))

    each_span(slots, UNROLL["summary"], load, body, nothing)
    give_blocks(packed, blocks, slots * rows)


def scan_kernel(rows, span, reverse, count, first_ref, order_in, rate_ref, *refs):
    sources, refs = refs[:count], refs[count if reverse else count + 1 :]
    targets, refs = refs[:count], refs[count:]
    if reverse:
        order_ref = order_in
        arrived, states = refs
    else:
        order_ref, arrived, states, homes, home_ref, home_sem = refs
    slots = states.shape[1] // rows
    spans = order_ref.shape[0]
    if not reverse:
        for k, ref in enumerate(sources):
            homes[k : k + 1, :] = ref[slots * rows :, :].astype(F32)[0:1].astype(jnp.int32)
        gather = pltpu.make_async_copy(homes, home_ref, home_sem)
        gather.start()
    for k, ref in enumerate(sources):
        arrived[k] = ref[: slots * rows]
    head = (own_index() * rows) // HEAD_SIZE
    factor = jnp.exp(jnp.full((8, LANES), -rate_ref[head] * span, F32))[0:1]
    if not reverse:
        gather.wait()

        def note(k, carry):
            for i in range(slots):
                order_ref[home_ref[k, i]] = k * slots + i
            return carry

        lax.fori_loop(0, count, note, 0)

    def body(i, state):
        c = spans - 1 - i if reverse else i
        place = order_ref[c]
        block, slot = place // slots, place % slots
        at = rows_at(slot, rows)
        states[block, at, :] = state.astype(BF16)
        carried = jnp.where(first_ref[c] >= span, factor * state, 0.0)
        return carried + arrived[block, at, :].astype(F32)

    lax.fori_loop(0, spans, body, jnp.zeros((rows, LANES), F32), unroll=4)
    for k, ref in enumerate(targets):
        ref[...] = states[k]


def local_kernel(
    heads, span, len_ref, home_ref, rate_ref, q_hbm, u_hbm, k_ref, v_ref,
    out_ref, q_ref, u_ref, seg_ref, decay, sem, u_sem,
):
    slots = home_ref.shape[0]
    load = lambda i: span_copies(i, span, (q_hbm,), (q_ref,), sem)
    later = lambda i: span_copies(i, span, (u_hbm,), (u_ref,), u_sem)
    for i in range(slots):
        start_all(load(i))
    for i in range(slots):
        start_all(later(i))
    fill_segments(seg_ref, len_ref, home_ref)
    fill_decay(decay, rate_ref, 0, span)

    def body(i):
        at = tokens_at(i, span)
        seg = seg_ref[pl.ds(i, 1), :]
        same = row_to_cols(seg, span) == seg
        for h in range(heads):
            cols = head_cols(h)
            scores = dot(q_ref[at, cols], k_ref[at, cols], 1, 1)
            mixing = (scores * jnp.where(same, decay[h], 0.0)).astype(BF16)
            out_ref[at, cols] = dot(mixing, v_ref[at, cols], 1, 0)

    each_span(slots, UNROLL["local"], load, body, nothing)
    for i in range(slots):
        wait_all(later(i))


def output_kernel(
    heads, rows, span, count, first_ref, home_ref, rate_ref, gain_ref, q_ref, u_ref, inner_ref, *refs
):
    blocks, refs = refs[:count], refs[count:]
    out_ref, sums_ref, prev, table = refs
    slots = home_ref.shape[0]
    take_blocks(blocks, prev)
    fill_query_table(table, rate_ref, 0, span)

    def body(i):
        at = tokens_at(i, span)
        live = token_index(span) < first_ref[home_ref[i]]
        squares = jnp.zeros((span, LANES), F32)
        crossed = jnp.zeros((span, LANES), F32)
        for h in range(heads):
            cols = head_cols(h)
            outer = dot(q_ref[at, cols], get_state(prev, i, h, rows), 1, 0)
            attn = inner_ref[at, cols] + jnp.where(live, table[h], 0.0) * outer
            out_ref[at, cols] = attn
            squares += attn * attn
            crossed += gain_ref[:, cols] * u_ref[at, cols].astype(F32) * attn
        sums_ref[0, pl.ds(i, 1), :] = cols_to_row(squares)
        sums_ref[1, pl.ds(i, 1), :] = cols_to_row(crossed)

    each_span(slots, UNROLL["output"], nothing, body, nothing)


def cotangent_kernel(
    heads, rows, span, count, channels, others, first_ref, home_ref, rate_ref, gain_ref, q_ref, u_ref, attn_ref, *refs
):
    sums, refs = refs[:others], refs[others:]
    g_ref, blocks = refs[0], refs[1 : 1 + count]
    table, factors, packed = refs[1 + count :]
    slots = home_ref.shape[0]
    scaling = 1.0 / jnp.sqrt(sum(ref[0] for ref in sums) / channels + EPSILON)
    pulled = sum(ref[1] for ref in sums) / channels
    factors[0] = scaling
    factors[1] = scaling * scaling * scaling * pulled
    fill_query_table(table, rate_ref, 0, span)

    def body(i):
        at = tokens_at(i, span)
        direct = row_to_cols(factors[0, pl.ds(i, 1), :], LANES)
        along = row_to_cols(factors[1, pl.ds(i, 1), :], LANES)
        live = token_index(span) < first_ref[home_ref[i]]
        for h in range(heads):
            cols = head_cols(h)
            grad = direct * gain_ref[:, cols] * u_ref[at, cols].astype(F32)
            grad = (grad - along * attn_ref[at, cols]).astype(BF16)
            g_ref[at, cols] = grad
            weighted = (jnp.where(live, table[h], 0.0) * grad.astype(F32)).astype(BF16)
            put_state(packed, i, h, rows, dot(q_ref[at, cols], weighted, 0, 0).astype(BF16))

    each_span(slots, UNROLL["cotangent"], nothing, body, nothing)
    give_blocks(packed, blocks, slots * rows)


def inner_grads_kernel(
    heads, rows, span, count, half, first_ref, home_ref, rate_ref, seg_ref, q_ref, k_ref, v_ref, g_ref, *refs
):
    blocks, refs = refs[:count], refs[count + half :]
    dq_hbm, dk_ref, dv_ref, dq_ref, prev, decay, table, out_sem = refs
    slots = home_ref.shape[0] // 2
    base = half * slots
    target = dq_hbm.at[pl.ds(base * span, slots * span)]
    store = lambda i: span_copies(i, span, (dq_ref,), (target,), out_sem)
    take_blocks(blocks, prev)
    fill_decay(decay, rate_ref, 0, span)
    fill_query_table(table, rate_ref, 0, span)

    def body(own):
        i = base + own
        at, own = tokens_at(i, span), tokens_at(own, span)
        seg = seg_ref[pl.ds(i, 1), :]
        same = row_to_cols(seg, span) == seg
        live = token_index(span) < first_ref[home_ref[i]]
        for h in range(heads):
            cols = head_cols(h)
            q, k, v, g = q_ref[at, cols], k_ref[at, cols], v_ref[at, cols], g_ref[at, cols]
            mask = jnp.where(same, decay[h], 0.0)
            mixing = (dot(q, k, 1, 1) * mask).astype(BF16)
            score_grad = (dot(g, v, 1, 1) * mask).astype(BF16)
            outer = dot(g, get_state(prev, i, h, rows), 1, 1)
            dq = dot(score_grad, k, 1, 0) + jnp.where(live, table[h], 0.0) * outer
            dq_ref[own, cols] = dq.astype(BF16)
            dk_ref[own, cols] = dot(score_grad, q, 0, 0)
            dv_ref[own, cols] = dot(mixing, g, 0, 0)

    each_span(slots, UNROLL["inner_grads"], nothing, body, store)
    for i in range(slots):
        wait_all(store(i))


def outer_grads_kernel(
    heads, rows, span, count, last_ref, home_ref, rate_ref, k_ref, v_ref, dk_0, dv_0, dk_1, dv_1, *refs
):
    blocks, refs = refs[:count], refs[count:]
    dk_hbm, dv_hbm, dk_ref, dv_ref, after_ref, table, out_sem = refs
    slots = home_ref.shape[0]
    store = lambda i: span_copies(i, span, (dk_ref, dv_ref), (dk_hbm, dv_hbm), out_sem)
    take_blocks(blocks, after_ref)
    fill_key_table(table, rate_ref, 0, span)

    def body(half, own):
        dk_in, dv_in = ((dk_0, dv_0), (dk_1, dv_1))[half]
        i = half * (slots // 2) + own
        at, own = tokens_at(i, span), tokens_at(own, span)
        live = token_index(span) >= last_ref[home_ref[i]]
        for h in range(heads):
            cols = head_cols(h)
            side = jnp.where(live, table[h], 0.0)
            after = get_state(after_ref, i, h, rows)
            dk = dk_in[own, cols] + side * dot(v_ref[at, cols], after, 1, 1)
            dv = dv_in[own, cols] + side * dot(k_ref[at, cols], after, 1, 0)
            dk_ref[at, cols] = dk.astype(BF16)
            dv_ref[at, cols] = dv.astype(BF16)

    for half in range(2):
        keep = lambda own, half=half: store(half * (slots // 2) + own)
        each_span(slots // 2, UNROLL["outer_grads"], nothing, functools.partial(body, half), keep)
    for i in range(slots):
        wait_all(store(i))


def exchange(blocks):
    devices = len(blocks)
    return tuple(
        lax.ppermute(block, "seq", [(i, i ^ mask) for i in range(devices)]) if mask else block
        for mask, block in zip(partner_masks(devices), blocks)
    )


def everyone(array, axis):
    devices = lax.axis_size(axis)
    return tuple(
        lax.ppermute(array, axis, [(i, i ^ mask) for i in range(devices)]) if mask else array
        for mask in partner_masks(devices)
    )


def shards(query, key, value, upstream, norm_gain, decay_rate, document_lengths, group_home):
    devices = lax.axis_size("seq")
    assert devices & (devices - 1) == 0
    tokens, width = query.shape
    heads = width // HEAD_SIZE
    slots = group_home.shape[0]
    span = tokens // slots
    spans = slots * devices
    rows = width // devices
    channels = width * lax.axis_size("head")

    gain = norm_gain.reshape(1, width)

    smem = pl.BlockSpec(memory_space=pltpu.SMEM)
    vmem = pl.BlockSpec(memory_space=pltpu.VMEM)
    hbm = pl.BlockSpec(memory_space=pl.ANY)
    spans_table = jax.ShapeDtypeStruct((spans + 1,), jnp.int32)
    whole = jax.ShapeDtypeStruct((tokens, width), BF16)
    token_bf16 = pltpu.VMEM((tokens, width), BF16)
    token_f32 = pltpu.VMEM((tokens, width), F32)
    table = pltpu.VMEM((heads, span, LANES), F32)
    decay = pltpu.VMEM((heads, span, span), F32)
    states = pltpu.VMEM((devices, slots * rows, LANES), BF16)
    out = [jax.ShapeDtypeStruct(states.shape[1:], BF16)] * devices
    sent = [jax.ShapeDtypeStruct((slots * rows + TAIL, LANES), BF16)] * devices
    taken = [vmem] * devices

    def sems(*shape):
        return pltpu.SemaphoreType.DMA(shape)

    def call(kernel, name, limit, flops, in_specs, out_specs, out_shape, scratch, *static, aliases={}):
        return pl.pallas_call(
            functools.partial(kernel, *static),
            in_specs=in_specs,
            out_specs=out_specs,
            out_shape=out_shape,
            scratch_shapes=scratch,
            input_output_aliases=aliases,
            compiler_params=pltpu.CompilerParams(vmem_limit_bytes=limit << 20),
            cost_estimate=pl.CostEstimate(flops=flops, bytes_accessed=0, transcendentals=0),
            name=name,
        )

    work = 2 * tokens * width * span
    *moving, key_v, value_v, first, last = call(
        summary_kernel, "summaries", ALONE, work // 2,
        [smem, smem, smem, hbm, hbm],
        taken + [vmem, vmem, smem, smem],
        sent + [token_bf16, token_bf16, spans_table, spans_table],
        [table, states, sems(2, slots)],
        heads, rows, span, devices,
    )(document_lengths, group_home, decay_rate, key, value)
    arrived = exchange(moving)

    inner, query_v, upstream_v, seg = call(
        local_kernel, "inner", LIMIT, 2 * work,
        [smem, smem, smem, hbm, hbm, vmem, vmem],
        [vmem, vmem, vmem, vmem],
        [token_f32, token_bf16, token_bf16, pltpu.VMEM((slots, span), F32)],
        [decay, sems(1, slots), sems(1, slots)],
        heads, span,
    )(document_lengths, group_home, decay_rate, query, upstream, key_v, value_v)

    def scan(arrived, order, reverse, *after_it):
        held = [states, states]
        if reverse:
            extra_specs, extra = [], []
        else:
            extra_specs, extra = [smem], [jax.ShapeDtypeStruct((spans,), jnp.int32)]
            table_shape = (devices, LANES)
            held += [pltpu.VMEM(table_shape, jnp.int32), pltpu.SMEM(table_shape, jnp.int32), pltpu.SemaphoreType.DMA]
        return call(
            scan_kernel, "scan", LIMIT, work // 8,
            [smem, smem, smem] + taken + [hbm] * len(after_it),
            taken + extra_specs,
            out + extra,
            held,
            rows, span, reverse, devices,
        )(first, order, decay_rate, *arrived, *after_it)

    *moving, order = scan(arrived, group_home, False, seg)
    prev = exchange(moving)
    attn, sums = call(
        output_kernel, "output", LIMIT, work // 2,
        [smem, smem, smem, vmem, vmem, vmem, vmem] + taken,
        [vmem, vmem],
        [token_f32, jax.ShapeDtypeStruct((2, slots, span), F32)],
        [states, table],
        heads, rows, span, devices,
    )(first, group_home, decay_rate, gain, query_v, upstream_v, inner, *prev)
    sums = everyone(sums, "head")

    grad_in, *moving = call(
        cotangent_kernel, "cotangent", LIMIT, work // 2,
        [smem, smem, smem, vmem, vmem, vmem, vmem] + [vmem] * len(sums),
        [vmem] + taken,
        [token_bf16] + out,
        [table, pltpu.VMEM((2, slots, span), F32), states],
        heads, rows, span, devices, channels, len(sums),
    )(first, group_home, decay_rate, gain, query_v, upstream_v, attn, *sums)
    arrived = exchange(moving)

    half_f32 = pltpu.VMEM((tokens // 2, width), F32)

    def inner_grads(half, *into):
        return call(
            inner_grads_kernel, "inner_grads", LIMIT, 3 * work,
            [smem, smem, smem, vmem, vmem, vmem, vmem, vmem] + taken + [hbm] * half,
            [hbm, vmem, vmem],
            [whole, half_f32, half_f32],
            [pltpu.VMEM((tokens // 2, width), BF16), states, decay, table, sems(1, slots // 2)],
            heads, rows, span, devices, half,
            aliases={8 + devices: 0} if half else {},
        )(first, group_home, decay_rate, seg, query_v, key_v, value_v, grad_in, *prev, *into)

    query_half, *parts = inner_grads(0)
    query_grad, *others = inner_grads(1, query_half)
    after = exchange(scan(arrived, order, True))
    key_grad, value_grad = call(
        outer_grads_kernel, "outer_grads", LIMIT, work,
        [smem, smem, smem, vmem, vmem, vmem, vmem, vmem, vmem] + taken,
        [hbm, hbm],
        [whole, whole],
        [token_bf16, token_bf16, states, table, sems(2, slots)],
        heads, rows, span, devices,
    )(last, group_home, decay_rate, key_v, value_v, *parts, *others, *after)
    return query_grad, key_grad, value_grad


def solution(mesh):
    in_specs = (
        P("seq", "head"),
        P("seq", "head"),
        P("seq", "head"),
        P("seq", "head"),
        P("head"),
        P("head"),
        P(),
        P("seq"),
    )
    out_specs = (P("seq", "head"), P("seq", "head"), P("seq", "head"))
    return jax.shard_map(shards, mesh=mesh, in_specs=in_specs, out_specs=out_specs, check_vma=False)
```

```python
import functools

import jax
import jax.numpy as jnp
from jax import lax
from jax.experimental import pallas as pl
from jax.experimental.pallas import tpu as pltpu
from jax.sharding import PartitionSpec as P


HEAD_SIZE = 128
LANES = 128
EPSILON = 1e-06
UNROLL = {"summary": 4, "local": 4, "output": 8, "cotangent": 8, "inner_grads": 4, "outer_grads": 2}
TAIL = 16
ALONE = 58
LIMIT = 16
F32 = jnp.float32
BF16 = jnp.bfloat16


def dot(a, b, ca, cb):
    return lax.dot_general(a, b, (((ca,), (cb,)), ((), ())), preferred_element_type=F32)


def head_cols(h):
    return slice(h * HEAD_SIZE, (h + 1) * HEAD_SIZE)


def token_index(span):
    return lax.broadcasted_iota(jnp.int32, (span, LANES), 0)


def key_side(rate, span):
    return jnp.exp(-rate * (span - 1.0 - token_index(span).astype(F32)))


def query_side(rate, span):
    return jnp.exp(-rate * (token_index(span).astype(F32) + 1.0))


def fill_decay(decay, rate_ref, base, span):
    j = lax.broadcasted_iota(jnp.int32, (span, span), 0)
    l = lax.broadcasted_iota(jnp.int32, (span, span), 1)
    spread = (j - l).astype(F32)
    for h in range(decay.shape[0]):
        falling = jnp.exp(-rate_ref[base + h] * jnp.maximum(spread, 0.0))
        decay[h] = jnp.where(spread >= 0.0, falling, 0.0)


def row_to_cols(row, width):
    cols = jnp.transpose(jnp.broadcast_to(row, (LANES, row.shape[1])))
    return jnp.concatenate([cols] * (width // LANES), axis=1) if width > LANES else cols


def cols_to_row(cols):
    return jnp.sum(jnp.transpose(cols), axis=0, keepdims=True)


def fill_tables(len_ref, first_ref, last_ref, span):
    spans = first_ref.shape[0] - 1
    far = jnp.int32(spans * span)

    def reset(c, carry):
        first_ref[c] = far
        last_ref[c] = 0
        return carry

    def note(d, end):
        end = end + len_ref[d]
        c = lax.shift_right_logical(end, span.bit_length() - 1) if span & (span - 1) == 0 else end // span
        inside = end - c * span
        last_ref[c] = inside
        first_ref[c] = jnp.minimum(first_ref[c], inside)
        return end

    lax.fori_loop(0, spans + 1, reset, 0, unroll=8)
    lax.fori_loop(0, len_ref.shape[0], note, jnp.int32(0), unroll=4)
    first_ref[0] = 0


def fill_segments(seg_ref, len_ref, home_ref):
    slots, span = seg_ref.shape
    slot = lax.broadcasted_iota(jnp.int32, (slots, span), 0)
    position = lax.broadcasted_iota(jnp.int32, (slots, span), 1)
    for i in range(slots):
        position += jnp.where(slot == i, home_ref[i] * span, 0)

    def note(d, carry):
        end, segment = carry
        end = end + len_ref[d]
        return end, segment + jnp.where(end <= position, 1.0, 0.0)

    start = (jnp.int32(0), jnp.zeros((slots, span), F32))
    seg_ref[...] = lax.fori_loop(0, len_ref.shape[0], note, start, unroll=4)[1]


def tokens_at(i, span):
    return pl.ds(pl.multiple_of(i * span, span), span)


def rows_at(i, rows):
    return pl.ds(pl.multiple_of(i * rows, rows), rows)


def get_state(ref, i, h, rows):
    chunks = HEAD_SIZE // rows
    return ref[h * chunks : (h + 1) * chunks, rows_at(i, rows), :].reshape(HEAD_SIZE, HEAD_SIZE)


def span_copies(i, span, sources, targets, sem):
    at = tokens_at(i, span)
    return [
        pltpu.make_async_copy(source.at[at], target.at[at], sem.at[a, i])
        for a, (source, target) in enumerate(zip(sources, targets))
    ]


def start_all(copies):
    for copy in copies:
        copy.start()


def wait_all(copies):
    for copy in copies:
        copy.wait()


def each_span(slots, unroll, load, compute, store):
    def turn(g, carry):
        group = [g * unroll + j for j in range(unroll)]
        for i in group:
            wait_all(load(i))
        for i in group:
            compute(i)
        for i in group:
            start_all(store(i))
        return carry

    lax.fori_loop(0, slots // unroll, turn, 0)


def nothing(i):
    return []


def own_index():
    return lax.axis_index("seq")


def group_head(group, chunks):
    head = jnp.bitwise_xor(own_index() // chunks, group)
    return head, pl.ds(pl.multiple_of(head * HEAD_SIZE, HEAD_SIZE), HEAD_SIZE)


def put_group(packed, g, i, rows, value):
    chunks = HEAD_SIZE // rows
    for part in range(chunks):
        packed[g * chunks + part, rows_at(i, rows), :] = value[part * rows : (part + 1) * rows]


def get_group(packed, g, i, rows):
    chunks = HEAD_SIZE // rows
    return packed[g * chunks : (g + 1) * chunks, rows_at(i, rows), :].reshape(HEAD_SIZE, HEAD_SIZE)


def give_groups(packed, blocks, chunks, size):
    turn = own_index() % chunks
    for n, block in enumerate(blocks):
        block[:size] = packed[n // chunks * chunks + jnp.bitwise_xor(turn, n % chunks)]


def take_groups(blocks, packed, chunks):
    turn = own_index() % chunks
    for n, block in enumerate(blocks):
        packed[n // chunks * chunks + jnp.bitwise_xor(turn, n % chunks)] = block[...]


def take_blocks(blocks, packed):
    me = own_index()
    for mask, block in enumerate(blocks):
        packed[jnp.bitwise_xor(me, mask)] = block[...]


def summary_kernel(groups, rows, span, count, lead, *refs):
    if lead:
        len_ref, home_ref, rate_ref, k_hbm, v_hbm = refs[:5]
        blocks, refs = refs[5 : 5 + count], refs[5 + count :]
        first_ref, last_ref, k_ref, v_ref, table, packed, sem = refs
    else:
        last_ref, home_ref, rate_ref, k_hbm, v_hbm = refs[:5]
        blocks, refs = refs[5 : 5 + count], refs[5 + count :]
        k_ref, v_ref, table, packed, sem = refs
    slots = home_ref.shape[0]
    chunks = HEAD_SIZE // rows
    heads = [group_head(p, chunks) for p in groups]
    sources = [ref.at[:, heads[0][1]] if lead else ref for ref in (k_hbm, v_hbm)]
    load = lambda i: span_copies(i, span, sources, (k_ref, v_ref), sem)
    for i in range(slots):
        start_all(load(i))
    if lead:
        fill_tables(len_ref, first_ref, last_ref, span)
    for g, (head, cols) in enumerate(heads):
        table[g] = key_side(rate_ref[head], span)
    tail = jnp.zeros((TAIL, LANES), F32)
    lane = lax.broadcasted_iota(jnp.int32, (TAIL, LANES), 1)
    for i in range(slots):
        tail = jnp.where(lane == i, home_ref[i].astype(F32), tail)
    for block in blocks:
        block[slots * rows :, :] = tail.astype(BF16)

    def body(i):
        at = tokens_at(i, span)
        live = token_index(span) >= last_ref[home_ref[i]]
        for g, (head, cols) in enumerate(heads):
            cols = slice(None) if lead else cols
            side = jnp.where(live, table[g], 0.0)
            weighted = (side * v_ref[at, cols].astype(F32)).astype(BF16)
            put_group(packed, g, i, rows, dot(k_ref[at, cols], weighted, 0, 0).astype(BF16))

    each_span(slots, UNROLL["summary"], load, body, nothing)
    give_groups(packed, blocks, chunks, slots * rows)


def scan_kernel(rows, span, reverse, count, first_ref, order_in, rate_ref, *refs):
    sources, refs = refs[:count], refs[count if reverse else count + 1 :]
    targets, refs = refs[:count], refs[count:]
    if reverse:
        order_ref = order_in
        arrived, states = refs
    else:
        order_ref, arrived, states, homes, home_ref, home_sem = refs
    slots = states.shape[1] // rows
    spans = order_ref.shape[0]
    if not reverse:
        for k, ref in enumerate(sources):
            homes[k : k + 1, :] = ref[slots * rows :, :].astype(F32)[0:1].astype(jnp.int32)
        gather = pltpu.make_async_copy(homes, home_ref, home_sem)
        gather.start()
    for k, ref in enumerate(sources):
        arrived[k] = ref[: slots * rows]
    head = (own_index() * rows) // HEAD_SIZE
    factor = jnp.exp(jnp.full((8, LANES), -rate_ref[head] * span, F32))[0:1]
    if not reverse:
        gather.wait()

        def note(k, carry):
            for i in range(slots):
                order_ref[home_ref[k, i]] = k * slots + i
            return carry

        lax.fori_loop(0, count, note, 0)

    def body(i, state):
        c = spans - 1 - i if reverse else i
        place = order_ref[c]
        block, slot = place // slots, place % slots
        at = rows_at(slot, rows)
        states[block, at, :] = state.astype(BF16)
        carried = jnp.where(first_ref[c] >= span, factor * state, 0.0)
        return carried + arrived[block, at, :].astype(F32)

    lax.fori_loop(0, spans, body, jnp.zeros((rows, LANES), F32), unroll=4)
    for k, ref in enumerate(targets):
        ref[...] = states[k]


def local_kernel(
    heads, span, len_ref, home_ref, rate_ref, q_hbm, u_hbm, k_ref, v_ref,
    out_ref, q_ref, u_ref, seg_ref, decay, sem, u_sem,
):
    slots = home_ref.shape[0]
    load = lambda i: span_copies(i, span, (q_hbm,), (q_ref,), sem)
    later = lambda i: span_copies(i, span, (u_hbm,), (u_ref,), u_sem)
    for i in range(slots):
        start_all(load(i))
    for i in range(slots):
        start_all(later(i))
    fill_segments(seg_ref, len_ref, home_ref)
    fill_decay(decay, rate_ref, 0, span)

    def body(i):
        at = tokens_at(i, span)
        seg = seg_ref[pl.ds(i, 1), :]
        same = row_to_cols(seg, span) == seg
        for h in range(heads):
            cols = head_cols(h)
            scores = dot(q_ref[at, cols], k_ref[at, cols], 1, 1)
            mixing = (scores * jnp.where(same, decay[h], 0.0)).astype(BF16)
            out_ref[at, cols] = dot(mixing, v_ref[at, cols], 1, 0)

    each_span(slots, UNROLL["local"], load, body, nothing)
    for i in range(slots):
        wait_all(later(i))


def output_kernel(
    groups, rows, span, count, again, first_ref, home_ref, rate_ref, gain_ref, q_ref, u_ref, inner_ref, *refs
):
    blocks, refs = refs[:count], refs[count:]
    if again:
        before_ref, refs = refs[0], refs[2:]
    out_ref, sums_ref, prev, table = refs
    slots = home_ref.shape[0]
    chunks = HEAD_SIZE // rows
    heads = [group_head(p, chunks) for p in groups]
    take_groups(blocks, prev, chunks)
    for g, (head, cols) in enumerate(heads):
        table[g] = query_side(rate_ref[head], span)

    def body(i):
        at = tokens_at(i, span)
        live = token_index(span) < first_ref[home_ref[i]]
        squares = jnp.zeros((span, LANES), F32)
        crossed = jnp.zeros((span, LANES), F32)
        for g, (head, cols) in enumerate(heads):
            outer = dot(q_ref[at, cols], get_group(prev, g, i, rows), 1, 0)
            attn = inner_ref[at, cols] + jnp.where(live, table[g], 0.0) * outer
            out_ref[at, cols] = attn
            squares += attn * attn
            crossed += gain_ref[:, cols] * u_ref[at, cols].astype(F32) * attn
        squares, crossed = cols_to_row(squares), cols_to_row(crossed)
        if again:
            squares += before_ref[0, pl.ds(i, 1), :]
            crossed += before_ref[1, pl.ds(i, 1), :]
        sums_ref[0, pl.ds(i, 1), :] = squares
        sums_ref[1, pl.ds(i, 1), :] = crossed

    each_span(slots, UNROLL["output"], nothing, body, nothing)


def cotangent_kernel(
    groups, rows, span, count, again, channels, others, first_ref, home_ref, rate_ref, gain_ref, q_ref, u_ref, attn_ref, *refs
):
    sums, refs = refs[:others], refs[others + again :]
    g_ref, blocks = refs[0], refs[1 : 1 + count]
    table, factors, packed = refs[1 + count :]
    slots = home_ref.shape[0]
    chunks = HEAD_SIZE // rows
    heads = [group_head(p, chunks) for p in groups]
    scaling = 1.0 / jnp.sqrt(sum(ref[0] for ref in sums) / channels + EPSILON)
    pulled = sum(ref[1] for ref in sums) / channels
    factors[0] = scaling
    factors[1] = scaling * scaling * scaling * pulled
    for g, (head, cols) in enumerate(heads):
        table[g] = query_side(rate_ref[head], span)

    def body(i):
        at = tokens_at(i, span)
        direct = row_to_cols(factors[0, pl.ds(i, 1), :], LANES)
        along = row_to_cols(factors[1, pl.ds(i, 1), :], LANES)
        live = token_index(span) < first_ref[home_ref[i]]
        for g, (head, cols) in enumerate(heads):
            grad = direct * gain_ref[:, cols] * u_ref[at, cols].astype(F32)
            grad = (grad - along * attn_ref[at, cols]).astype(BF16)
            g_ref[at, cols] = grad
            weighted = (jnp.where(live, table[g], 0.0) * grad.astype(F32)).astype(BF16)
            put_group(packed, g, i, rows, dot(q_ref[at, cols], weighted, 0, 0).astype(BF16))

    each_span(slots, UNROLL["cotangent"], nothing, body, nothing)
    give_groups(packed, blocks, chunks, slots * rows)


def inner_grads_kernel(
    heads, rows, span, count, half, first_ref, home_ref, rate_ref, seg_ref, q_ref, k_ref, v_ref, g_ref, *refs
):
    blocks, refs = refs[:count], refs[count + half :]
    dq_hbm, dk_ref, dv_ref, dq_ref, prev, decay, table, out_sem = refs
    slots = home_ref.shape[0] // 2
    base = half * slots
    target = dq_hbm.at[pl.ds(base * span, slots * span)]
    store = lambda i: span_copies(i, span, (dq_ref,), (target,), out_sem)
    take_blocks(blocks, prev)
    fill_decay(decay, rate_ref, 0, span)
    for h in range(heads):
        table[h] = query_side(rate_ref[h], span)

    def body(own):
        i = base + own
        at, own = tokens_at(i, span), tokens_at(own, span)
        seg = seg_ref[pl.ds(i, 1), :]
        same = row_to_cols(seg, span) == seg
        live = token_index(span) < first_ref[home_ref[i]]
        for h in range(heads):
            cols = head_cols(h)
            q, k, v, g = q_ref[at, cols], k_ref[at, cols], v_ref[at, cols], g_ref[at, cols]
            mask = jnp.where(same, decay[h], 0.0)
            mixing = (dot(q, k, 1, 1) * mask).astype(BF16)
            score_grad = (dot(g, v, 1, 1) * mask).astype(BF16)
            outer = dot(g, get_state(prev, i, h, rows), 1, 1)
            dq = dot(score_grad, k, 1, 0) + jnp.where(live, table[h], 0.0) * outer
            dq_ref[own, cols] = dq.astype(BF16)
            dk_ref[own, cols] = dot(score_grad, q, 0, 0)
            dv_ref[own, cols] = dot(mixing, g, 0, 0)

    each_span(slots, UNROLL["inner_grads"], nothing, body, store)
    for i in range(slots):
        wait_all(store(i))


def outer_grads_kernel(
    groups, rows, span, count, again, last_ref, home_ref, rate_ref, k_ref, v_ref, dk_0, dv_0, dk_1, dv_1, *refs
):
    blocks, refs = refs[:count], refs[count + 2 * again :]
    dk_hbm, dv_hbm, dk_ref, dv_ref, after_ref, table, out_sem = refs
    slots = home_ref.shape[0]
    chunks = HEAD_SIZE // rows
    heads = [group_head(p, chunks) for p in groups]

    def store(i):
        copies = []
        for g, (head, cols) in enumerate(heads):
            targets = (dk_hbm.at[:, cols], dv_hbm.at[:, cols])
            sources = (dk_ref.at[g], dv_ref.at[g])
            copies += span_copies(i, span, sources, targets, out_sem.at[g])
        return copies

    take_groups(blocks, after_ref, chunks)
    for g, (head, cols) in enumerate(heads):
        table[g] = key_side(rate_ref[head], span)

    def body(half, own):
        dk_in, dv_in = ((dk_0, dv_0), (dk_1, dv_1))[half]
        i = half * (slots // 2) + own
        at, own = tokens_at(i, span), tokens_at(own, span)
        live = token_index(span) >= last_ref[home_ref[i]]
        for g, (head, cols) in enumerate(heads):
            side = jnp.where(live, table[g], 0.0)
            after = get_group(after_ref, g, i, rows)
            dk = dk_in[own, cols] + side * dot(v_ref[at, cols], after, 1, 1)
            dv = dv_in[own, cols] + side * dot(k_ref[at, cols], after, 1, 0)
            dk_ref[g, at, :] = dk.astype(BF16)
            dv_ref[g, at, :] = dv.astype(BF16)

    for half in range(2):
        keep = lambda own, half=half: store(half * (slots // 2) + own)
        each_span(slots // 2, 4 if len(groups) == 1 else UNROLL["outer_grads"], nothing, functools.partial(body, half), keep)
    for i in range(slots):
        wait_all(store(i))


def swap(array, axis, mask):
    if mask == 0:
        return array
    return lax.ppermute(array, axis, [(i, i ^ mask) for i in range(lax.axis_size(axis))])


def exchange(blocks):
    moved = [None] * len(blocks)
    for mask in range(len(blocks) - 1, -1, -1):
        moved[mask] = swap(blocks[mask], "seq", mask)
    return moved


def shards(query, key, value, upstream, norm_gain, decay_rate, document_lengths, group_home):
    devices = lax.axis_size("seq")
    assert devices & (devices - 1) == 0
    tokens, width = query.shape
    heads = width // HEAD_SIZE
    slots = group_home.shape[0]
    span = tokens // slots
    spans = slots * devices
    rows = width // devices
    channels = width * lax.axis_size("head")

    gain = norm_gain.reshape(1, width)

    smem = pl.BlockSpec(memory_space=pltpu.SMEM)
    vmem = pl.BlockSpec(memory_space=pltpu.VMEM)
    hbm = pl.BlockSpec(memory_space=pl.ANY)
    spans_table = jax.ShapeDtypeStruct((spans + 1,), jnp.int32)
    whole = jax.ShapeDtypeStruct((tokens, width), BF16)
    token_bf16 = pltpu.VMEM((tokens, width), BF16)
    token_f32 = pltpu.VMEM((tokens, width), F32)
    table = pltpu.VMEM((heads, span, LANES), F32)
    decay = pltpu.VMEM((heads, span, span), F32)
    states = pltpu.VMEM((devices, slots * rows, LANES), BF16)
    out = [jax.ShapeDtypeStruct(states.shape[1:], BF16)] * devices
    taken = [vmem] * devices
    chunks = devices // heads
    assert heads > 1 and heads & (heads - 1) == 0
    final = heads // 2
    ahead, behind = (heads - 1,), tuple(range(heads - 2, -1, -1))
    early, late = tuple(p for p in range(heads - 1, -1, -1) if p != final), (final,)

    def masks_of(groups):
        return [p * chunks + n for p in groups for n in range(chunks)]

    def pick(blocks, groups):
        return [blocks[mask] for mask in masks_of(groups)]

    def states_of(groups):
        return pltpu.VMEM((len(groups) * chunks, slots * rows, LANES), BF16)

    def table_of(groups):
        return pltpu.VMEM((len(groups), span, LANES), F32)

    def sems(*shape):
        return pltpu.SemaphoreType.DMA(shape)

    def call(kernel, limit, flops, in_specs, out_specs, out_shape, scratch, *static, aliases={}):
        return pl.pallas_call(
            functools.partial(kernel, *static),
            in_specs=in_specs,
            out_specs=out_specs,
            out_shape=out_shape,
            scratch_shapes=scratch,
            input_output_aliases=aliases,
            compiler_params=pltpu.CompilerParams(vmem_limit_bytes=limit << 20),
            cost_estimate=pl.CostEstimate(flops=flops, bytes_accessed=0, transcendentals=0),
        )

    work = 2 * tokens * width * span
    shape = [jax.ShapeDtypeStruct((slots * rows + TAIL, LANES), BF16)]
    count = len(masks_of(ahead))
    *sent, first, last = call(
        summary_kernel, ALONE, work // 8,
        [smem, smem, smem, hbm, hbm],
        [vmem] * count + [smem, smem],
        shape * count + [spans_table, spans_table],
        [pltpu.VMEM((tokens, HEAD_SIZE), BF16)] * 2 + [table_of(ahead), states_of(ahead), sems(2, slots)],
        ahead, rows, span, count, True,
    )(document_lengths, group_home, decay_rate, key, value)
    moving = dict(zip(masks_of(ahead), sent))
    count = len(masks_of(behind))
    *sent, key_v, value_v = call(
        summary_kernel, ALONE, work // 2,
        [smem, smem, smem, hbm, hbm],
        [vmem] * (count + 2),
        shape * count + [token_bf16, token_bf16],
        [table_of(behind), states_of(behind), sems(2, slots)],
        behind, rows, span, count, False,
    )(last, group_home, decay_rate, key, value)
    moving.update(zip(masks_of(behind), sent))
    arrived = exchange(moving)

    inner, query_v, upstream_v, seg = call(
        local_kernel, LIMIT, 2 * work,
        [smem, smem, smem, hbm, hbm, vmem, vmem],
        [vmem, vmem, vmem, vmem],
        [token_f32, token_bf16, token_bf16, pltpu.VMEM((slots, span), F32)],
        [decay, sems(1, slots), sems(1, slots)],
        heads, span,
    )(document_lengths, group_home, decay_rate, query, upstream, key_v, value_v)

    def scan(arrived, order, reverse, *after_it):
        held = [states, states]
        if reverse:
            extra_specs, extra = [], []
        else:
            extra_specs, extra = [smem], [jax.ShapeDtypeStruct((spans,), jnp.int32)]
            table_shape = (devices, LANES)
            held += [pltpu.VMEM(table_shape, jnp.int32), pltpu.SMEM(table_shape, jnp.int32), pltpu.SemaphoreType.DMA]
        return call(
            scan_kernel, LIMIT, work // 8,
            [smem, smem, smem] + taken + [hbm] * len(after_it),
            taken + extra_specs,
            out + extra,
            held,
            rows, span, reverse, devices,
        )(first, order, decay_rate, *arrived, *after_it)

    *moving, order = scan(arrived, group_home, False, seg)
    prev = exchange(moving)

    def outputs(groups, *before):
        count = len(masks_of(groups))
        again = len(before) > 0
        return call(
            output_kernel, LIMIT, work // 4,
            [smem, smem, smem] + [vmem] * (4 + count + len(before)),
            [vmem, vmem],
            [token_f32, jax.ShapeDtypeStruct((2, slots, span), F32)],
            [states_of(groups), table_of(groups)],
            groups, rows, span, count, again,
            aliases={8 + count: 0} if again else {},
        )(first, group_home, decay_rate, gain, query_v, upstream_v, inner, *pick(prev, groups), *before)

    attn, sums = outputs(early)
    attn, sums = outputs(late, sums, attn)
    sums = [swap(sums, "head", mask) for mask in range(lax.axis_size("head") - 1, -1, -1)]

    def cotangents(groups, *before):
        count = len(masks_of(groups))
        others = len(sums)
        return call(
            cotangent_kernel, LIMIT, work // 4,
            [smem, smem, smem] + [vmem] * (4 + others + len(before)),
            [vmem] * (1 + count),
            [token_bf16] + out[:count],
            [table_of(groups), pltpu.VMEM((2, slots, span), F32), states_of(groups)],
            groups, rows, span, count, len(before), channels, others,
            aliases={7 + others: 0} if before else {},
        )(first, group_home, decay_rate, gain, query_v, upstream_v, attn, *sums, *before)

    grad_in, *sent = cotangents(ahead)
    moving = dict(zip(masks_of(ahead), sent))
    grad_in, *sent = cotangents(behind, grad_in)
    moving.update(zip(masks_of(behind), sent))
    arrived = exchange(moving)

    half_f32 = pltpu.VMEM((tokens // 2, width), F32)

    def inner_grads(half, *into):
        return call(
            inner_grads_kernel, LIMIT, 3 * work,
            [smem, smem, smem, vmem, vmem, vmem, vmem, vmem] + taken + [hbm] * half,
            [hbm, vmem, vmem],
            [whole, half_f32, half_f32],
            [pltpu.VMEM((tokens // 2, width), BF16), states, decay, table, sems(1, slots // 2)],
            heads, rows, span, devices, half,
            aliases={8 + devices: 0} if half else {},
        )(first, group_home, decay_rate, seg, query_v, key_v, value_v, grad_in, *prev, *into)

    query_half, *parts = inner_grads(0)
    query_grad, *others = inner_grads(1, query_half)
    after = exchange(scan(arrived, order, True))

    def outer_grads(groups, *before):
        count = len(masks_of(groups))
        part = pltpu.VMEM((len(groups), tokens, HEAD_SIZE), BF16)
        return call(
            outer_grads_kernel, LIMIT, work // 2,
            [smem, smem, smem] + [vmem] * (6 + count) + [hbm] * len(before),
            [hbm, hbm],
            [whole, whole],
            [part, part, states_of(groups), table_of(groups), sems(len(groups), 2, slots)],
            groups, rows, span, count, len(before) > 0,
            aliases={9 + count: 0, 10 + count: 1} if before else {},
        )(last, group_home, decay_rate, key_v, value_v, *parts, *others, *pick(after, groups), *before)

    finals = outer_grads(early)
    key_grad, value_grad = outer_grads(late, *finals)
    return query_grad, key_grad, value_grad


def solution(mesh):
    in_specs = (
        P("seq", "head"),
        P("seq", "head"),
        P("seq", "head"),
        P("seq", "head"),
        P("head"),
        P("head"),
        P(),
        P("seq"),
    )
    out_specs = (P("seq", "head"), P("seq", "head"), P("seq", "head"))

    return jax.shard_map(shards, mesh=mesh, in_specs=in_specs, out_specs=out_specs, check_vma=False)
```

```python
import functools

import jax
import jax.numpy as jnp
from jax import lax
from jax.experimental import pallas as pl
from jax.experimental.pallas import tpu as pltpu
from jax.sharding import PartitionSpec as P


HEAD_SIZE = 128
LANES = 128
EPSILON = 1e-06
UNROLL = {"summary": 4, "local": 4, "output": 8, "cotangent": 8, "inner_grads": 4, "outer_grads": 2}
TAIL = 16
ALONE = 58
LIMIT = 16
F32 = jnp.float32
BF16 = jnp.bfloat16


def dot(a, b, ca, cb):
    return lax.dot_general(a, b, (((ca,), (cb,)), ((), ())), preferred_element_type=F32)


def head_cols(h):
    return slice(h * HEAD_SIZE, (h + 1) * HEAD_SIZE)


def token_index(span):
    return lax.broadcasted_iota(jnp.int32, (span, LANES), 0)


def key_side(rate, span):
    return jnp.exp(-rate * (span - 1.0 - token_index(span).astype(F32)))


def query_side(rate, span):
    return jnp.exp(-rate * (token_index(span).astype(F32) + 1.0))


def fill_decay(decay, rate_ref, base, span):
    j = lax.broadcasted_iota(jnp.int32, (span, span), 0)
    l = lax.broadcasted_iota(jnp.int32, (span, span), 1)
    spread = (j - l).astype(F32)
    for h in range(decay.shape[0]):
        falling = jnp.exp(-rate_ref[base + h] * jnp.maximum(spread, 0.0))
        decay[h] = jnp.where(spread >= 0.0, falling, 0.0)


def row_to_cols(row, width):
    cols = jnp.transpose(jnp.broadcast_to(row, (LANES, row.shape[1])))
    return jnp.concatenate([cols] * (width // LANES), axis=1) if width > LANES else cols


def cols_to_row(cols):
    return jnp.sum(jnp.transpose(cols), axis=0, keepdims=True)


def fill_tables(len_ref, first_ref, last_ref, span):
    spans = first_ref.shape[0] - 1
    far = jnp.int32(spans * span)

    def reset(c, carry):
        first_ref[c] = far
        last_ref[c] = 0
        return carry

    def note(d, end):
        end = end + len_ref[d]
        c = lax.shift_right_logical(end, span.bit_length() - 1) if span & (span - 1) == 0 else end // span
        inside = end - c * span
        last_ref[c] = inside
        first_ref[c] = jnp.minimum(first_ref[c], inside)
        return end

    lax.fori_loop(0, spans + 1, reset, 0, unroll=8)
    lax.fori_loop(0, len_ref.shape[0], note, jnp.int32(0), unroll=4)
    first_ref[0] = 0


def fill_segments(seg_ref, len_ref, home_ref):
    slots, span = seg_ref.shape
    slot = lax.broadcasted_iota(jnp.int32, (slots, span), 0)
    position = lax.broadcasted_iota(jnp.int32, (slots, span), 1)
    for i in range(slots):
        position += jnp.where(slot == i, home_ref[i] * span, 0)

    def note(d, carry):
        end, segment = carry
        end = end + len_ref[d]
        return end, segment + jnp.where(end <= position, 1.0, 0.0)

    start = (jnp.int32(0), jnp.zeros((slots, span), F32))
    seg_ref[...] = lax.fori_loop(0, len_ref.shape[0], note, start, unroll=4)[1]


def tokens_at(i, span):
    return pl.ds(pl.multiple_of(i * span, span), span)


def rows_at(i, rows):
    return pl.ds(pl.multiple_of(i * rows, rows), rows)


def get_state(ref, i, h, rows):
    chunks = HEAD_SIZE // rows
    return ref[h * chunks : (h + 1) * chunks, rows_at(i, rows), :].reshape(HEAD_SIZE, HEAD_SIZE)


def span_copies(i, span, sources, targets, sem):
    at = tokens_at(i, span)
    return [
        pltpu.make_async_copy(source.at[at], target.at[at], sem.at[a, i])
        for a, (source, target) in enumerate(zip(sources, targets))
    ]


def start_all(copies):
    for copy in copies:
        copy.start()


def wait_all(copies):
    for copy in copies:
        copy.wait()


def each_span(slots, unroll, load, compute, store):
    def turn(g, carry):
        group = [g * unroll + j for j in range(unroll)]
        for i in group:
            wait_all(load(i))
        for i in group:
            compute(i)
        for i in group:
            start_all(store(i))
        return carry

    lax.fori_loop(0, slots // unroll, turn, 0)


def nothing(i):
    return []


def own_index():
    return lax.axis_index("seq")


def group_head(group, chunks):
    head = jnp.bitwise_xor(own_index() // chunks, group)
    return head, pl.ds(pl.multiple_of(head * HEAD_SIZE, HEAD_SIZE), HEAD_SIZE)


def put_group(packed, g, i, rows, value):
    chunks = HEAD_SIZE // rows
    for part in range(chunks):
        packed[g * chunks + part, rows_at(i, rows), :] = value[part * rows : (part + 1) * rows]


def get_group(packed, g, i, rows):
    chunks = HEAD_SIZE // rows
    return packed[g * chunks : (g + 1) * chunks, rows_at(i, rows), :].reshape(HEAD_SIZE, HEAD_SIZE)


def give_groups(packed, blocks, chunks, size):
    turn = own_index() % chunks
    for n, block in enumerate(blocks):
        block[:size] = packed[n // chunks * chunks + jnp.bitwise_xor(turn, n % chunks)]


def take_groups(blocks, packed, chunks):
    turn = own_index() % chunks
    for n, block in enumerate(blocks):
        packed[n // chunks * chunks + jnp.bitwise_xor(turn, n % chunks)] = block[...]


def take_blocks(blocks, packed):
    me = own_index()
    for mask, block in enumerate(blocks):
        packed[jnp.bitwise_xor(me, mask)] = block[...]


def summary_kernel(groups, rows, span, count, lead, *refs):
    if lead:
        len_ref, home_ref, rate_ref, k_hbm, v_hbm = refs[:5]
        blocks, refs = refs[5 : 5 + count], refs[5 + count :]
        first_ref, last_ref, k_ref, v_ref, table, packed, sem = refs
    else:
        last_ref, home_ref, rate_ref, k_hbm, v_hbm = refs[:5]
        blocks, refs = refs[5 : 5 + count], refs[5 + count :]
        k_ref, v_ref, table, packed, sem = refs
    slots = home_ref.shape[0]
    chunks = HEAD_SIZE // rows
    heads = [group_head(p, chunks) for p in groups]
    sources = [ref.at[:, heads[0][1]] if lead else ref for ref in (k_hbm, v_hbm)]
    load = lambda i: span_copies(i, span, sources, (k_ref, v_ref), sem)
    for i in range(slots):
        start_all(load(i))
    if lead:
        fill_tables(len_ref, first_ref, last_ref, span)
    for g, (head, cols) in enumerate(heads):
        table[g] = key_side(rate_ref[head], span)
    tail = jnp.zeros((TAIL, LANES), F32)
    lane = lax.broadcasted_iota(jnp.int32, (TAIL, LANES), 1)
    for i in range(slots):
        tail = jnp.where(lane == i, home_ref[i].astype(F32), tail)
    for block in blocks:
        block[slots * rows :, :] = tail.astype(BF16)

    def body(i):
        at = tokens_at(i, span)
        live = token_index(span) >= last_ref[home_ref[i]]
        for g, (head, cols) in enumerate(heads):
            cols = slice(None) if lead else cols
            side = jnp.where(live, table[g], 0.0)
            weighted = (side * v_ref[at, cols].astype(F32)).astype(BF16)
            put_group(packed, g, i, rows, dot(k_ref[at, cols], weighted, 0, 0).astype(BF16))

    each_span(slots, UNROLL["summary"], load, body, nothing)
    give_groups(packed, blocks, chunks, slots * rows)


def scan_kernel(rows, span, reverse, count, first_ref, order_in, rate_ref, *refs):
    sources, refs = refs[:count], refs[count if reverse else count + 1 :]
    targets, refs = refs[:count], refs[count:]
    if reverse:
        order_ref = order_in
        arrived, states = refs
    else:
        order_ref, arrived, states, homes, home_ref, home_sem = refs
    spans = order_ref.shape[0]
    slots = spans // count
    size = slots * rows
    if not reverse:
        for k, ref in enumerate(sources):
            homes[k : k + 1, :] = ref[slots * rows :, :].astype(F32)[0:1].astype(jnp.int32)
        gather = pltpu.make_async_copy(homes, home_ref, home_sem)
        gather.start()
    for k, ref in enumerate(sources):
        arrived[k * size : (k + 1) * size] = ref[:size]
    head = (own_index() * rows) // HEAD_SIZE
    factor = jnp.exp(jnp.full((8, LANES), -rate_ref[head] * span, F32))[0:1]
    if not reverse:
        gather.wait()

        def note(k, carry):
            for i in range(slots):
                order_ref[home_ref[k, i]] = k * slots + i
            return carry

        lax.fori_loop(0, count, note, 0, unroll=2)

    def body(i, state):
        c = spans - 1 - i if reverse else i
        place = order_ref[c]
        at = rows_at(place, rows)
        states[at, :] = state.astype(BF16)
        carried = jnp.where(first_ref[c] >= span, factor * state, 0.0)
        return carried + arrived[at, :].astype(F32)

    lax.fori_loop(0, spans, body, jnp.zeros((rows, LANES), F32), unroll=8)
    for k, ref in enumerate(targets):
        ref[...] = states[k * size : (k + 1) * size]


def local_kernel(
    heads, span, len_ref, home_ref, rate_ref, q_hbm, u_hbm, k_ref, v_ref,
    out_ref, q_ref, u_ref, seg_ref, decay, sem, u_sem,
):
    slots = home_ref.shape[0]
    load = lambda i: span_copies(i, span, (q_hbm,), (q_ref,), sem)
    later = lambda i: span_copies(i, span, (u_hbm,), (u_ref,), u_sem)
    for i in range(slots):
        start_all(load(i))
    for i in range(slots):
        start_all(later(i))
    fill_segments(seg_ref, len_ref, home_ref)
    fill_decay(decay, rate_ref, 0, span)

    def body(i):
        at = tokens_at(i, span)
        seg = seg_ref[pl.ds(i, 1), :]
        same = row_to_cols(seg, span) == seg
        for h in range(heads):
            cols = head_cols(h)
            scores = dot(q_ref[at, cols], k_ref[at, cols], 1, 1)
            mixing = (scores * jnp.where(same, decay[h], 0.0)).astype(BF16)
            out_ref[at, cols] = dot(mixing, v_ref[at, cols], 1, 0)

    each_span(slots, UNROLL["local"], load, body, nothing)
    for i in range(slots):
        wait_all(later(i))


def output_kernel(
    groups, rows, span, count, again, first_ref, home_ref, rate_ref, gain_ref, q_ref, u_ref, inner_ref, *refs
):
    blocks, refs = refs[:count], refs[count:]
    if again:
        before_ref, refs = refs[0], refs[2:]
    out_ref, sums_ref, prev, table = refs
    slots = home_ref.shape[0]
    chunks = HEAD_SIZE // rows
    heads = [group_head(p, chunks) for p in groups]
    take_groups(blocks, prev, chunks)
    for g, (head, cols) in enumerate(heads):
        table[g] = query_side(rate_ref[head], span)

    def body(i):
        at = tokens_at(i, span)
        live = token_index(span) < first_ref[home_ref[i]]
        squares = jnp.zeros((span, LANES), F32)
        crossed = jnp.zeros((span, LANES), F32)
        for g, (head, cols) in enumerate(heads):
            outer = dot(q_ref[at, cols], get_group(prev, g, i, rows), 1, 0)
            attn = inner_ref[at, cols] + jnp.where(live, table[g], 0.0) * outer
            out_ref[at, cols] = attn
            squares += attn * attn
            crossed += gain_ref[:, cols] * u_ref[at, cols].astype(F32) * attn
        squares, crossed = cols_to_row(squares), cols_to_row(crossed)
        if again:
            squares += before_ref[0, pl.ds(i, 1), :]
            crossed += before_ref[1, pl.ds(i, 1), :]
        sums_ref[0, pl.ds(i, 1), :] = squares
        sums_ref[1, pl.ds(i, 1), :] = crossed

    each_span(slots, UNROLL["output"], nothing, body, nothing)


def cotangent_kernel(
    groups, rows, span, count, again, channels, others, first_ref, home_ref, rate_ref, gain_ref, q_ref, u_ref, attn_ref, *refs
):
    sums, refs = refs[:others], refs[others + again :]
    g_ref, blocks = refs[0], refs[1 : 1 + count]
    table, factors, packed = refs[1 + count :]
    slots = home_ref.shape[0]
    chunks = HEAD_SIZE // rows
    heads = [group_head(p, chunks) for p in groups]
    scaling = 1.0 / jnp.sqrt(sum(ref[0] for ref in sums) / channels + EPSILON)
    pulled = sum(ref[1] for ref in sums) / channels
    factors[0] = scaling
    factors[1] = scaling * scaling * scaling * pulled
    for g, (head, cols) in enumerate(heads):
        table[g] = query_side(rate_ref[head], span)

    def body(i):
        at = tokens_at(i, span)
        direct = row_to_cols(factors[0, pl.ds(i, 1), :], LANES)
        along = row_to_cols(factors[1, pl.ds(i, 1), :], LANES)
        live = token_index(span) < first_ref[home_ref[i]]
        for g, (head, cols) in enumerate(heads):
            grad = direct * gain_ref[:, cols] * u_ref[at, cols].astype(F32)
            grad = (grad - along * attn_ref[at, cols]).astype(BF16)
            g_ref[at, cols] = grad
            weighted = (jnp.where(live, table[g], 0.0) * grad.astype(F32)).astype(BF16)
            put_group(packed, g, i, rows, dot(q_ref[at, cols], weighted, 0, 0).astype(BF16))

    each_span(slots, UNROLL["cotangent"], nothing, body, nothing)
    give_groups(packed, blocks, chunks, slots * rows)


def inner_grads_kernel(
    heads, rows, span, count, half, first_ref, home_ref, rate_ref, seg_ref, q_ref, k_ref, v_ref, g_ref, *refs
):
    blocks, refs = refs[:count], refs[count + half :]
    dq_hbm, dk_ref, dv_ref, dq_ref, prev, decay, table, out_sem = refs
    slots = home_ref.shape[0] // 2
    base = half * slots
    target = dq_hbm.at[pl.ds(base * span, slots * span)]
    store = lambda i: span_copies(i, span, (dq_ref,), (target,), out_sem)
    take_blocks(blocks, prev)
    fill_decay(decay, rate_ref, 0, span)
    for h in range(heads):
        table[h] = query_side(rate_ref[h], span)

    def body(own):
        i = base + own
        at, own = tokens_at(i, span), tokens_at(own, span)
        seg = seg_ref[pl.ds(i, 1), :]
        same = row_to_cols(seg, span) == seg
        live = token_index(span) < first_ref[home_ref[i]]
        for h in range(heads):
            cols = head_cols(h)
            q, k, v, g = q_ref[at, cols], k_ref[at, cols], v_ref[at, cols], g_ref[at, cols]
            mask = jnp.where(same, decay[h], 0.0)
            mixing = (dot(q, k, 1, 1) * mask).astype(BF16)
            score_grad = (dot(g, v, 1, 1) * mask).astype(BF16)
            outer = dot(g, get_state(prev, i, h, rows), 1, 1)
            dq = dot(score_grad, k, 1, 0) + jnp.where(live, table[h], 0.0) * outer
            dq_ref[own, cols] = dq.astype(BF16)
            dk_ref[own, cols] = dot(score_grad, q, 0, 0)
            dv_ref[own, cols] = dot(mixing, g, 0, 0)

    each_span(slots, UNROLL["inner_grads"], nothing, body, store)
    for i in range(slots):
        wait_all(store(i))


def outer_grads_kernel(
    groups, rows, span, count, again, last_ref, home_ref, rate_ref, k_ref, v_ref, dk_0, dv_0, dk_1, dv_1, *refs
):
    blocks, refs = refs[:count], refs[count + 2 * again :]
    dk_hbm, dv_hbm, dk_ref, dv_ref, after_ref, table, out_sem = refs
    slots = home_ref.shape[0]
    chunks = HEAD_SIZE // rows
    heads = [group_head(p, chunks) for p in groups]

    def store(i):
        copies = []
        for g, (head, cols) in enumerate(heads):
            targets = (dk_hbm.at[:, cols], dv_hbm.at[:, cols])
            sources = (dk_ref.at[g], dv_ref.at[g])
            copies += span_copies(i, span, sources, targets, out_sem.at[g])
        return copies

    take_groups(blocks, after_ref, chunks)
    for g, (head, cols) in enumerate(heads):
        table[g] = key_side(rate_ref[head], span)

    def body(half, own):
        dk_in, dv_in = ((dk_0, dv_0), (dk_1, dv_1))[half]
        i = half * (slots // 2) + own
        at, own = tokens_at(i, span), tokens_at(own, span)
        live = token_index(span) >= last_ref[home_ref[i]]
        for g, (head, cols) in enumerate(heads):
            side = jnp.where(live, table[g], 0.0)
            after = get_group(after_ref, g, i, rows)
            dk = dk_in[own, cols] + side * dot(v_ref[at, cols], after, 1, 1)
            dv = dv_in[own, cols] + side * dot(k_ref[at, cols], after, 1, 0)
            dk_ref[g, at, :] = dk.astype(BF16)
            dv_ref[g, at, :] = dv.astype(BF16)

    for half in range(2):
        keep = lambda own, half=half: store(half * (slots // 2) + own)
        each_span(slots // 2, 4 if len(groups) == 1 else UNROLL["outer_grads"], nothing, functools.partial(body, half), keep)
    for i in range(slots):
        wait_all(store(i))


def swap(array, axis, mask):
    if mask == 0:
        return array
    return lax.ppermute(array, axis, [(i, i ^ mask) for i in range(lax.axis_size(axis))])


def exchange(blocks):
    moved = [None] * len(blocks)
    for mask in range(len(blocks) - 1, -1, -1):
        moved[mask] = swap(blocks[mask], "seq", mask)
    return moved


def shards(query, key, value, upstream, norm_gain, decay_rate, document_lengths, group_home):
    devices = lax.axis_size("seq")
    assert devices & (devices - 1) == 0
    tokens, width = query.shape
    heads = width // HEAD_SIZE
    slots = group_home.shape[0]
    span = tokens // slots
    spans = slots * devices
    rows = width // devices
    channels = width * lax.axis_size("head")

    gain = norm_gain.reshape(1, width)

    smem = pl.BlockSpec(memory_space=pltpu.SMEM)
    vmem = pl.BlockSpec(memory_space=pltpu.VMEM)
    hbm = pl.BlockSpec(memory_space=pl.ANY)
    spans_table = jax.ShapeDtypeStruct((spans + 1,), jnp.int32)
    whole = jax.ShapeDtypeStruct((tokens, width), BF16)
    token_bf16 = pltpu.VMEM((tokens, width), BF16)
    token_f32 = pltpu.VMEM((tokens, width), F32)
    table = pltpu.VMEM((heads, span, LANES), F32)
    decay = pltpu.VMEM((heads, span, span), F32)
    states = pltpu.VMEM((devices, slots * rows, LANES), BF16)
    out = [jax.ShapeDtypeStruct(states.shape[1:], BF16)] * devices
    taken = [vmem] * devices
    chunks = devices // heads
    assert heads > 1 and heads & (heads - 1) == 0
    final = heads // 2
    ahead, behind = (heads - 1,), tuple(range(heads - 2, -1, -1))
    early, late = tuple(p for p in range(heads - 1, -1, -1) if p != final), (final,)

    def masks_of(groups):
        return [p * chunks + n for p in groups for n in range(chunks)]

    def pick(blocks, groups):
        return [blocks[mask] for mask in masks_of(groups)]

    def states_of(groups):
        return pltpu.VMEM((len(groups) * chunks, slots * rows, LANES), BF16)

    def table_of(groups):
        return pltpu.VMEM((len(groups), span, LANES), F32)

    def sems(*shape):
        return pltpu.SemaphoreType.DMA(shape)

    def call(kernel, limit, flops, in_specs, out_specs, out_shape, scratch, *static, aliases={}):
        return pl.pallas_call(
            functools.partial(kernel, *static),
            in_specs=in_specs,
            out_specs=out_specs,
            out_shape=out_shape,
            scratch_shapes=scratch,
            input_output_aliases=aliases,
            compiler_params=pltpu.CompilerParams(vmem_limit_bytes=limit << 20),
            cost_estimate=pl.CostEstimate(flops=flops, bytes_accessed=0, transcendentals=0),
        )

    work = 2 * tokens * width * span
    shape = [jax.ShapeDtypeStruct((slots * rows + TAIL, LANES), BF16)]
    count = len(masks_of(ahead))
    *sent, first, last = call(
        summary_kernel, ALONE, work // 8,
        [smem, smem, smem, hbm, hbm],
        [vmem] * count + [smem, smem],
        shape * count + [spans_table, spans_table],
        [pltpu.VMEM((tokens, HEAD_SIZE), BF16)] * 2 + [table_of(ahead), states_of(ahead), sems(2, slots)],
        ahead, rows, span, count, True,
    )(document_lengths, group_home, decay_rate, key, value)
    moving = dict(zip(masks_of(ahead), sent))
    count = len(masks_of(behind))
    *sent, key_v, value_v = call(
        summary_kernel, ALONE, work // 2,
        [smem, smem, smem, hbm, hbm],
        [vmem] * (count + 2),
        shape * count + [token_bf16, token_bf16],
        [table_of(behind), states_of(behind), sems(2, slots)],
        behind, rows, span, count, False,
    )(last, group_home, decay_rate, key, value)
    moving.update(zip(masks_of(behind), sent))
    arrived = exchange(moving)

    inner, query_v, upstream_v, seg = call(
        local_kernel, LIMIT, 2 * work,
        [smem, smem, smem, hbm, hbm, vmem, vmem],
        [vmem, vmem, vmem, vmem],
        [token_f32, token_bf16, token_bf16, pltpu.VMEM((slots, span), F32)],
        [decay, sems(1, slots), sems(1, slots)],
        heads, span,
    )(document_lengths, group_home, decay_rate, query, upstream, key_v, value_v)

    def scan(arrived, order, reverse, *after_it):
        held = [pltpu.VMEM((devices * slots * rows, LANES), BF16)] * 2
        if reverse:
            extra_specs, extra = [], []
        else:
            extra_specs, extra = [smem], [jax.ShapeDtypeStruct((spans,), jnp.int32)]
            table_shape = (devices, LANES)
            held += [pltpu.VMEM(table_shape, jnp.int32), pltpu.SMEM(table_shape, jnp.int32), pltpu.SemaphoreType.DMA]
        return call(
            scan_kernel, LIMIT, work // 8,
            [smem, smem, smem] + taken + [hbm] * len(after_it),
            taken + extra_specs,
            out + extra,
            held,
            rows, span, reverse, devices,
        )(first, order, decay_rate, *arrived, *after_it)

    *moving, order = scan(arrived, group_home, False, seg)
    prev = exchange(moving)

    def outputs(groups, *before):
        count = len(masks_of(groups))
        again = len(before) > 0
        return call(
            output_kernel, LIMIT, work // 4,
            [smem, smem, smem] + [vmem] * (4 + count + len(before)),
            [vmem, vmem],
            [token_f32, jax.ShapeDtypeStruct((2, slots, span), F32)],
            [states_of(groups), table_of(groups)],
            groups, rows, span, count, again,
            aliases={8 + count: 0} if again else {},
        )(first, group_home, decay_rate, gain, query_v, upstream_v, inner, *pick(prev, groups), *before)

    attn, sums = outputs(early)
    attn, sums = outputs(late, sums, attn)
    sums = [swap(sums, "head", mask) for mask in range(lax.axis_size("head") - 1, -1, -1)]

    def cotangents(groups, *before):
        count = len(masks_of(groups))
        others = len(sums)
        return call(
            cotangent_kernel, LIMIT, work // 4,
            [smem, smem, smem] + [vmem] * (4 + others + len(before)),
            [vmem] * (1 + count),
            [token_bf16] + out[:count],
            [table_of(groups), pltpu.VMEM((2, slots, span), F32), states_of(groups)],
            groups, rows, span, count, len(before), channels, others,
            aliases={7 + others: 0} if before else {},
        )(first, group_home, decay_rate, gain, query_v, upstream_v, attn, *sums, *before)

    grad_in, *sent = cotangents(ahead)
    moving = dict(zip(masks_of(ahead), sent))
    grad_in, *sent = cotangents(behind, grad_in)
    moving.update(zip(masks_of(behind), sent))
    arrived = exchange(moving)

    half_f32 = pltpu.VMEM((tokens // 2, width), F32)

    def inner_grads(half, *into):
        return call(
            inner_grads_kernel, LIMIT, 3 * work,
            [smem, smem, smem, vmem, vmem, vmem, vmem, vmem] + taken + [hbm] * half,
            [hbm, vmem, vmem],
            [whole, half_f32, half_f32],
            [pltpu.VMEM((tokens // 2, width), BF16), states, decay, table, sems(1, slots // 2)],
            heads, rows, span, devices, half,
            aliases={8 + devices: 0} if half else {},
        )(first, group_home, decay_rate, seg, query_v, key_v, value_v, grad_in, *prev, *into)

    query_half, *parts = inner_grads(0)
    query_grad, *others = inner_grads(1, query_half)
    after = exchange(scan(arrived, order, True))

    def outer_grads(groups, *before):
        count = len(masks_of(groups))
        part = pltpu.VMEM((len(groups), tokens, HEAD_SIZE), BF16)
        return call(
            outer_grads_kernel, LIMIT, work // 2,
            [smem, smem, smem] + [vmem] * (6 + count) + [hbm] * len(before),
            [hbm, hbm],
            [whole, whole],
            [part, part, states_of(groups), table_of(groups), sems(len(groups), 2, slots)],
            groups, rows, span, count, len(before) > 0,
            aliases={9 + count: 0, 10 + count: 1} if before else {},
        )(last, group_home, decay_rate, key_v, value_v, *parts, *others, *pick(after, groups), *before)

    finals = outer_grads(early)
    key_grad, value_grad = outer_grads(late, *finals)
    return query_grad, key_grad, value_grad


def solution(mesh):
    in_specs = (
        P("seq", "head"),
        P("seq", "head"),
        P("seq", "head"),
        P("seq", "head"),
        P("head"),
        P("head"),
        P(),
        P("seq"),
    )
    out_specs = (P("seq", "head"), P("seq", "head"), P("seq", "head"))

    return jax.shard_map(shards, mesh=mesh, in_specs=in_specs, out_specs=out_specs, check_vma=False)
```

```python
import functools

import jax
import jax.numpy as jnp
from jax import lax
from jax.experimental import pallas as pl
from jax.experimental.pallas import tpu as pltpu
from jax.sharding import PartitionSpec as P


HEAD_SIZE = 128
LANES = 128
EPSILON = 1e-06
UNROLL = {"summary": 4, "local": 4, "output": 8, "cotangent": 8, "inner_grads": 4, "outer_grads": 2}
TAIL = 16
ALONE = 58
LIMIT = 16
F32 = jnp.float32
BF16 = jnp.bfloat16


def dot(a, b, ca, cb):
    return lax.dot_general(a, b, (((ca,), (cb,)), ((), ())), preferred_element_type=F32)


def head_cols(h):
    return slice(h * HEAD_SIZE, (h + 1) * HEAD_SIZE)


def token_index(span):
    return lax.broadcasted_iota(jnp.int32, (span, LANES), 0)


def key_side(rate, span):
    return jnp.exp(-rate * (span - 1.0 - token_index(span).astype(F32)))


def query_side(rate, span):
    return jnp.exp(-rate * (token_index(span).astype(F32) + 1.0))


def fill_decay(decay, rate_ref, base, span):
    j = lax.broadcasted_iota(jnp.int32, (span, span), 0)
    l = lax.broadcasted_iota(jnp.int32, (span, span), 1)
    spread = (j - l).astype(F32)
    for h in range(decay.shape[0]):
        falling = jnp.exp(-rate_ref[base + h] * jnp.maximum(spread, 0.0))
        decay[h] = jnp.where(spread >= 0.0, falling, 0.0)


def row_to_cols(row, width):
    cols = jnp.transpose(jnp.broadcast_to(row, (LANES, row.shape[1])))
    return jnp.concatenate([cols] * (width // LANES), axis=1) if width > LANES else cols


def cols_to_row(cols):
    return jnp.sum(jnp.transpose(cols), axis=0, keepdims=True)


def fill_tables(len_ref, first_ref, last_ref, span):
    spans = first_ref.shape[0] - 1
    far = jnp.int32(spans * span)

    def reset(c, carry):
        first_ref[c] = far
        last_ref[c] = 0
        return carry

    def note(d, end):
        end = end + len_ref[d]
        c = lax.shift_right_logical(end, span.bit_length() - 1) if span & (span - 1) == 0 else end // span
        inside = end - c * span
        last_ref[c] = inside
        first_ref[c] = jnp.minimum(first_ref[c], inside)
        return end

    lax.fori_loop(0, spans + 1, reset, 0, unroll=8)
    lax.fori_loop(0, len_ref.shape[0], note, jnp.int32(0), unroll=4)
    first_ref[0] = 0


def fill_segments(seg_ref, len_ref, home_ref):
    slots, span = seg_ref.shape
    slot = lax.broadcasted_iota(jnp.int32, (slots, span), 0)
    position = lax.broadcasted_iota(jnp.int32, (slots, span), 1)
    for i in range(slots):
        position += jnp.where(slot == i, home_ref[i] * span, 0)

    def note(d, carry):
        end, segment = carry
        end = end + len_ref[d]
        return end, segment + jnp.where(end <= position, 1.0, 0.0)

    start = (jnp.int32(0), jnp.zeros((slots, span), F32))
    seg_ref[...] = lax.fori_loop(0, len_ref.shape[0], note, start, unroll=4)[1]


def tokens_at(i, span):
    return pl.ds(pl.multiple_of(i * span, span), span)


def rows_at(i, rows):
    return pl.ds(pl.multiple_of(i * rows, rows), rows)


def get_state(ref, i, h, rows):
    chunks = HEAD_SIZE // rows
    return ref[h * chunks : (h + 1) * chunks, rows_at(i, rows), :].reshape(HEAD_SIZE, HEAD_SIZE)


def span_copies(i, span, sources, targets, sem):
    at = tokens_at(i, span)
    return [
        pltpu.make_async_copy(source.at[at], target.at[at], sem.at[a, i])
        for a, (source, target) in enumerate(zip(sources, targets))
    ]


def start_all(copies):
    for copy in copies:
        copy.start()


def wait_all(copies):
    for copy in copies:
        copy.wait()


def each_span(slots, unroll, load, compute, store):
    def turn(g, carry):
        group = [g * unroll + j for j in range(unroll)]
        for i in group:
            wait_all(load(i))
        for i in group:
            compute(i)
        for i in group:
            start_all(store(i))
        return carry

    lax.fori_loop(0, slots // unroll, turn, 0)


def nothing(i):
    return []


def own_index():
    return lax.axis_index("seq")


def group_head(group, chunks):
    head = jnp.bitwise_xor(own_index() // chunks, group)
    return head, pl.ds(pl.multiple_of(head * HEAD_SIZE, HEAD_SIZE), HEAD_SIZE)


def put_group(packed, g, i, rows, value):
    chunks = HEAD_SIZE // rows
    for part in range(chunks):
        packed[g * chunks + part, rows_at(i, rows), :] = value[part * rows : (part + 1) * rows]


def get_group(packed, g, i, rows):
    chunks = HEAD_SIZE // rows
    return packed[g * chunks : (g + 1) * chunks, rows_at(i, rows), :].reshape(HEAD_SIZE, HEAD_SIZE)


def give_groups(packed, blocks, chunks, size):
    turn = own_index() % chunks
    for n, block in enumerate(blocks):
        block[:size] = packed[n // chunks * chunks + jnp.bitwise_xor(turn, n % chunks)]


def take_groups(blocks, packed, chunks):
    turn = own_index() % chunks
    for n, block in enumerate(blocks):
        packed[n // chunks * chunks + jnp.bitwise_xor(turn, n % chunks)] = block[...]


def take_blocks(blocks, packed):
    me = own_index()
    for mask, block in enumerate(blocks):
        packed[jnp.bitwise_xor(me, mask)] = block[...]


def summary_kernel(groups, rows, span, count, lead, *refs):
    if lead:
        len_ref, home_ref, rate_ref, k_hbm, v_hbm = refs[:5]
        blocks, refs = refs[5 : 5 + count], refs[5 + count :]
        first_ref, last_ref, k_ref, v_ref, table, packed, sem = refs
    else:
        last_ref, home_ref, rate_ref, k_hbm, v_hbm = refs[:5]
        blocks, refs = refs[5 : 5 + count], refs[5 + count :]
        k_ref, v_ref, table, packed, sem = refs
    slots = home_ref.shape[0]
    chunks = HEAD_SIZE // rows
    heads = [group_head(p, chunks) for p in groups]
    sources = [ref.at[:, heads[0][1]] if lead else ref for ref in (k_hbm, v_hbm)]
    load = lambda i: span_copies(i, span, sources, (k_ref, v_ref), sem)
    for i in range(slots):
        start_all(load(i))
    if lead:
        fill_tables(len_ref, first_ref, last_ref, span)
    for g, (head, cols) in enumerate(heads):
        table[g] = key_side(rate_ref[head], span)
    tail = jnp.zeros((TAIL, LANES), F32)
    lane = lax.broadcasted_iota(jnp.int32, (TAIL, LANES), 1)
    for i in range(slots):
        tail = jnp.where(lane == i, home_ref[i].astype(F32), tail)
    for block in blocks:
        block[slots * rows :, :] = tail.astype(BF16)

    def body(i):
        at = tokens_at(i, span)
        live = token_index(span) >= last_ref[home_ref[i]]
        for g, (head, cols) in enumerate(heads):
            cols = slice(None) if lead else cols
            side = jnp.where(live, table[g], 0.0)
            weighted = (side * v_ref[at, cols].astype(F32)).astype(BF16)
            put_group(packed, g, i, rows, dot(k_ref[at, cols], weighted, 0, 0).astype(BF16))

    each_span(slots, UNROLL["summary"], load, body, nothing)
    give_groups(packed, blocks, chunks, slots * rows)


def scan_kernel(rows, span, reverse, count, first_ref, order_in, rate_ref, *refs):
    sources, refs = refs[:count], refs[count if reverse else count + 1 :]
    targets, refs = refs[:count], refs[count:]
    if reverse:
        order_ref = order_in
        arrived, states = refs
    else:
        order_ref, arrived, states, homes, home_ref, home_sem = refs
    spans = order_ref.shape[0]
    slots = spans // count
    size = slots * rows
    if not reverse:
        for k, ref in enumerate(sources):
            homes[k : k + 1, :] = ref[slots * rows :, :].astype(F32)[0:1].astype(jnp.int32)
        gather = pltpu.make_async_copy(homes, home_ref, home_sem)
        gather.start()
    for k, ref in enumerate(sources):
        arrived[k * size : (k + 1) * size] = ref[:size]
    head = (own_index() * rows) // HEAD_SIZE
    factor = jnp.exp(jnp.full((8, LANES), -rate_ref[head] * span, F32))[0:1]
    if not reverse:
        gather.wait()

        def note(k, carry):
            for i in range(slots):
                order_ref[home_ref[k, i]] = k * slots + i
            return carry

        lax.fori_loop(0, count, note, 0, unroll=2)

    def body(i, state):
        c = spans - 1 - i if reverse else i
        place = order_ref[c]
        at = rows_at(place, rows)
        states[at, :] = state.astype(BF16)
        carried = jnp.where(first_ref[c] >= span, factor * state, 0.0)
        return carried + arrived[at, :].astype(F32)

    lax.fori_loop(0, spans, body, jnp.zeros((rows, LANES), F32), unroll=8)
    for k, ref in enumerate(targets):
        ref[...] = states[k * size : (k + 1) * size]


def local_kernel(
    heads, span, len_ref, home_ref, rate_ref, q_hbm, u_hbm, k_ref, v_ref,
    out_ref, q_ref, u_ref, seg_ref, side_ref, decay, sem, u_sem,
):
    slots = home_ref.shape[0]
    load = lambda i: span_copies(i, span, (q_hbm,), (q_ref,), sem)
    later = lambda i: span_copies(i, span, (u_hbm,), (u_ref,), u_sem)
    for i in range(slots):
        start_all(load(i))
    for i in range(slots):
        start_all(later(i))
    fill_segments(seg_ref, len_ref, home_ref)
    for h in range(heads):
        side_ref[h] = query_side(rate_ref[h], span)
    fill_decay(decay, rate_ref, 0, span)

    def body(i):
        at = tokens_at(i, span)
        seg = seg_ref[pl.ds(i, 1), :]
        same = row_to_cols(seg, span) == seg
        for h in range(heads):
            cols = head_cols(h)
            scores = dot(q_ref[at, cols], k_ref[at, cols], 1, 1)
            mixing = (scores * jnp.where(same, decay[h], 0.0)).astype(BF16)
            out_ref[at, cols] = dot(mixing, v_ref[at, cols], 1, 0)

    each_span(slots, UNROLL["local"], load, body, nothing)
    for i in range(slots):
        wait_all(later(i))


def output_kernel(
    groups, rows, span, count, again, first_ref, home_ref, side_ref, gain_ref, q_ref, u_ref, inner_ref, *refs
):
    blocks, refs = refs[:count], refs[count:]
    if again:
        before_ref, refs = refs[0], refs[2:]
    out_ref, sums_ref, prev = refs
    slots = home_ref.shape[0]
    chunks = HEAD_SIZE // rows
    heads = [group_head(p, chunks) for p in groups]
    take_groups(blocks, prev, chunks)

    def body(i):
        at = tokens_at(i, span)
        live = token_index(span) < first_ref[home_ref[i]]
        squares = jnp.zeros((span, LANES), F32)
        crossed = jnp.zeros((span, LANES), F32)
        for g, (head, cols) in enumerate(heads):
            outer = dot(q_ref[at, cols], get_group(prev, g, i, rows), 1, 0)
            attn = inner_ref[at, cols] + jnp.where(live, side_ref[head], 0.0) * outer
            out_ref[at, cols] = attn
            squares += attn * attn
            crossed += gain_ref[:, cols] * u_ref[at, cols].astype(F32) * attn
        squares, crossed = cols_to_row(squares), cols_to_row(crossed)
        if again:
            squares += before_ref[0, pl.ds(i, 1), :]
            crossed += before_ref[1, pl.ds(i, 1), :]
        sums_ref[0, pl.ds(i, 1), :] = squares
        sums_ref[1, pl.ds(i, 1), :] = crossed

    each_span(slots, UNROLL["output"], nothing, body, nothing)


def cotangent_kernel(
    groups, rows, span, count, again, channels, others, first_ref, home_ref, side_ref, gain_ref, q_ref, u_ref, attn_ref, *refs
):
    sums, refs = refs[:others], refs[others + again :]
    g_ref, blocks = refs[0], refs[1 : 1 + count]
    factors, packed = refs[1 + count :]
    slots = home_ref.shape[0]
    chunks = HEAD_SIZE // rows
    heads = [group_head(p, chunks) for p in groups]
    scaling = 1.0 / jnp.sqrt(sum(ref[0] for ref in sums) / channels + EPSILON)
    pulled = sum(ref[1] for ref in sums) / channels
    factors[0] = scaling
    factors[1] = scaling * scaling * scaling * pulled

    def body(i):
        at = tokens_at(i, span)
        direct = row_to_cols(factors[0, pl.ds(i, 1), :], LANES)
        along = row_to_cols(factors[1, pl.ds(i, 1), :], LANES)
        live = token_index(span) < first_ref[home_ref[i]]
        for g, (head, cols) in enumerate(heads):
            grad = direct * gain_ref[:, cols] * u_ref[at, cols].astype(F32)
            grad = (grad - along * attn_ref[at, cols]).astype(BF16)
            g_ref[at, cols] = grad
            weighted = (jnp.where(live, side_ref[head], 0.0) * grad.astype(F32)).astype(BF16)
            put_group(packed, g, i, rows, dot(q_ref[at, cols], weighted, 0, 0).astype(BF16))

    each_span(slots, UNROLL["cotangent"], nothing, body, nothing)
    give_groups(packed, blocks, chunks, slots * rows)


def inner_grads_kernel(
    heads, rows, span, count, half, first_ref, home_ref, rate_ref, seg_ref, q_ref, k_ref, v_ref, g_ref, *refs
):
    blocks, refs = refs[:count], refs[count + half :]
    dq_hbm, dk_ref, dv_ref, dq_ref, prev, decay, table, out_sem = refs
    slots = home_ref.shape[0] // 2
    base = half * slots
    target = dq_hbm.at[pl.ds(base * span, slots * span)]
    store = lambda i: span_copies(i, span, (dq_ref,), (target,), out_sem)
    take_blocks(blocks, prev)
    fill_decay(decay, rate_ref, 0, span)
    for h in range(heads):
        table[h] = query_side(rate_ref[h], span)

    def body(own):
        i = base + own
        at, own = tokens_at(i, span), tokens_at(own, span)
        seg = seg_ref[pl.ds(i, 1), :]
        same = row_to_cols(seg, span) == seg
        live = token_index(span) < first_ref[home_ref[i]]
        for h in range(heads):
            cols = head_cols(h)
            q, k, v, g = q_ref[at, cols], k_ref[at, cols], v_ref[at, cols], g_ref[at, cols]
            mask = jnp.where(same, decay[h], 0.0)
            mixing = (dot(q, k, 1, 1) * mask).astype(BF16)
            score_grad = (dot(g, v, 1, 1) * mask).astype(BF16)
            outer = dot(g, get_state(prev, i, h, rows), 1, 1)
            dq = dot(score_grad, k, 1, 0) + jnp.where(live, table[h], 0.0) * outer
            dq_ref[own, cols] = dq.astype(BF16)
            dk_ref[own, cols] = dot(score_grad, q, 0, 0)
            dv_ref[own, cols] = dot(mixing, g, 0, 0)

    each_span(slots, UNROLL["inner_grads"], nothing, body, store)
    for i in range(slots):
        wait_all(store(i))


def outer_grads_kernel(
    groups, rows, span, count, again, last_ref, home_ref, rate_ref, k_ref, v_ref, dk_0, dv_0, dk_1, dv_1, *refs
):
    blocks, refs = refs[:count], refs[count + 2 * again :]
    dk_hbm, dv_hbm, dk_ref, dv_ref, after_ref, table, out_sem = refs
    slots = home_ref.shape[0]
    chunks = HEAD_SIZE // rows
    heads = [group_head(p, chunks) for p in groups]

    def store(i):
        copies = []
        for g, (head, cols) in enumerate(heads):
            targets = (dk_hbm.at[:, cols], dv_hbm.at[:, cols])
            sources = (dk_ref.at[g], dv_ref.at[g])
            copies += span_copies(i, span, sources, targets, out_sem.at[g])
        return copies

    take_groups(blocks, after_ref, chunks)
    for g, (head, cols) in enumerate(heads):
        table[g] = key_side(rate_ref[head], span)

    def body(half, own):
        dk_in, dv_in = ((dk_0, dv_0), (dk_1, dv_1))[half]
        i = half * (slots // 2) + own
        at, own = tokens_at(i, span), tokens_at(own, span)
        live = token_index(span) >= last_ref[home_ref[i]]
        for g, (head, cols) in enumerate(heads):
            side = jnp.where(live, table[g], 0.0)
            after = get_group(after_ref, g, i, rows)
            dk = dk_in[own, cols] + side * dot(v_ref[at, cols], after, 1, 1)
            dv = dv_in[own, cols] + side * dot(k_ref[at, cols], after, 1, 0)
            dk_ref[g, at, :] = dk.astype(BF16)
            dv_ref[g, at, :] = dv.astype(BF16)

    for half in range(2):
        keep = lambda own, half=half: store(half * (slots // 2) + own)
        each_span(slots // 2, 4 if len(groups) == 1 else UNROLL["outer_grads"], nothing, functools.partial(body, half), keep)
    for i in range(slots):
        wait_all(store(i))


def swap(array, axis, mask):
    if mask == 0:
        return array
    return lax.ppermute(array, axis, [(i, i ^ mask) for i in range(lax.axis_size(axis))])


def exchange(blocks):
    moved = [None] * len(blocks)
    for mask in range(len(blocks) - 1, -1, -1):
        moved[mask] = swap(blocks[mask], "seq", mask)
    return moved


def shards(query, key, value, upstream, norm_gain, decay_rate, document_lengths, group_home):
    devices = lax.axis_size("seq")
    assert devices & (devices - 1) == 0
    tokens, width = query.shape
    heads = width // HEAD_SIZE
    slots = group_home.shape[0]
    span = tokens // slots
    spans = slots * devices
    rows = width // devices
    channels = width * lax.axis_size("head")

    gain = norm_gain.reshape(1, width)

    smem = pl.BlockSpec(memory_space=pltpu.SMEM)
    vmem = pl.BlockSpec(memory_space=pltpu.VMEM)
    hbm = pl.BlockSpec(memory_space=pl.ANY)
    spans_table = jax.ShapeDtypeStruct((spans + 1,), jnp.int32)
    whole = jax.ShapeDtypeStruct((tokens, width), BF16)
    token_bf16 = pltpu.VMEM((tokens, width), BF16)
    token_f32 = pltpu.VMEM((tokens, width), F32)
    table = pltpu.VMEM((heads, span, LANES), F32)
    decay = pltpu.VMEM((heads, span, span), F32)
    states = pltpu.VMEM((devices, slots * rows, LANES), BF16)
    out = [jax.ShapeDtypeStruct(states.shape[1:], BF16)] * devices
    taken = [vmem] * devices
    chunks = devices // heads
    assert heads > 1 and heads & (heads - 1) == 0
    final = heads // 2
    ahead, behind = (heads - 1,), tuple(range(heads - 2, -1, -1))
    early, late = tuple(p for p in range(heads - 1, -1, -1) if p != final), (final,)

    def masks_of(groups):
        return [p * chunks + n for p in groups for n in range(chunks)]

    def pick(blocks, groups):
        return [blocks[mask] for mask in masks_of(groups)]

    def states_of(groups):
        return pltpu.VMEM((len(groups) * chunks, slots * rows, LANES), BF16)

    def table_of(groups):
        return pltpu.VMEM((len(groups), span, LANES), F32)

    def sems(*shape):
        return pltpu.SemaphoreType.DMA(shape)

    def call(kernel, limit, flops, in_specs, out_specs, out_shape, scratch, *static, aliases={}):
        return pl.pallas_call(
            functools.partial(kernel, *static),
            in_specs=in_specs,
            out_specs=out_specs,
            out_shape=out_shape,
            scratch_shapes=scratch,
            input_output_aliases=aliases,
            compiler_params=pltpu.CompilerParams(vmem_limit_bytes=limit << 20),
            cost_estimate=pl.CostEstimate(flops=flops, bytes_accessed=0, transcendentals=0),
        )

    work = 2 * tokens * width * span
    shape = [jax.ShapeDtypeStruct((slots * rows + TAIL, LANES), BF16)]
    count = len(masks_of(ahead))
    *sent, first, last = call(
        summary_kernel, ALONE, work // 8,
        [smem, smem, smem, hbm, hbm],
        [vmem] * count + [smem, smem],
        shape * count + [spans_table, spans_table],
        [pltpu.VMEM((tokens, HEAD_SIZE), BF16)] * 2 + [table_of(ahead), states_of(ahead), sems(2, slots)],
        ahead, rows, span, count, True,
    )(document_lengths, group_home, decay_rate, key, value)
    moving = dict(zip(masks_of(ahead), sent))
    count = len(masks_of(behind))
    *sent, key_v, value_v = call(
        summary_kernel, ALONE, work // 2,
        [smem, smem, smem, hbm, hbm],
        [vmem] * (count + 2),
        shape * count + [token_bf16, token_bf16],
        [table_of(behind), states_of(behind), sems(2, slots)],
        behind, rows, span, count, False,
    )(last, group_home, decay_rate, key, value)
    moving.update(zip(masks_of(behind), sent))
    arrived = exchange(moving)

    inner, query_v, upstream_v, seg, side = call(
        local_kernel, LIMIT, 2 * work,
        [smem, smem, smem, hbm, hbm, vmem, vmem],
        [vmem] * 5,
        [token_f32, token_bf16, token_bf16, pltpu.VMEM((slots, span), F32), table],
        [decay, sems(1, slots), sems(1, slots)],
        heads, span,
    )(document_lengths, group_home, decay_rate, query, upstream, key_v, value_v)

    def scan(arrived, order, reverse, *after_it):
        held = [pltpu.VMEM((devices * slots * rows, LANES), BF16)] * 2
        if reverse:
            extra_specs, extra = [], []
        else:
            extra_specs, extra = [smem], [jax.ShapeDtypeStruct((spans,), jnp.int32)]
            table_shape = (devices, LANES)
            held += [pltpu.VMEM(table_shape, jnp.int32), pltpu.SMEM(table_shape, jnp.int32), pltpu.SemaphoreType.DMA]
        return call(
            scan_kernel, LIMIT, work // 8,
            [smem, smem, smem] + taken + [hbm] * len(after_it),
            taken + extra_specs,
            out + extra,
            held,
            rows, span, reverse, devices,
        )(first, order, decay_rate, *arrived, *after_it)

    *moving, order = scan(arrived, group_home, False, seg)
    prev = exchange(moving)

    def outputs(groups, *before):
        count = len(masks_of(groups))
        again = len(before) > 0
        return call(
            output_kernel, LIMIT, work // 4,
            [smem, smem, vmem] + [vmem] * (4 + count + len(before)),
            [vmem, vmem],
            [token_f32, jax.ShapeDtypeStruct((2, slots, span), F32)],
            [states_of(groups)],
            groups, rows, span, count, again,
            aliases={8 + count: 0} if again else {},
        )(first, group_home, side, gain, query_v, upstream_v, inner, *pick(prev, groups), *before)

    attn, sums = outputs(early)
    attn, sums = outputs(late, sums, attn)
    sums = [swap(sums, "head", mask) for mask in range(lax.axis_size("head") - 1, -1, -1)]

    def cotangents(groups, *before):
        count = len(masks_of(groups))
        others = len(sums)
        return call(
            cotangent_kernel, LIMIT, work // 4,
            [smem, smem, vmem] + [vmem] * (4 + others + len(before)),
            [vmem] * (1 + count),
            [token_bf16] + out[:count],
            [pltpu.VMEM((2, slots, span), F32), states_of(groups)],
            groups, rows, span, count, len(before), channels, others,
            aliases={7 + others: 0} if before else {},
        )(first, group_home, side, gain, query_v, upstream_v, attn, *sums, *before)

    grad_in, *sent = cotangents(ahead)
    moving = dict(zip(masks_of(ahead), sent))
    grad_in, *sent = cotangents(behind, grad_in)
    moving.update(zip(masks_of(behind), sent))
    arrived = exchange(moving)

    half_f32 = pltpu.VMEM((tokens // 2, width), F32)

    def inner_grads(half, *into):
        return call(
            inner_grads_kernel, LIMIT, 3 * work,
            [smem, smem, smem, vmem, vmem, vmem, vmem, vmem] + taken + [hbm] * half,
            [hbm, vmem, vmem],
            [whole, half_f32, half_f32],
            [pltpu.VMEM((tokens // 2, width), BF16), states, decay, table, sems(1, slots // 2)],
            heads, rows, span, devices, half,
            aliases={8 + devices: 0} if half else {},
        )(first, group_home, decay_rate, seg, query_v, key_v, value_v, grad_in, *prev, *into)

    query_half, *parts = inner_grads(0)
    query_grad, *others = inner_grads(1, query_half)
    after = exchange(scan(arrived, order, True))

    def outer_grads(groups, *before):
        count = len(masks_of(groups))
        part = pltpu.VMEM((len(groups), tokens, HEAD_SIZE), BF16)
        return call(
            outer_grads_kernel, LIMIT, work // 2,
            [smem, smem, smem] + [vmem] * (6 + count) + [hbm] * len(before),
            [hbm, hbm],
            [whole, whole],
            [part, part, states_of(groups), table_of(groups), sems(len(groups), 2, slots)],
            groups, rows, span, count, len(before) > 0,
            aliases={9 + count: 0, 10 + count: 1} if before else {},
        )(last, group_home, decay_rate, key_v, value_v, *parts, *others, *pick(after, groups), *before)

    finals = outer_grads(early)
    key_grad, value_grad = outer_grads(late, *finals)
    return query_grad, key_grad, value_grad


def solution(mesh):
    in_specs = (
        P("seq", "head"),
        P("seq", "head"),
        P("seq", "head"),
        P("seq", "head"),
        P("head"),
        P("head"),
        P(),
        P("seq"),
    )
    out_specs = (P("seq", "head"), P("seq", "head"), P("seq", "head"))

    return jax.shard_map(shards, mesh=mesh, in_specs=in_specs, out_specs=out_specs, check_vma=False)
```
